32 devices in a mesh: dp: 4 (over y, core), fsdp: 8 (over z, x).
Axes of the slice: x: 2, y: 2, z: 4, core: 2. Of those that a mesh axis runs over, the one named last changes fastest.
Arguments:
- tokens: bfloat16 [64, 384, 768], P(('dp', 'fsdp')), may hold values from -6 to 6
- lengths: int32 [64, 4], P(('dp', 'fsdp')), may hold values from 1 to 192, 384 in all within a row
- w_query: bfloat16 [768, 768], P('fsdp'), may hold values from -0.3125 to 0.3125
- w_key: bfloat16 [768, 768], P('fsdp'), may hold values from -0.3125 to 0.3125
- w_value: bfloat16 [768, 768], P('fsdp'), may hold values from -0.21875 to 0.21875
- w_out: bfloat16 [768, 768], P('fsdp'), may hold values from -0.875 to 0.875
- w_gate: bfloat16 [768, 2048], P('fsdp'), may hold values from -0.21875 to 0.21875
- w_up: bfloat16 [768, 2048], P('fsdp'), may hold values from -0.21875 to 0.21875
- w_down: bfloat16 [2048, 768], P('fsdp'), may hold values from -0.25 to 0.25
- gain_attn: bfloat16 [768], P('fsdp'), may hold values from 0.5 to 1.5
- gain_ffn: bfloat16 [768], P('fsdp'), may hold values from 0.5 to 1.5
- output_gradient: bfloat16 [64, 384, 768], P(('dp', 'fsdp')), may hold values from -6 to 6
Outputs:
- output: bfloat16 [64, 384, 768], P(('dp', 'fsdp'))
- grad_tokens: bfloat16 [64, 384, 768], P(('dp', 'fsdp'))
- grad_w_query: float32 [768, 768], P('fsdp')
- grad_w_key: float32 [768, 768], P('fsdp')
- grad_w_value: float32 [768, 768], P('fsdp')
- grad_w_out: float32 [768, 768], P('fsdp')
- grad_w_gate: float32 [768, 2048], P('fsdp')
- grad_w_up: float32 [768, 2048], P('fsdp')
- grad_w_down: float32 [2048, 768], P('fsdp')
- grad_gain_attn: float32 [768], P('fsdp')
- grad_gain_ffn: float32 [768], P('fsdp')
The draws below stay inside these ranges and needn't reach their ends.
Inputs may be any that keep to these rules, and one draw needn't show every extreme that they name: Each row holds the lengths of 4 pieces that fill a slot of 384 positions in order; the last piece is padding; in every row the longest is 192.
All inputs are finite; a program needn't handle non-finite values.
Results may differ from the reference program's by a relative error of at most 0.018.
Values may be sent and summed in bfloat16 or wider, within the bound.
A program may use at most 192 MiB of HBM per device.

```python
import math
import jax
import jax.numpy as jnp
import numpy as np
from jax import lax

MODEL_WIDTH = 768
HEADS = 12
HEAD_DIM = 64
FF = 2048
SLOT_LENGTH = 384
SLOT_PIECES = 4
SLOT_COUNT = 64


def level_of(own_key, extent, cuts, low, largest):
    loudness, own = 1.0, jax.random.fold_in(own_key, 6)
    for dim, parts in cuts:
        draws = jnp.exp(jax.random.uniform(jax.random.fold_in(own, dim), (parts,), jnp.float32, low / len(cuts), largest / len(cuts)))
        loudness = loudness * jnp.repeat(draws, extent[dim] // parts).reshape([-1 if axis == dim else 1 for axis in range(len(extent))])
    return loudness


def length_profile(amount, total, reach, slope):
    portions = [(1 << 20) // math.isqrt(standing ** slope) + 1 for standing in range(2, amount + 1)]
    spare, holding = total - reach - (amount - 1), [1] * (amount - 1)
    while spare > 0:
        free = [i for i in range(amount - 1) if holding[i] < reach]
        pool, remaining = sum([portions[i] for i in free]), spare
        for i in free:
            more = min(reach - holding[i], max(1, remaining * portions[i] // pool), spare)
            holding[i] = holding[i] + more
            spare = spare - more
    return np.array([reach] + holding)


def uneven_parts(stream_key, amount, total, most, skew):
    if amount == 2:
        one = jax.random.randint(stream_key, (), max(1, total - most), min(most, total - 1) + 1)
        return jnp.stack([one, total - one])
    sizes = jnp.asarray(length_profile(amount, total, most, skew), jnp.int32)
    couples = (amount - 1) // 2
    source_of, receiver = sizes[1:1 + 2 * couples:2], sizes[2:2 + 2 * couples:2]
    slack = jnp.minimum(source_of - 1, most - receiver)
    passed = jax.random.randint(jax.random.fold_in(stream_key, 1), (couples,), 0, 1 << 20) % (slack + 1)
    sizes = sizes.at[1:1 + 2 * couples:2].set(source_of - passed).at[2:2 + 2 * couples:2].set(receiver + passed)
    return sizes[jax.random.permutation(jax.random.fold_in(stream_key, 2), amount)]


def scatter_about(own_key, extent, scale, bound, cuts=(), dtype=jnp.bfloat16):
    array = scale * jax.random.normal(own_key, extent, jnp.float32)
    if cuts:
        array = array * level_of(own_key, extent, cuts, -0.22, 0.18)
    return jnp.clip(array, -bound, bound).astype(dtype)


def setup_inputs(seed: int = 0) -> dict:
    keys = jax.random.split(jax.random.key(seed), 13)
    return {
        "tokens": scatter_about(keys[0], (SLOT_COUNT, SLOT_LENGTH, MODEL_WIDTH), 1.0, 6.0, ((0, 32),)),
        "lengths": jax.vmap(lambda own: uneven_parts(own, SLOT_PIECES, SLOT_LENGTH, SLOT_LENGTH // 2, 2))(jax.random.split(keys[1], SLOT_COUNT)).reshape((SLOT_COUNT, SLOT_PIECES)).astype(jnp.int32),
        "w_query": scatter_about(keys[2], (MODEL_WIDTH, MODEL_WIDTH), (MODEL_WIDTH // 2) ** -0.5, 0.3125, ((0, 8),)),
        "w_key": scatter_about(keys[3], (MODEL_WIDTH, MODEL_WIDTH), (MODEL_WIDTH // 2) ** -0.5, 0.3125, ((0, 8),)),
        "w_value": scatter_about(keys[4], (MODEL_WIDTH, MODEL_WIDTH), MODEL_WIDTH ** -0.5, 0.21875, ((0, 8),)),
        "w_out": scatter_about(keys[5], (MODEL_WIDTH, MODEL_WIDTH), (MODEL_WIDTH // 16) ** -0.5, 0.875, ((0, 8),)),
        "w_gate": scatter_about(keys[6], (MODEL_WIDTH, FF), MODEL_WIDTH ** -0.5, 0.21875, ((0, 8),)),
        "w_up": scatter_about(keys[7], (MODEL_WIDTH, FF), MODEL_WIDTH ** -0.5, 0.21875, ((0, 8),)),
        "w_down": scatter_about(keys[8], (FF, MODEL_WIDTH), (FF // 4) ** -0.5, 0.25, ((0, 8),)),
        "gain_attn": jnp.clip(1.0 + 0.1 * jax.random.normal(keys[9], (MODEL_WIDTH,), jnp.float32), 0.5, 1.5).astype(jnp.bfloat16),
        "gain_ffn": jnp.clip(1.0 + 0.1 * jax.random.normal(keys[10], (MODEL_WIDTH,), jnp.float32), 0.5, 1.5).astype(jnp.bfloat16),
        "output_gradient": scatter_about(keys[11], (SLOT_COUNT, SLOT_LENGTH, MODEL_WIDTH), 1.0, 6.0, ((0, 32),)),
    }


@jax.custom_vjp
def low(v):
    return lax.optimization_barrier(v.astype(jnp.bfloat16)).astype(jnp.float32)

@jax.custom_vjp
def low_back(v):
    return v

def low_keep(v):
    return (low(v), None)

def low_pass(kept, grad):
    return (grad,)

def back_keep(v):
    return (v, None)

def back_low(kept, grad):
    return (low(grad),)
low.defvjp(low_keep, low_pass)
low_back.defvjp(back_keep, back_low)
epsilon = 1e-05

def layout(lengths, slot):
    pieces = lengths.shape[0]
    bounds = jnp.cumsum(lengths).astype(jnp.int32)
    places = lax.iota(jnp.int32, slot)
    piece_of = lax.optimization_barrier(jnp.sum((places[:, None] >= bounds[None, :]).astype(jnp.int32), axis=1)).astype(jnp.int32)
    piece_begins = (bounds - lengths).astype(jnp.int32)
    member = piece_of[:, None] == lax.iota(jnp.int32, pieces)[None, :]
    begins = lax.optimization_barrier(jnp.sum(jnp.where(member, piece_begins[None, :], 0), axis=1)).astype(jnp.int32)
    offsets = places - begins
    live = (piece_of < pieces - 1).astype(jnp.float32)
    visible = (piece_of[:, None] == piece_of[None, :]) & (places[None, :] <= places[:, None])
    return (offsets, live, visible)

def rotary(offsets, head_dim):
    half = head_dim // 2
    rates = jnp.power(10000.0, -2.0 * lax.iota(jnp.float32, half) / head_dim)
    angle = offsets.astype(jnp.float32)[:, None] * rates[None, :]
    angle = jnp.concatenate([angle, angle], axis=1)
    return (jnp.cos(angle), jnp.sin(angle))

def turn(values, cosine, sine, sign):
    half = values.shape[-1] // 2
    swapped = jnp.concatenate([-values[..., half:], values[..., :half]], axis=-1)
    return values * cosine[:, None, :] + sign * swapped * sine[:, None, :]

def matmul_full(left, right):
    return jnp.dot(left, right, precision=lax.Precision.HIGHEST, preferred_element_type=jnp.float32)

def slot_forward(params, stream, lengths):
    w_query, w_key, w_value, w_out, w_gate, w_up, w_down, gain_attn, gain_ffn = params
    slot = stream.shape[0]
    offsets, live, visible = layout(lengths, slot)
    cosine, sine = rotary(offsets, HEAD_DIM)
    scale_attn = lax.rsqrt(lax.optimization_barrier(jnp.mean(stream * stream, axis=1, keepdims=True)) + epsilon)
    normed_attn = low(stream * scale_attn * gain_attn)
    query_unrotated = low_back(matmul_full(normed_attn, w_query)).reshape(slot, HEADS, HEAD_DIM)
    key_pre = low_back(matmul_full(normed_attn, w_key)).reshape(slot, HEADS, HEAD_DIM)
    query_rows = low(turn(query_unrotated, cosine, sine, 1.0))
    key_rows = low(turn(key_pre, cosine, sine, 1.0))
    value_rows = low(low_back(matmul_full(normed_attn, w_value))).reshape(slot, HEADS, HEAD_DIM)
    scores = jnp.einsum('qhd,khd->hqk', query_rows, key_rows, precision=lax.Precision.HIGHEST) * HEAD_DIM ** (-0.5)
    scores = low_back(scores)
    masked = jnp.where(visible[None], scores, -1e+30)
    top = lax.optimization_barrier(jnp.max(masked, axis=-1, keepdims=True))
    weights = jnp.exp(masked - top)
    probs = weights / lax.optimization_barrier(jnp.sum(weights, axis=-1, keepdims=True))
    mixed = jnp.einsum('hqk,khd->qhd', low(probs), value_rows, precision=lax.Precision.HIGHEST)
    heads_out = low(low_back(mixed.reshape(slot, HEADS * HEAD_DIM)))
    stream_mid = stream + low_back(matmul_full(heads_out, w_out))
    scale_ffn = lax.rsqrt(lax.optimization_barrier(jnp.mean(stream_mid * stream_mid, axis=1, keepdims=True)) + epsilon)
    normed_ffn = low(stream_mid * scale_ffn * gain_ffn)
    gate_pre = low_back(matmul_full(normed_ffn, w_gate))
    up_branch = low_back(matmul_full(normed_ffn, w_up))
    hidden = low(gate_pre * jax.nn.sigmoid(gate_pre) * up_branch)
    return stream_mid + low_back(matmul_full(hidden, w_down))

def live_of(lengths_row):
    return layout(lengths_row, SLOT_LENGTH)[1]

def reference(tokens, lengths, w_query, w_key, w_value, w_out, w_gate, w_up, w_down, gain_attn, gain_ffn, output_gradient):
    params = tuple((weight.astype(jnp.float32) for weight in (w_query, w_key, w_value, w_out, w_gate, w_up, w_down, gain_attn, gain_ffn)))
    grouped = tokens.shape[0] // 8
    token_blocks = tokens.reshape((grouped, 8) + tokens.shape[1:])
    length_blocks = lengths.reshape((grouped, 8) + lengths.shape[1:])
    cotangent_blocks = output_gradient.reshape((grouped, 8) + output_gradient.shape[1:])

    def step(totals, item):
        token_block, length_block, cotangent_block = item

        def run(weights, streams):
            return jax.vmap(slot_forward, in_axes=(None, 0, 0))(weights, streams, length_block)
        outputs, pull = jax.vjp(run, params, token_block.astype(jnp.float32))
        live_rows = jax.vmap(live_of)(length_block)
        weight_grads, stream_grads = pull(cotangent_block.astype(jnp.float32) * live_rows[..., None])
        totals = tuple((total + extra for total, extra in zip(totals, weight_grads)))
        return (totals, (outputs.astype(jnp.bfloat16), stream_grads.astype(jnp.bfloat16)))
    zeros = tuple((jnp.zeros_like(weight) for weight in params))
    totals, (outputs, stream_grads) = lax.scan(step, zeros, (token_blocks, length_blocks, cotangent_blocks))
    output = outputs.reshape(tokens.shape)
    grad_tokens = stream_grads.reshape(tokens.shape)
    return (output, grad_tokens, totals[0], totals[1], totals[2], totals[3], totals[4], totals[5], totals[6], totals[7], totals[8])
```

```python
import math
import jax
import jax.numpy as jnp
from jax import lax
from jax.experimental import pallas as pl
from jax.experimental.pallas import tpu as pltpu
from jax.sharding import PartitionSpec as P

HEADS = 12
HEAD_DIM = 64
HALF = HEAD_DIM // 2
FACTOR = HEAD_DIM ** (-0.5)
epsilon = 1e-05
f32 = jnp.float32
bf16 = jnp.bfloat16
MESH = pl.DeviceIdType.MESH


def mm(a, b, ca=1, cb=0):
    return lax.dot_general(a, b, (((ca,), (cb,)), ((), ())), preferred_element_type=f32)


def rope(v, cosine, sine_low, sine_high):
    return (
        v * cosine
        + pltpu.roll(v, 128 - HALF, 1) * sine_low
        + pltpu.roll(v, HALF, 1) * sine_high
    )


def split_heads(x):
    lane = lax.broadcasted_iota(jnp.int32, x.shape, 1)
    zero = jnp.zeros_like(x)
    return jnp.concatenate(
        [jnp.where(lane < HEAD_DIM, x, zero), jnp.where(lane < HEAD_DIM, zero, x)], axis=0
    )


def join_heads(y):
    rows = y.shape[0] // 2
    lane = lax.broadcasted_iota(jnp.int32, (rows, 128), 1)
    return jnp.where(lane < HEAD_DIM, y[:rows], y[rows:])


class Copies:
    def __init__(self, send, recv):
        self.send, self.recv, self.started = send, recv, {}

    def start(self, key, src, dst, device):
        copy = pltpu.make_async_remote_copy(
            src_ref=src,
            dst_ref=dst,
            send_sem=self.send.at[key],
            recv_sem=self.recv.at[key],
            device_id=device,
            device_id_type=MESH,
        )
        copy.start()
        self.started[key] = copy

    def arrived(self, key, dst, device):
        pltpu.make_async_remote_copy(
            src_ref=dst,
            dst_ref=dst,
            send_sem=self.send.at[key],
            recv_sem=self.recv.at[key],
            device_id=device,
            device_id_type=MESH,
        ).wait_recv()

    def sent(self, *keys):
        for key in keys:
            self.started.pop(key).wait_send()


def build(mesh, slots, slot, width, ff):
    dps, fs = mesh.shape["dp"], mesh.shape["fsdp"]
    Z, ZH = fs // 2, fs // 4
    T = slots * slot
    R, RD = width // fs // 2, ff // fs // 4
    FH = ff // 2
    NB = FH // 2
    HW = width // 2
    QN = 256
    QB = width // QN
    PAIRS = width // 128
    NAG = 10
    G_SHAPE, D_SHAPE, O_SHAPE, Q_SHAPE = (2, R, NB), (1, RD, width), (1, R, width), (3, R, QN)
    PIECES = (
        [("g", G_SHAPE), ("g", G_SHAPE), ("d", D_SHAPE)] * 2
        + [("o", O_SHAPE)]
        + [("q", Q_SHAPE)] * QB
    )
    NRS = len(PIECES)

    def kernel(
        lens, gains8, tokens, gradient, w_query, w_key, w_value, w_out, w_gate, w_up, w_down,
        out_main, out_tokens, out_gains, *rest,
    ):
        out_pieces, rest = rest[:NRS], rest[NRS:]
        (
            wq, wk, wv, wo, wg0, wu0, wd0, wg1, wu1, wd1,
            tok, na, q, k, v, ho, smid, nf, db, dnf, outacc,
            cos_t, low_t, high_t, stats, bias_t, lse, hs, dgs, dus,
            gsum, grecv, gains, gg, ggrecv,
            g_slots, d_slots, o_slot, q_slots,
        ) = rest[:39]
        rest = rest[39:]
        bufs, rest = rest[: 5 * NRS], rest[5 * NRS :]
        c1_g, c1_d, c1_o, c1_q = rest[:4]
        (local_sem, ag_send, ag_recv, rs_send, rs_recv, gn_send, gn_recv, out_sem) = rest[4:]

        d, f = lax.axis_index("dp"), lax.axis_index("fsdp")
        y, c = d // 2, d % 2
        z, x = f // 2, f % 2
        nx, ny, nc = 1 - x, 1 - y, 1 - c
        dev_x, dev_y, dev_c = (d, z * 2 + nx), (ny * 2 + c, f), (y * 2 + nc, f)

        def dev_z(zt):
            return (d, zt * 2 + x)

        JS = [1, Z - 1] + list(range(2, Z - 1))

        locals_ = []

        def fetch(src, dst):
            copy = pltpu.make_async_copy(src, dst, local_sem.at[len(locals_)])
            copy.start()
            locals_.append(copy)

        def own(w):
            return w.at[z, x]

        for src, w in ((w_query, wq), (w_key, wk), (w_value, wv), (w_out, wo)):
            for h in range(2):
                fetch(src.at[pl.ds(h * R, R)], w.at[z, x, h])
        per = width // fs
        for src, held_in in ((w_gate, hs), (w_up, dus)):
            for j in range(ff // NB):
                fetch(src.at[:, pl.ds(j * NB, NB)], held_in.at[pl.ds(j * per, per)])
        for kk, w in ((0, wd0), (1, wd1)):
            for h in range(2):
                fetch(w_down.at[pl.ds((2 * kk + h) * RD, RD)], w.at[z, x, h])
        for s in range(slots):
            fetch(tokens.at[s], tok.at[pl.ds(s * slot, slot)])
            fetch(gradient.at[s], db.at[pl.ds(s * slot, slot)])
        partners = [dev_c, dev_x, dev_y] + [dev_z(lax.rem(z + j, Z)) for j in range(1, Z)]
        barrier = pltpu.get_barrier_semaphore()
        for p in partners:
            pl.semaphore_signal(barrier, inc=1, device_id=p, device_id_type=MESH)
        for copy in locals_:
            copy.wait()
        for g, pair in enumerate(((wg0, wg1), (wu0, wu1))):
            for kk, w in enumerate(pair):
                for j in range(fs):
                    b, o = divmod((2 * j + kk) * 128, NB)
                    val = (hs, dus)[g][b * per : (b + 1) * per, o : o + 128]
                    w[z, x, :, :, j * 128 : (j + 1) * 128] = val.reshape(2, R, 128)
        pl.semaphore_wait(barrier, len(partners))

        ag = Copies(ag_send, ag_recv)
        AG = [wq, wk, wv, wo, wg0, wu0, wd0, wg1, wu1, wd1]

        def cols(n, which):
            return pl.ds(pl.multiple_of(which * (n // 2), n // 2), n // 2)

        def side_of(p):
            return [3] if p % 2 else []

        def ag_z(p):
            w = AG[p]
            n = w.shape[-1]
            for j in JS:
                r = w.at[z, x, c, :, cols(n, y)]
                ag.start((p, j - 1), r, r, dev_z(lax.rem(z + j, Z)))
            r = w.at[z, x, c]
            ag.start((p, 3), r, r, dev_x)

        def ag_f(p):
            w = AG[p]
            n = w.shape[-1]
            for j in JS:
                zs = lax.rem(z - j + Z, Z)
                r = w.at[zs, x, c, :, cols(n, y)]
                ag.arrived((p, j - 1), r, dev_z(zs))
                ag.start((p, 3 + j), r, r, dev_x)
                ag.start((p, 6 + j), r, r, dev_y)

        def ag_d(p):
            w = AG[p]
            n = w.shape[-1]
            for j in JS:
                zs = lax.rem(z - j + Z, Z)
                r = w.at[zs, nx, c, :, cols(n, y)]
                ag.arrived((p, 3 + j), r, dev_x)
                if j not in side_of(p):
                    ag.start((p, 9 + j), r, r, dev_y)
                r = w.at[zs, x, c, :, cols(n, ny)]
                ag.arrived((p, 6 + j), r, dev_y)
                if j in side_of(p):
                    ag.start((p, 9 + j), r, r, dev_x)
                r = w.at[zs, x, c]
                ag.start((p, 12 + j), r, r, dev_c)
            ag.arrived((p, 3), w.at[z, nx, c], dev_x)

        def ag_c(p):
            w = AG[p]
            n = w.shape[-1]
            for j in JS:
                zs = lax.rem(z - j + Z, Z)
                r = w.at[zs, nx, c, :, cols(n, ny)]
                ag.arrived((p, 9 + j), r, dev_x if j in side_of(p) else dev_y)
            r = w.at[:, nx, c]
            ag.start((p, 16), r, r, dev_c)

        def ag_e(p):
            w = AG[p]
            for j in JS:
                ag.arrived((p, 12 + j), w.at[lax.rem(z - j + Z, Z), x, nc], dev_c)
            ag.arrived((p, 16), w.at[:, nx, nc], dev_c)
            ag.sent(*((p, i) for i in range(17)))

        def ag_tick(t):
            if 0 <= t < NAG:
                ag_f(t)
            if 0 <= t + 2 < NAG:
                ag_z(t + 2)
            if 0 <= t - 1 < NAG:
                ag_d(t - 1)
            if 0 <= t - 2 < NAG:
                ag_c(t - 2)
            if 0 <= t - 3 < NAG:
                ag_e(t - 3)

        rs = Copies(rs_send, rs_recv)
        held = []
        counts = {"g": 0, "d": 0, "o": 0, "q": 0}
        for r, (kind, _) in enumerate(PIECES):
            i = counts[kind]
            counts[kind] += 1
            slots_of = {"g": g_slots, "d": d_slots, "o": o_slot, "q": q_slots}[kind]
            c1_of = {"g": c1_g, "d": c1_d, "o": c1_o, "q": c1_q}[kind]
            held.append(
                (slots_of.at[i % slots_of.shape[0]], c1_of.at[i % c1_of.shape[0]])
                + tuple(bufs[5 * r : 5 * r + 5])
            )

        def rs_1(r):
            G, C1 = held[r][:2]
            rs.start((r, 0), G.at[:, :, :, :, nc], C1, dev_c)

        def rs_2(r):
            G, C1, XA, YB, S3, ZR, FIN = held[r]
            n = C1.shape[-1]
            rs.arrived((r, 0), C1, dev_c)
            for a in range(C1.shape[0]):
                for zh in range(ZH):
                    for zl in range(2):
                        C1[a, zh, zl] = (
                            C1[a, zh, zl].astype(f32) + G[a, zh, zl, :, c].astype(f32)
                        ).astype(bf16)
            rs.start((r, 1), C1.at[:, :, 0, nx], XA, dev_x)
            rs.start((r, 2), C1.at[:, :, 1, :, :, cols(n, ny)], YB, dev_y)
            rs.sent((r, 0))

        def rs_3(r):
            G, C1, XA, YB, S3, ZR, FIN = held[r]
            n = C1.shape[-1]
            rs.arrived((r, 1), XA, dev_x)
            XA[...] = (XA[...].astype(f32) + C1[:, :, 0, x].astype(f32)).astype(bf16)
            rs.start((r, 3), XA.at[:, :, :, cols(n, ny)], S3.at[:, :, 0], dev_y)
            rs.arrived((r, 2), YB, dev_y)
            YB[...] = (
                YB[...].astype(f32) + C1[:, :, 1, :, :, cols(n, y)].astype(f32)
            ).astype(bf16)
            rs.start((r, 4), YB.at[:, :, nx], S3.at[:, :, 1], dev_x)
            rs.sent((r, 1), (r, 2))

        def rs_4(r):
            G, C1, XA, YB, S3, ZR, FIN = held[r]
            n = C1.shape[-1]
            rs.arrived((r, 3), S3.at[:, :, 0], dev_y)
            S3[:, :, 0] = (
                S3[:, :, 0].astype(f32) + XA[:, :, :, cols(n, y)].astype(f32)
            ).astype(bf16)
            rs.arrived((r, 4), S3.at[:, :, 1], dev_x)
            S3[:, :, 1] = (S3[:, :, 1].astype(f32) + YB[:, :, x].astype(f32)).astype(bf16)
            for j in JS:
                zt = lax.rem(z + j, Z)
                rs.start((r, 4 + j), S3.at[:, zt // 2, zt % 2], ZR.at[j - 1], dev_z(zt))
            rs.sent((r, 3), (r, 4))

        def rs_5(r):
            G, C1, XA, YB, S3, ZR, FIN = held[r]
            n = C1.shape[-1]
            total = S3[:, z // 2, z % 2].astype(f32)
            for j in JS:
                rs.arrived((r, 4 + j), ZR.at[j - 1], dev_z(lax.rem(z - j + Z, Z)))
                total = total + ZR[j - 1].astype(f32)
            FIN[:, c, :, cols(n, y)] = total.astype(bf16)
            part = FIN.at[:, c, :, cols(n, y)]
            rs.start((r, 8), part, part, dev_y)
            rs.sent((r, 5), (r, 6), (r, 7))

        def rs_6(r):
            FIN = held[r][6]
            n = FIN.shape[-1]
            rs.arrived((r, 8), FIN.at[:, c, :, cols(n, ny)], dev_y)
            rs.start((r, 9), FIN.at[:, c], FIN.at[:, c], dev_c)
            rs.sent((r, 8))

        outs = []

        def put(src, dst):
            copy = pltpu.make_async_copy(src, dst, out_sem.at[len(outs)])
            copy.start()
            outs.append(copy)

        def rs_7(r):
            FIN = held[r][6]
            rs.arrived((r, 9), FIN.at[:, nc], dev_c)
            rs.sent((r, 9))
            put(FIN, out_pieces[r])

        RS_STEPS = [rs_2, rs_3, rs_4, rs_5, rs_6, rs_7]
        progress = {}

        def rs_begin(r):
            rs_1(r)
            progress[r] = 0

        def rs_tick():
            for r in sorted(progress):
                RS_STEPS[progress[r]](r)
                progress[r] += 1
                if progress[r] == len(RS_STEPS):
                    del progress[r]

        gn = Copies(gn_send, gn_recv)
        axis_partners = [dev_x, dev_z(z ^ 1)] + ([dev_z(z ^ 2)] if Z == 4 else [])
        lane = lax.broadcasted_iota(jnp.int32, (128, width), 0)
        at = lax.broadcasted_iota(jnp.int32, (128, width), 1)
        place = jnp.where((lane == at % per), 1.0, 0.0).astype(bf16)
        spread = mm(gains8[...].astype(bf16), place)
        mine = lax.broadcasted_iota(jnp.int32, (8, width), 1) // per == f
        gsum[0] = jnp.where(mine, spread, 0.0)

        def gn_start(i):
            gn.start(i, gsum.at[i], grecv.at[i], axis_partners[i])

        def gn_finish(i):
            gn.arrived(i, grecv.at[i], axis_partners[i])
            gsum[i + 1] = gsum[i] + grecv[i]

        all_partners = [dev_c, dev_y] + axis_partners
        NA = len(axis_partners)

        def gg_start(i):
            gn.start(NA + i, gg.at[i], ggrecv.at[i], all_partners[i])

        def gg_finish(i):
            gn.arrived(NA + i, ggrecv.at[i], all_partners[i])
            gg[i + 1] = gg[i] + ggrecv[i]

        lane128 = lax.broadcasted_iota(jnp.int32, (slot, 128), 1) % HEAD_DIM
        prow = lax.broadcasted_iota(jnp.int32, (slot, 128), 0)

        def tables():
            rate = jnp.exp(
                (lane128 % HALF).astype(f32) * (-2.0 * math.log(10000.0) / HEAD_DIM)
            )
            for s in range(slots):
                e0 = lens[s, 0]
                e1 = e0 + lens[s, 1]
                e2 = e1 + lens[s, 2]
                e3 = e2 + lens[s, 3]

                def begins(p):
                    b = jnp.where(p >= e0, e0, 0)
                    b = jnp.where(p >= e1, e1, b)
                    b = jnp.where(p >= e2, e2, b)
                    return jnp.where(p >= e3, e3, b)

                angle = (prow - begins(prow)).astype(f32) * rate
                sine = jnp.sin(angle)
                rows = slice(s * slot, (s + 1) * slot)
                cos_t[rows, :] = jnp.cos(angle)
                low_t[rows, :] = jnp.where(lane128 < HALF, -sine, 0.0)
                high_t[rows, :] = jnp.where(lane128 < HALF, 0.0, sine)
                kpos = lax.broadcasted_iota(jnp.int32, (slot, slot), 0)
                qpos = lax.broadcasted_iota(jnp.int32, (slot, slot), 1)
                seen = (kpos >= begins(qpos)) & (kpos <= qpos)
                bias_t[s] = jnp.where(seen, 0.0, -1e30).astype(f32)
                live = jnp.where(prow < e2, 1.0, 0.0)[:, 0:1]
                db[rows, :] = (db[rows, :].astype(f32) * live).astype(bf16)

        def chunks(rows_each, body):
            def step(i, carry):
                body(pl.ds(pl.multiple_of(i * rows_each, rows_each), rows_each))
                return carry

            lax.fori_loop(0, T // rows_each, step, 0)

        def norm_first():
            def body(r):
                s = tok[r, :].astype(f32)
                sc = lax.rsqrt(jnp.mean(s * s, axis=1, keepdims=True) + epsilon)
                na[r, :] = (s * sc * gains[0:1, :]).astype(bf16)
                stats[r, :] = jnp.broadcast_to(sc, (sc.shape[0], 128))

            chunks(128, body)

        def flat(w, n0, n):
            val = w[:, :, :, :, pl.ds(n0, n)]
            return val.reshape(-1, n)

        def project(w, o, turned):
            N = 256

            def step(i, carry):
                n0 = pl.multiple_of(i * N, N)
                a = mm(na[...], flat(w, n0, N))
                if turned:
                    for j in range(N // 128):
                        o[:, pl.ds(n0 + j * 128, 128)] = rope(
                            a[:, j * 128 : (j + 1) * 128], cos_t[...], low_t[...], high_t[...]
                        ).astype(bf16)
                else:
                    o[:, pl.ds(n0, N)] = a.astype(bf16)
                return carry

            lax.fori_loop(0, width // N, step, 0)

        def attend(first, count):
            def step(i, carry):
                s, pair = i // PAIRS, i % PAIRS
                rows = pl.ds(pl.multiple_of(s * slot, slot), slot)
                cs = pl.ds(pl.multiple_of(pair * 128, 128), 128)
                q2, k2, v2 = q[rows, cs], k[rows, cs], v[rows, cs]
                st = mm(split_heads(k2), q2, 1, 1)
                probs = []
                for h in range(2):
                    sc = st[h * slot : (h + 1) * slot] * FACTOR + bias_t[s]
                    top = jnp.max(sc, axis=0, keepdims=True)
                    e = jnp.exp(sc - top)
                    total = jnp.sum(e, axis=0, keepdims=True)
                    probs.append((e * (1.0 / total)).astype(bf16))
                    lse[s, pair, h : h + 1, :] = top + jnp.log(total)
                p = jnp.concatenate(probs, axis=0)
                ho[rows, cs] = mm(p, split_heads(v2), 0, 0).astype(bf16)
                return carry

            lax.fori_loop(first, first + count, step, 0)

        def middle():
            def body(r):
                s = tok[r, :].astype(f32) + mm(ho[r, :], wo[...].reshape(width, width))
                sc = lax.rsqrt(jnp.mean(s * s, axis=1, keepdims=True) + epsilon)
                smid[r, :] = s
                outacc[r, :] = s
                dnf[r, :] = jnp.zeros_like(s)
                nf[r, :] = (s * sc * gains[1:2, :]).astype(bf16)
                stats[r, :] = jnp.where(
                    lax.broadcasted_iota(jnp.int32, (sc.shape[0], 128), 1) == 0, stats[r, :], sc
                )

            chunks(256, body)

        def ffn(kk, i):
            wg, wu, wd = ((wg0, wu0, wd0), (wg1, wu1, wd1))[kk]
            G, D = held[3 * kk + i][0], held[3 * kk + 2][0]
            wg_n = wg[:, :, :, :, i * NB : (i + 1) * NB].reshape(width, NB)
            wu_n = wu[:, :, :, :, i * NB : (i + 1) * NB].reshape(width, NB)
            half = Z // 2
            wd_n = wd[i * half : (i + 1) * half].reshape(NB, width)

            def part(r):
                g = mm(nf[r, :], wg_n)
                u = mm(nf[r, :], wu_n)
                dh = mm(db[r, :], wd_n, 1, 1)
                sg = 1.0 / (1.0 + jnp.exp(-g))
                si = g * sg
                hs[r, :] = (si * u).astype(bf16)
                dus[r, :] = (dh * si).astype(bf16)
                dgs[r, :] = (dh * u * (sg * (1.0 + g * (1.0 - sg)))).astype(bf16)

            chunks(slot, part)
            outacc[...] += mm(hs[...], wd_n)
            dnf[...] += mm(dgs[...], wg_n, 1, 1)
            dnf[...] += mm(dus[...], wu_n, 1, 1)
            D[0, i] = mm(hs[...], db[...], 0, 0).astype(bf16).reshape(D.shape[2:])
            G[0] = mm(nf[...], dgs[...], 0, 0).astype(bf16).reshape(G.shape[1:])
            G[1] = mm(nf[...], dus[...], 0, 0).astype(bf16).reshape(G.shape[1:])

        def middle_back():
            C = 128

            def step(i, acc):
                r = pl.ds(pl.multiple_of(i * C, C), C)
                dn, s, sc = dnf[r, :], smid[r, :], stats[r, 1:2]
                w = dn * gains[1:2, :]
                acc = acc + jnp.sum((dn * (s * sc)).reshape(C // 8, 8, width), axis=0)
                back = sc * w - s * (sc * sc * sc * jnp.mean(w * s, axis=1, keepdims=True))
                dm = db[r, :].astype(f32) + back
                dnf[r, :] = dm
                db[r, :] = dm.astype(bf16)
                return acc

            acc = lax.fori_loop(0, T // C, step, jnp.zeros((8, width), f32))
            gg[0, 1:2] = jnp.sum(acc, axis=0, keepdims=True)

        def grad_out_proj():
            G = held[6][0]
            N = 256

            def step(i, carry):
                n = pl.ds(pl.multiple_of(i * N, N), N)
                val = mm(ho[...], db[:, n], 0, 0).astype(bf16)
                G[0, :, :, :, :, :, n] = val.reshape(G.shape[1:-1] + (N,))
                return carry

            lax.fori_loop(0, width // N, step, 0)

        def heads_back():
            for zi in range(Z):
                w = wo[zi].reshape(4 * R, width)
                nf[:, zi * 4 * R : (zi + 1) * 4 * R] = mm(db[...], w, 1, 1).astype(bf16)

        def attend_back(block):
            per_block = QN // 128

            def step(i, carry):
                s, pair = i // per_block, i % per_block + block * per_block
                rows = pl.ds(pl.multiple_of(s * slot, slot), slot)
                cs = pl.ds(pl.multiple_of(pair * 128, 128), 128)
                q2, k2, v2, d2 = q[rows, cs], k[rows, cs], v[rows, cs], nf[rows, cs]
                km = split_heads(k2)
                st = mm(km, q2, 1, 1)
                dp = mm(split_heads(v2), d2, 1, 1)
                probs, dscores = [], []
                for h in range(2):
                    part = slice(h * slot, (h + 1) * slot)
                    p = jnp.exp(st[part] * FACTOR + bias_t[s] - lse[s, pair, h : h + 1, :])
                    probs.append(p.astype(bf16))
                    dph = dp[part]
                    centre = jnp.sum(p * dph, axis=0, keepdims=True)
                    dscores.append((p * (dph - centre)).astype(bf16))
                p2 = jnp.concatenate(probs, axis=0)
                ds2 = jnp.concatenate(dscores, axis=0)
                co, lo, hi = cos_t[rows, :], -low_t[rows, :], -high_t[rows, :]
                v[rows, cs] = join_heads(mm(p2, d2)).astype(bf16)
                k[rows, cs] = rope(join_heads(mm(ds2, q2)) * FACTOR, co, lo, hi).astype(bf16)
                q[rows, cs] = rope(mm(ds2, km, 0, 0) * FACTOR, co, lo, hi).astype(bf16)
                return carry

            lax.fori_loop(0, slots * per_block, step, 0)
            G = held[7 + block][0]
            for a, grad in enumerate((q, k, v)):
                val = mm(na[...], grad[:, block * QN : (block + 1) * QN], 0, 0)
                G[a] = val.astype(bf16).reshape(G.shape[1:])

        def first_back():
            C = 256

            def step(i, acc):
                r = pl.ds(pl.multiple_of(i * C, C), C)
                dn = (
                    mm(q[r, :], wq[...].reshape(width, width), 1, 1)
                    + mm(k[r, :], wk[...].reshape(width, width), 1, 1)
                    + mm(v[r, :], wv[...].reshape(width, width), 1, 1)
                )
                s, sc = tok[r, :].astype(f32), stats[r, 0:1]
                w = dn * gains[0:1, :]
                acc = acc + jnp.sum((dn * (s * sc)).reshape(C // 8, 8, width), axis=0)
                back = sc * w - s * (sc * sc * sc * jnp.mean(w * s, axis=1, keepdims=True))
                tok[r, :] = (dnf[r, :] + back).astype(bf16)
                return acc

            acc = lax.fori_loop(0, T // C, step, jnp.zeros((8, width), f32))
            gg[0, 0:1] = jnp.sum(acc, axis=0, keepdims=True)

        ag_z(0)
        gn_start(0)
        ag_z(1)
        tables()
        gn_finish(0)
        gn_start(1)
        ag_tick(0)
        gn_finish(1)
        if NA > 2:
            gn_start(2)
        ag_tick(1)
        if NA > 2:
            gn_finish(2)
        gains[...] = gsum[NA]
        norm_first()
        ag_tick(2)
        ag_tick(3)
        project(wq, q, True)
        ag_tick(4)
        project(wk, k, True)
        ag_tick(5)
        project(wv, v, False)
        per_tick = slots * PAIRS // 4
        ag_tick(6)
        attend(0, per_tick)
        attend(per_tick, per_tick)
        ag_tick(7)
        attend(2 * per_tick, per_tick)
        attend(3 * per_tick, per_tick)
        ag_tick(8)
        middle()
        ag_tick(9)
        ffn(0, 0)
        rs_begin(0)
        ag_tick(10)
        ffn(0, 1)
        rs_tick()
        rs_begin(1)
        rs_begin(2)
        ag_tick(11)
        ag_tick(12)
        rs_tick()
        ffn(1, 0)
        rs_begin(3)
        rs_tick()
        ffn(1, 1)
        rs_begin(4)
        rs_begin(5)
        put(outacc, out_main)
        rs_tick()
        middle_back()
        grad_out_proj()
        rs_begin(6)
        rs_tick()
        heads_back()
        for b in range(QB):
            attend_back(b)
            rs_begin(7 + b)
            rs_tick()
        first_back()
        put(tok, out_tokens)
        i = 0
        gg_start(0)
        while progress or i < len(all_partners):
            rs_tick()
            if i < len(all_partners):
                gg_finish(i)
                i += 1
                if i < len(all_partners):
                    gg_start(i)
        gn.sent(*range(NA + len(all_partners)))
        put(gg.at[len(all_partners)], out_gains)
        for copy in outs:
            copy.wait()

    VM, HB = pltpu.VMEM, pl.BlockSpec(memory_space=pl.ANY)
    S = jax.ShapeDtypeStruct

    def full(rows_half, n):
        return VM((Z, 2, 2, rows_half, n), bf16)

    def piece_bufs(kind):
        a, r, n = dict(g=G_SHAPE, d=D_SHAPE, o=O_SHAPE, q=Q_SHAPE)[kind]
        return [
            VM((a, ZH, r, n), bf16),
            VM((a, ZH, 2, r, n // 2), bf16),
            VM((a, ZH, 2, r, n // 2), bf16),
            VM((Z - 1, a, r, n // 2), bf16),
            VM((a, 2, r, n), bf16),
        ]

    def grads_of(count, shape):
        a, r, n = shape
        return VM((count, a, ZH, 2, 2, 2, r, n), bf16)

    def first_of(count, shape):
        a, r, n = shape
        return VM((count, a, ZH, 2, 2, r, n), bf16)

    axes = 3 if Z == 4 else 2
    NL = 8 + 2 * (ff // NB) + 4 + 2 * slots
    scratch = [full(R, width)] * 4 + [full(R, FH), full(R, FH), full(RD, width)] * 2
    scratch += [VM((T, width), bf16)] * 6
    scratch += [VM((T, width), f32), VM((T, width), bf16), VM((T, width), bf16)]
    scratch += [VM((T, width), f32)] * 2
    scratch += [VM((T, 128), f32)] * 4
    scratch += [VM((slots, slot, slot), f32), VM((slots, PAIRS, 8, slot), f32)]
    scratch += [VM((T, NB), bf16)] * 3
    scratch += [VM((axes + 1, 8, width), f32), VM((axes, 8, width), f32), VM((8, width), f32)]
    scratch += [VM((axes + 3, 8, width), f32), VM((axes + 2, 8, width), f32)]
    scratch += [grads_of(2, G_SHAPE), grads_of(1, D_SHAPE), grads_of(1, O_SHAPE), grads_of(2, Q_SHAPE)]
    for kind, _ in PIECES:
        scratch += piece_bufs(kind)
    scratch += [first_of(4, G_SHAPE), first_of(2, D_SHAPE), first_of(1, O_SHAPE), first_of(QB, Q_SHAPE)]
    DMA = pltpu.SemaphoreType.DMA
    scratch += [DMA((NL,)), DMA((NAG, 17)), DMA((NAG, 17)), DMA((NRS, 10)), DMA((NRS, 10))]
    scratch += [DMA((2 * axes + 2,)), DMA((2 * axes + 2,)), DMA((NRS + 3,))]
    out_shape = [S((T, width), f32), S((T, width), bf16), S((8, width), f32)]
    for _, (a, r, n) in PIECES:
        out_shape.append(S((a, 2, r, n), bf16))
    call = pl.pallas_call(
        kernel,
        out_shape=out_shape,
        in_specs=[pl.BlockSpec(memory_space=pltpu.SMEM), pl.BlockSpec(memory_space=VM)] + [HB] * 9,
        out_specs=[HB] * len(out_shape),
        scratch_shapes=scratch,
        compiler_params=pltpu.CompilerParams(
            collective_id=0, has_side_effects=True, vmem_limit_bytes=66000000
        ),
    )

    def local(tokens, lengths, wq, wk, wv, wo, wg, wu, wd, gain_attn, gain_ffn, gradient):
        per = width // fs
        gains8 = jnp.zeros((8, 128), f32)
        gains8 = gains8.at[0, :per].set(gain_attn.astype(f32)).at[1, :per].set(gain_ffn.astype(f32))
        main, g_tok, gsums, *pieces = call(
            lengths, gains8, tokens, gradient, wq, wk, wv, wo, wg, wu, wd
        )
        f = lax.axis_index("fsdp")
        gg = lax.dynamic_slice(gsums, (0, f * per), (2, per))

        def columns(i):
            parts = jnp.stack([jnp.stack([pieces[3 * kk + b][i] for b in range(2)]) for kk in range(2)])
            parts = parts.reshape(2, 2, per, NB // 128, 128)
            return parts.transpose(2, 1, 3, 0, 4).reshape(per, ff).astype(f32)

        down = jnp.concatenate([pieces[3 * kk + 2].reshape(2 * RD, width) for kk in range(2)]).astype(f32)
        proj = pieces[6].reshape(per, width).astype(f32)
        qkv = [
            jnp.concatenate([pieces[7 + b][a].reshape(per, QN) for b in range(QB)], axis=1).astype(f32)
            for a in range(3)
        ]
        return (
            main.reshape(tokens.shape).astype(bf16),
            g_tok.reshape(tokens.shape),
            *qkv,
            proj,
            columns(0),
            columns(1),
            down,
            gg[0],
            gg[1],
        )

    return local


def layout(lengths, slot):
    pieces = lengths.shape[0]
    bounds = jnp.stack([jnp.sum(lengths[: j + 1]) for j in range(pieces)])
    places = lax.iota(jnp.int32, slot)
    piece_of = jnp.sum((places[:, None] >= bounds[None, :]).astype(jnp.int32), axis=1)
    piece_begins = bounds - lengths
    member = piece_of[:, None] == lax.iota(jnp.int32, pieces)[None, :]
    begins = jnp.sum(jnp.where(member, piece_begins[None, :], 0), axis=1)
    offsets = places - begins
    live = (piece_of < pieces - 1).astype(jnp.float32)
    visible = (piece_of[:, None] == piece_of[None, :]) & (places[None, :] <= places[:, None])
    return (offsets, live, visible)


def rotary(offsets, head_dim):
    half = head_dim // 2
    rates = jnp.power(10000.0, -2.0 * lax.iota(jnp.float32, half) / head_dim)
    angle = offsets.astype(jnp.float32)[:, None] * rates[None, :]
    angle = jnp.concatenate([angle, angle], axis=1)
    return (jnp.cos(angle), jnp.sin(angle))


def turn(values, cosine, sine, sign):
    half = values.shape[-1] // 2
    swapped = jnp.concatenate([-values[..., half:], values[..., :half]], axis=-1)
    return values * cosine[:, None, :] + sign * swapped * sine[:, None, :]


def matmul(left, right):
    return jnp.dot(left, right, preferred_element_type=jnp.float32)


def left_inner(left, right):
    return lax.dot_general(
        left, right, (((0,), (0,)), ((), ())), preferred_element_type=jnp.float32
    )


def right_inner(left, right):
    return lax.dot_general(
        left, right, (((1,), (1,)), ((), ())), preferred_element_type=jnp.float32
    )


def norm_back(grad_normed, gain, stream, scale):
    weighted = grad_normed * gain.astype(jnp.float32)
    gain_grad = jnp.sum(grad_normed * stream * scale, axis=0)
    stream_grad = scale * weighted - stream * scale * scale * scale * jnp.mean(
        weighted * stream, axis=1, keepdims=True
    )
    return (stream_grad, gain_grad)


def forward_pass(tokens_slot, weights, cosine, sine, visible):
    w_query, w_key, w_value, w_out, w_gate, w_up, w_down, gain_attn, gain_ffn = weights
    slot = tokens_slot.shape[0]
    factor = HEAD_DIM ** (-0.5)
    stream = tokens_slot.astype(jnp.float32)
    scale_attn = lax.rsqrt(jnp.mean(stream * stream, axis=1, keepdims=True) + epsilon)
    normed_attn = (stream * scale_attn * gain_attn.astype(jnp.float32)).astype(jnp.bfloat16)
    query_rows = turn(
        matmul(normed_attn, w_query).reshape(slot, HEADS, HEAD_DIM), cosine, sine, 1.0
    ).astype(jnp.bfloat16)
    key_rows = turn(
        matmul(normed_attn, w_key).reshape(slot, HEADS, HEAD_DIM), cosine, sine, 1.0
    ).astype(jnp.bfloat16)
    value_rows = matmul(normed_attn, w_value).astype(jnp.bfloat16).reshape(slot, HEADS, HEAD_DIM)
    scores = (
        jnp.einsum("qhd,khd->hqk", query_rows, key_rows, preferred_element_type=jnp.float32)
        * factor
    )
    scores = jnp.where(visible[None], scores, -1e30)
    top = jnp.max(scores, axis=-1, keepdims=True)
    weights_exp = jnp.exp(scores - top)
    totals = jnp.sum(weights_exp, axis=-1, keepdims=True)
    probs = weights_exp / totals
    log_total = top + jnp.log(totals)
    mixed = jnp.einsum(
        "hqk,khd->qhd", probs.astype(jnp.bfloat16), value_rows, preferred_element_type=jnp.float32
    )
    heads_out = mixed.reshape(slot, HEADS * HEAD_DIM).astype(jnp.bfloat16)
    stream_mid = stream + matmul(heads_out, w_out)
    scale_ffn = lax.rsqrt(jnp.mean(stream_mid * stream_mid, axis=1, keepdims=True) + epsilon)
    normed_ffn = (stream_mid * scale_ffn * gain_ffn.astype(jnp.float32)).astype(jnp.bfloat16)
    gate_pre = matmul(normed_ffn, w_gate)
    up_branch = matmul(normed_ffn, w_up)
    hidden = (gate_pre * jax.nn.sigmoid(gate_pre) * up_branch).astype(jnp.bfloat16)
    result = stream_mid + matmul(hidden, w_down)
    kept = (
        stream,
        scale_attn,
        normed_attn,
        query_rows,
        key_rows,
        value_rows,
        log_total,
        heads_out,
        stream_mid,
        scale_ffn,
        normed_ffn,
        gate_pre,
        up_branch,
        hidden,
    )
    return (kept, result)


def backward_pass(kept, weights, cotangent, live, cosine, sine, visible):
    w_query, w_key, w_value, w_out, w_gate, w_up, w_down, gain_attn, gain_ffn = weights
    (
        stream,
        scale_attn,
        normed_attn,
        query_rows,
        key_rows,
        value_rows,
        log_total,
        heads_out,
        stream_mid,
        scale_ffn,
        normed_ffn,
        gate_pre,
        up_branch,
        hidden,
    ) = kept
    slot = stream.shape[0]
    factor = HEAD_DIM ** (-0.5)
    d_out = cotangent.astype(jnp.float32) * live[:, None]
    d_branch = d_out.astype(jnp.bfloat16)
    grad_down = left_inner(hidden, d_branch)
    d_hidden = right_inner(d_branch, w_down)
    sigma = jax.nn.sigmoid(gate_pre)
    d_gate = (d_hidden * up_branch * sigma * (1.0 + gate_pre * (1.0 - sigma))).astype(jnp.bfloat16)
    d_up = (d_hidden * gate_pre * sigma).astype(jnp.bfloat16)
    grad_gate = left_inner(normed_ffn, d_gate)
    grad_up = left_inner(normed_ffn, d_up)
    d_normed_ffn = right_inner(d_gate, w_gate) + right_inner(d_up, w_up)
    mid_back, grad_gain_ffn = norm_back(d_normed_ffn, gain_ffn, stream_mid, scale_ffn)
    d_mid = d_out + mid_back
    d_attn = d_mid.astype(jnp.bfloat16)
    grad_out_proj = left_inner(heads_out, d_attn)
    d_heads = right_inner(d_attn, w_out).astype(jnp.bfloat16).reshape(slot, HEADS, HEAD_DIM)
    scores = (
        jnp.einsum("qhd,khd->hqk", query_rows, key_rows, preferred_element_type=jnp.float32)
        * factor
    )
    probs = jnp.where(visible[None], jnp.exp(scores - log_total), 0.0)
    d_probs = jnp.einsum("qhd,khd->hqk", d_heads, value_rows, preferred_element_type=jnp.float32)
    d_values = jnp.einsum(
        "hqk,qhd->khd", probs.astype(jnp.bfloat16), d_heads, preferred_element_type=jnp.float32
    )
    d_values = d_values.astype(jnp.bfloat16).reshape(slot, HEADS * HEAD_DIM)
    centre = jnp.sum(probs * d_probs, axis=-1, keepdims=True)
    d_scores = (probs * (d_probs - centre)).astype(jnp.bfloat16)
    d_query_rot = (
        jnp.einsum("hqk,khd->qhd", d_scores, key_rows, preferred_element_type=jnp.float32) * factor
    )
    d_key_rot = (
        jnp.einsum("hqk,qhd->khd", d_scores, query_rows, preferred_element_type=jnp.float32)
        * factor
    )
    d_queries = (
        turn(d_query_rot, cosine, sine, -1.0).astype(jnp.bfloat16).reshape(slot, HEADS * HEAD_DIM)
    )
    d_keys = (
        turn(d_key_rot, cosine, sine, -1.0).astype(jnp.bfloat16).reshape(slot, HEADS * HEAD_DIM)
    )
    grad_query = left_inner(normed_attn, d_queries)
    grad_key = left_inner(normed_attn, d_keys)
    grad_value = left_inner(normed_attn, d_values)
    d_normed_attn = (
        right_inner(d_queries, w_query)
        + right_inner(d_keys, w_key)
        + right_inner(d_values, w_value)
    )
    stream_back, grad_gain_attn = norm_back(d_normed_attn, gain_attn, stream, scale_attn)
    grad_input = d_mid + stream_back
    grads = (
        grad_query,
        grad_key,
        grad_value,
        grad_out_proj,
        grad_gate,
        grad_up,
        grad_down,
        grad_gain_attn,
        grad_gain_ffn,
    )
    return (grads, grad_input)


def local_general(
    tokens, lengths, w_query, w_key, w_value, w_out, w_gate, w_up, w_down, gain_attn, gain_ffn,
    output_gradient,
):
    rows = (w_query, w_key, w_value, w_out, w_gate, w_up, w_down, gain_attn, gain_ffn)
    weights = tuple(lax.all_gather(w, "fsdp", axis=0, tiled=True) for w in rows)
    results, input_grads, totals = [], [], None
    for i in range(tokens.shape[0]):
        offsets, live, visible = layout(lengths[i], tokens.shape[1])
        cosine, sine = rotary(offsets, HEAD_DIM)
        kept, result = forward_pass(tokens[i], weights, cosine, sine, visible)
        grads, grad_input = backward_pass(
            kept, weights, output_gradient[i], live, cosine, sine, visible
        )
        results.append(result.astype(jnp.bfloat16))
        input_grads.append(grad_input.astype(jnp.bfloat16))
        totals = grads if totals is None else tuple(a + b for a, b in zip(totals, grads))
    shares = (lax.psum_scatter(g, "fsdp", scatter_dimension=0, tiled=True) for g in totals)
    summed = tuple(lax.psum(g, "dp") for g in shares)
    return (jnp.stack(results), jnp.stack(input_grads)) + summed


def solution(mesh):
    row, vec = P("fsdp", None), P("fsdp")
    wide = P(("dp", "fsdp"), None, None)
    in_specs = (wide, P(("dp", "fsdp"), None)) + (row,) * 7 + (vec, vec, wide)
    out_specs = (wide, wide) + (row,) * 7 + (vec, vec)

    def local(tokens, lengths, *rest):
        slots, slot, width = tokens.shape
        ff = rest[4].shape[1]
        if (mesh.shape["dp"], mesh.shape["fsdp"]) == (4, 8) and (width, ff) == (768, 2048):
            return build(mesh, slots, slot, width, ff)(tokens, lengths, *rest)
        return local_general(tokens, lengths, *rest)

    return jax.shard_map(local, mesh=mesh, in_specs=in_specs, out_specs=out_specs, check_vma=False)
```

```python
import math
import jax
import jax.numpy as jnp
from jax import lax
from jax.experimental import pallas as pl
from jax.experimental.pallas import tpu as pltpu
from jax.sharding import PartitionSpec as P

HEADS = 12
HEAD_DIM = 64
HALF = HEAD_DIM // 2
FACTOR = HEAD_DIM ** (-0.5)
epsilon = 1e-05
f32 = jnp.float32
bf16 = jnp.bfloat16
MESH = pl.DeviceIdType.MESH
VMEM_BYTES = 66_900_000
ALONG_Z_FIRST = (0, 5)

ORDER = (
    "Z0", "Z1", "Z2", "gs0", "tables", "F0", "gf0", "F1", "Z3", "D0", "F2", "Z4", "D1", "gf1",
    "C0", "F3", "Z5", "E0", "D2", "C1", "F4", "Z6", "gf2", "norm", "D3", "E1", "projq", "C2",
    "projk", "F5", "Z7", "E2", "projv", "D4", "att0", "att1", "C3", "F6", "Z8", "att2", "att3",
    "D5", "E3", "F7", "Z9", "mid", "C4", "F8", "D6", "E4", "C5", "F9", "E5", "D7", "C6", "D8",
    "E6", "ffnA0", "D9", "ffnC0", "R1_0", "C7", "ffnB0", "C8", "R2_0", "C9", "E7", "ffnA1",
    "E8", "E9", "ffnC1", "R1_1", "ffnB1", "ffnA2", "R2_1", "ffnC2", "R1_2", "ffnB2", "ffnA3",
    "R3_1", "R3_0", "R2_2", "ffnC3", "R1_3", "R1_4", "R1_5", "R4_1", "ffnB3", "R4_0", "R2_3",
    "midback", "R5_0", "R5_1", "R3_2", "R2_4", "R2_5", "go", "R1_6", "heads", "R6_0", "R3_3",
    "R6_1", "attb0", "R4_2", "R2_6", "R7_0", "R7_1", "wg0", "R1_7", "R3_4", "attb1", "R4_3",
    "R2_7", "wg1", "R1_8", "R3_6", "attb2", "R4_4", "R3_5", "R3_7", "R2_8", "R4_6", "wg2",
    "R1_9", "R5_2", "fbackA", "R4_5", "R4_7", "R5_3", "R2_9", "fbackB", "gg0", "R6_2", "R6_3",
    "R5_4", "R5_5", "R3_8", "outcast", "gh0", "R7_2", "R7_3", "R3_9", "R5_6", "R6_4", "R6_5",
    "R7_4", "R7_5", "R4_8", "R5_7", "gh1", "R4_9", "gh2", "R6_6", "R6_7", "R7_6", "R5_8",
    "R7_7", "R6_8", "R5_9", "gh3", "R7_8", "R6_9", "gh4", "R7_9",
)


def mm(a, b, ca=1, cb=0):
    return lax.dot_general(a, b, (((ca,), (cb,)), ((), ())), preferred_element_type=f32)


def rope(v, cosine, sine):
    lane = lax.broadcasted_iota(jnp.int32, v.shape, 1) % HEAD_DIM
    swapped = jnp.where(lane < HALF, pltpu.roll(v, 128 - HALF, 1), pltpu.roll(v, HALF, 1))
    return v * cosine + swapped * sine


def split_heads(x):
    lane = lax.broadcasted_iota(jnp.int32, x.shape, 1)
    zero = jnp.zeros_like(x)
    return jnp.where(lane < HEAD_DIM, x, zero), jnp.where(lane < HEAD_DIM, zero, x)


def stack2(pair, begin, end):
    return jnp.concatenate([pair[0][begin:end], pair[1][begin:end]], axis=0)


class Copies:
    def __init__(self, send, recv):
        self.send, self.recv, self.started = send, recv, {}

    def start(self, key, src, dst, device):
        copy = pltpu.make_async_remote_copy(
            src_ref=src,
            dst_ref=dst,
            send_sem=self.send.at[key],
            recv_sem=self.recv.at[key],
            device_id=device,
            device_id_type=MESH,
        )
        copy.start()
        self.started[key] = copy

    def arrived(self, key, dst, device):
        pltpu.make_async_remote_copy(
            src_ref=dst,
            dst_ref=dst,
            send_sem=self.send.at[key],
            recv_sem=self.recv.at[key],
            device_id=device,
            device_id_type=MESH,
        ).wait_recv()

    def sent(self, *keys):
        for key in keys:
            self.started.pop(key).wait_send()


def build(mesh, slots, slot, width, ff):
    dps, fs = mesh.shape["dp"], mesh.shape["fsdp"]
    Z, ZH = fs // 2, fs // 4
    T = slots * slot
    R, RD = width // fs // 2, ff // fs // 4
    per = width // fs
    NB = ff // Z
    QN = 256
    QB = width // QN
    PAIRS = width // 128
    NAG = 6 + Z
    G_SHAPE, D_SHAPE, Q_SHAPE = (2, R, NB), (1, RD, width), (3, R, QN)
    PIECES = (
        [("g", G_SHAPE)] * Z
        + [("d", D_SHAPE)] * 2
        + [("q", Q_SHAPE)] * (1 + QB)
    )
    NRS = len(PIECES)
    COUNTS = [4 if r in ALONG_Z_FIRST else 5 for r in range(NRS)]

    def kernel(
        lens, gains2, tokens, gradient, w_query, w_key, w_value, w_out, w_gate, w_up, w_down,
        out_main, out_tokens, out_gains, *rest,
    ):
        out_pieces, rest = rest[:NRS], rest[NRS:]
        wq, wk, wv, wo, wd = rest[:5]
        wgu, rest = rest[5 : 5 + Z], rest[5 + Z :]
        (
            tok, na, q, k, v, ho, smid, nf, db, dnf, outacc,
            cos_t, sin_t, stats, bias_t, lse, hs, dgs, dus,
            gsum, grecv, gains, gg, ggrecv,
            g_slots, d_slots, q_slots,
        ) = rest[:27]
        rest = rest[27:]
        bufs, rest = rest[: sum(COUNTS)], rest[sum(COUNTS) :]
        c1_g, c1_d, c1_q = rest[:3]
        (local_sem, ag_send, ag_recv, rs_send, rs_recv, gn_send, gn_recv, out_sem) = rest[3:]

        d, f = lax.axis_index("dp"), lax.axis_index("fsdp")
        y, c = d // 2, d % 2
        z, x = f // 2, f % 2
        nx, ny, nc = 1 - x, 1 - y, 1 - c
        dev_x, dev_y, dev_c = (d, z * 2 + nx), (ny * 2 + c, f), (y * 2 + nc, f)

        def dev_z(zt):
            return (d, zt * 2 + x)

        JS = [1, Z - 1] + list(range(2, Z - 1))

        partners = [dev_c, dev_x, dev_y] + [dev_z(lax.rem(z + j, Z)) for j in range(1, Z)]
        barrier = pltpu.get_barrier_semaphore()
        for p in partners:
            pl.semaphore_signal(barrier, inc=1, device_id=p, device_id_type=MESH)
        fetched = []

        def fetch(group, src, dst):
            copy = pltpu.make_async_copy(src, dst, local_sem.at[len(fetched)])
            copy.start()
            fetched.append((group, copy))

        def have(group):
            for g, copy in fetched:
                if g == group:
                    copy.wait()

        for i, (src, w) in enumerate(((w_query, wq), (w_key, wk), (w_value, wv), (w_out, wo))):
            for h in range(2):
                fetch(i, src.at[pl.ds(h * R, R)], w.at[z, x, h])
        for s in range(slots):
            fetch("tokens", tokens.at[s], tok.at[pl.ds(s * slot, slot)])
            fetch("tokens", gradient.at[s], db.at[pl.ds(s * slot, slot)])
        for h in range(2):
            for sub in range(2):
                rows = pl.ds((2 * h + sub) * RD, RD)
                fetch(4 + sub, w_down.at[rows], wd.at[z, x, h, sub])
        for i in range(Z):
            for a, src in enumerate((w_gate, w_up)):
                for h in range(2):
                    part = src.at[pl.ds(h * R, R), pl.ds(i * NB, NB)]
                    fetch(6 + i, part, wgu[i].at[a, z, x, h])

        ag = Copies(ag_send, ag_recv)

        def view(p, zi, xi, ci, at=slice(None)):
            if p < 4:
                return (wq, wk, wv, wo)[p].at[zi, xi, ci, :, at]
            if p < 6:
                return wd.at[zi, xi, ci, p - 4, :, at]
            return wgu[p - 6].at[:, zi, xi, ci, :, at]

        def cols(n, which):
            return pl.ds(pl.multiple_of(which * (n // 2), n // 2), n // 2)

        def side_of(p):
            return [3] if p % 2 else []

        def width_of(p):
            return width if p < 6 else NB

        def ag_z(p):
            have(p)
            n = width_of(p)
            for j in JS:
                r = view(p, z, x, c, cols(n, y))
                ag.start((p, j - 1), r, r, dev_z(lax.rem(z + j, Z)))
            r = view(p, z, x, c)
            ag.start((p, 3), r, r, dev_x)

        def ag_f(p):
            n = width_of(p)
            for j in JS:
                zs = lax.rem(z - j + Z, Z)
                r = view(p, zs, x, c, cols(n, y))
                ag.arrived((p, j - 1), r, dev_z(zs))
                ag.start((p, 3 + j), r, r, dev_x)
                ag.start((p, 6 + j), r, r, dev_y)

        def ag_d(p):
            n = width_of(p)
            for j in JS:
                zs = lax.rem(z - j + Z, Z)
                r = view(p, zs, nx, c, cols(n, y))
                ag.arrived((p, 3 + j), r, dev_x)
                if j not in side_of(p):
                    ag.start((p, 9 + j), r, r, dev_y)
                r = view(p, zs, x, c, cols(n, ny))
                ag.arrived((p, 6 + j), r, dev_y)
                if j in side_of(p):
                    ag.start((p, 9 + j), r, r, dev_x)
                r = view(p, zs, x, c)
                ag.start((p, 12 + j), r, r, dev_c)
            ag.arrived((p, 3), view(p, z, nx, c), dev_x)

        def ag_c(p):
            n = width_of(p)
            for j in JS:
                zs = lax.rem(z - j + Z, Z)
                r = view(p, zs, nx, c, cols(n, ny))
                ag.arrived((p, 9 + j), r, dev_x if j in side_of(p) else dev_y)
            r = view(p, slice(None), nx, c)
            ag.start((p, 16), r, r, dev_c)

        def ag_e(p):
            for j in JS:
                ag.arrived((p, 12 + j), view(p, lax.rem(z - j + Z, Z), x, nc), dev_c)
            ag.arrived((p, 16), view(p, slice(None), nx, nc), dev_c)
            ag.sent(*((p, i) for i in range(17)))

        rs = Copies(rs_send, rs_recv)
        held = []
        counts = {"g": 0, "d": 0, "q": 0}
        for r, (kind, _) in enumerate(PIECES):
            i = counts[kind]
            counts[kind] += 1
            slots_of = {"g": g_slots, "d": d_slots, "q": q_slots}[kind]
            c1_of = {"g": c1_g, "d": c1_d, "q": c1_q}[kind]
            held.append(
                (slots_of.at[i % slots_of.shape[0]], c1_of.at[i % c1_of.shape[0]])
                + tuple(bufs[sum(COUNTS[:r]) : sum(COUNTS[: r + 1])])
            )

        def rs_1(r):
            G, C1 = held[r][:2]
            rs.start((r, 0), G.at[:, :, :, :, nc], C1, dev_c)

        def rs_2(r):
            G, C1, XA, YB, S3, ZR, FIN = held[r]
            n = C1.shape[-1]
            rs.arrived((r, 0), C1, dev_c)
            for a in range(C1.shape[0]):
                for zh in range(ZH):
                    for zl in range(2):
                        C1[a, zh, zl] += G[a, zh, zl, :, c]
            rs.start((r, 1), C1.at[:, :, 0, nx], XA, dev_x)
            rs.start((r, 2), C1.at[:, :, 1, :, :, cols(n, ny)], YB, dev_y)
            rs.sent((r, 0))

        def rs_3(r):
            G, C1, XA, YB, S3, ZR, FIN = held[r]
            n = C1.shape[-1]
            rs.arrived((r, 1), XA, dev_x)
            XA[...] += C1[:, :, 0, x]
            rs.start((r, 3), XA.at[:, :, :, cols(n, ny)], S3.at[:, :, 0], dev_y)
            rs.arrived((r, 2), YB, dev_y)
            YB[...] += C1[:, :, 1, :, :, cols(n, y)]
            rs.start((r, 4), YB.at[:, :, nx], S3.at[:, :, 1], dev_x)
            rs.sent((r, 1), (r, 2))

        def rs_4(r):
            G, C1, XA, YB, S3, ZR, FIN = held[r]
            n = C1.shape[-1]
            rs.arrived((r, 3), S3.at[:, :, 0], dev_y)
            S3[:, :, 0] += XA[:, :, :, cols(n, y)]
            rs.arrived((r, 4), S3.at[:, :, 1], dev_x)
            S3[:, :, 1] += YB[:, :, x]
            for j in JS:
                zt = lax.rem(z + j, Z)
                rs.start((r, 4 + j), S3.at[:, zt // 2, zt % 2], ZR.at[j - 1], dev_z(zt))
            rs.sent((r, 3), (r, 4))

        def rs_5(r):
            G, C1, XA, YB, S3, ZR, FIN = held[r]
            n = C1.shape[-1]
            total = S3[:, z // 2, z % 2].astype(f32)
            for j in JS:
                rs.arrived((r, 4 + j), ZR.at[j - 1], dev_z(lax.rem(z - j + Z, Z)))
                total = total + ZR[j - 1].astype(f32)
            FIN[:, c, :, cols(n, y)] = total.astype(bf16)
            part = FIN.at[:, c, :, cols(n, y)]
            rs.start((r, 8), part, part, dev_y)
            rs.sent((r, 5), (r, 6), (r, 7))

        def zs_2(r):
            G, C1, ZR, XR, YR, FIN = held[r]
            rs.arrived((r, 0), C1, dev_c)
            for a in range(C1.shape[0]):
                for zh in range(ZH):
                    for zl in range(2):
                        C1[a, zh, zl] += G[a, zh, zl, :, c]
            for j in JS:
                zt = lax.rem(z + j, Z)
                rs.start((r, 4 + j), C1.at[:, zt // 2, zt % 2], ZR.at[j - 1], dev_z(zt))
            rs.sent((r, 0))

        def zs_3(r):
            G, C1, ZR, XR, YR, FIN = held[r]
            total = C1[:, z // 2, z % 2].astype(f32)
            for j in JS:
                rs.arrived((r, 4 + j), ZR.at[j - 1], dev_z(lax.rem(z - j + Z, Z)))
                total = total + ZR[j - 1].astype(f32)
            C1[:, z // 2, z % 2] = total.astype(bf16)
            rs.start((r, 1), C1.at[:, z // 2, z % 2, nx], XR, dev_x)
            rs.sent((r, 5), (r, 6), (r, 7))

        def zs_4(r):
            G, C1, ZR, XR, YR, FIN = held[r]
            rs.arrived((r, 1), XR, dev_x)
            XR[...] += C1[:, z // 2, z % 2, x]
            rs.start((r, 3), XR.at[:, :, cols(XR.shape[-1], ny)], YR, dev_y)
            rs.sent((r, 1))

        def zs_5(r):
            G, C1, ZR, XR, YR, FIN = held[r]
            n = XR.shape[-1]
            rs.arrived((r, 3), YR, dev_y)
            FIN[:, c, :, cols(n, y)] = XR[:, :, cols(n, y)] + YR[...]
            part = FIN.at[:, c, :, cols(n, y)]
            rs.start((r, 8), part, part, dev_y)
            rs.sent((r, 3))

        def rs_6(r):
            FIN = held[r][-1]
            n = FIN.shape[-1]
            rs.arrived((r, 8), FIN.at[:, c, :, cols(n, ny)], dev_y)
            rs.start((r, 9), FIN.at[:, c], FIN.at[:, c], dev_c)
            rs.sent((r, 8))

        outs = []

        def put(src, dst):
            copy = pltpu.make_async_copy(src, dst, out_sem.at[len(outs)])
            copy.start()
            outs.append(copy)

        def rs_7(r):
            FIN = held[r][-1]
            rs.arrived((r, 9), FIN.at[:, nc], dev_c)
            rs.sent((r, 9))
            put(FIN, out_pieces[r])

        gn = Copies(gn_send, gn_recv)
        axis_partners = [dev_x, dev_z(z ^ 1)] + ([dev_z(z ^ 2)] if Z == 4 else [])
        lane = lax.broadcasted_iota(jnp.int32, (per, width), 0)
        at = lax.broadcasted_iota(jnp.int32, (per, width), 1)
        place = jnp.where(lane == at % per, 1.0, 0.0).astype(bf16)
        spread = mm(gains2[...], place)
        spread = jnp.concatenate([spread, jnp.zeros((6, width), f32)], axis=0)
        mine = lax.broadcasted_iota(jnp.int32, (8, width), 1) // per == f
        gsum[0] = jnp.where(mine, spread, 0.0)

        def gn_start(i):
            gn.start(i, gsum.at[i], grecv.at[i], axis_partners[i])

        def gn_finish(i):
            gn.arrived(i, grecv.at[i], axis_partners[i])
            gsum[i + 1] = gsum[i] + grecv[i]

        all_partners = [dev_c, dev_y] + axis_partners
        NA = len(axis_partners)

        def gg_start(i):
            gn.start(NA + i, gg.at[i], ggrecv.at[i], all_partners[i])

        def gg_finish(i):
            gn.arrived(NA + i, ggrecv.at[i], all_partners[i])
            gg[i + 1] = gg[i] + ggrecv[i]

        lane128 = lax.broadcasted_iota(jnp.int32, (slot, 128), 1) % HEAD_DIM
        prow = lax.broadcasted_iota(jnp.int32, (slot, 128), 0)

        def tables():
            rate = jnp.exp(
                (lane128 % HALF).astype(f32) * (-2.0 * math.log(10000.0) / HEAD_DIM)
            )
            for s in range(slots):
                e0 = lens[s, 0]
                e1 = e0 + lens[s, 1]
                e2 = e1 + lens[s, 2]
                e3 = e2 + lens[s, 3]

                def begins(p):
                    b = jnp.where(p >= e0, e0, 0)
                    b = jnp.where(p >= e1, e1, b)
                    b = jnp.where(p >= e2, e2, b)
                    return jnp.where(p >= e3, e3, b)

                angle = (prow - begins(prow)).astype(f32) * rate
                sine = jnp.sin(angle)
                rows = slice(s * slot, (s + 1) * slot)
                cos_t[rows, :] = jnp.cos(angle)
                sin_t[rows, :] = jnp.where(lane128 < HALF, -sine, sine)
                kpos = lax.broadcasted_iota(jnp.int32, (slot, slot), 0)
                qpos = lax.broadcasted_iota(jnp.int32, (slot, slot), 1)
                seen = (kpos >= begins(qpos)) & (kpos <= qpos)
                bias_t[s] = jnp.where(seen, 0.0, -1e30).astype(f32)
                live = jnp.where(prow < e2, 1.0, 0.0)[:, 0:1]
                db[rows, :] = (db[rows, :].astype(f32) * live).astype(bf16)

        def chunks(rows_each, body):
            def step(i, carry):
                body(pl.ds(pl.multiple_of(i * rows_each, rows_each), rows_each))
                return carry

            lax.fori_loop(0, T // rows_each, step, 0)

        def norm_first():
            def body(r):
                s = tok[r, :].astype(f32)
                sc = lax.rsqrt(jnp.mean(s * s, axis=1, keepdims=True) + epsilon)
                na[r, :] = (s * sc * gains[0:1, :]).astype(bf16)
                stats[r, :] = jnp.broadcast_to(sc, (sc.shape[0], 128))

            chunks(128, body)

        def flat(w, n0, n):
            val = w[:, :, :, :, pl.ds(n0, n)]
            return val.reshape(-1, n)

        def project(w, o, turned, factor=1.0):
            N = 256

            def step(i, carry):
                n0 = pl.multiple_of(i * N, N)
                a = mm(na[...], flat(w, n0, N))
                if turned:
                    for j in range(N // 128):
                        turned_part = rope(
                            a[:, j * 128 : (j + 1) * 128], cos_t[...], sin_t[...]
                        )
                        o[:, pl.ds(n0 + j * 128, 128)] = (turned_part * factor).astype(bf16)
                else:
                    o[:, pl.ds(n0, N)] = a.astype(bf16)
                return carry

            lax.fori_loop(0, width // N, step, 0)

        THIRD = slot // 3
        BLOCKS = [(i * THIRD, (i + 1) * THIRD, (i + 1) * THIRD) for i in range(3)]

        def attend_one(s, pair):
            rows = pl.ds(pl.multiple_of(s * slot, slot), slot)
            cs = pl.ds(pl.multiple_of(pair * 128, 128), 128)
            q2, k2, v2 = q[rows, cs], k[rows, cs], v[rows, cs]
            km, vm, om = split_heads(k2), split_heads(v2), split_heads(jnp.ones_like(v2))
            for begin, end, seen in BLOCKS:
                st = mm(stack2(km, 0, seen), q2[begin:end], 1, 1)
                expo = []
                for h in range(2):
                    sc = st[h * seen : (h + 1) * seen] + bias_t[s, :seen, begin:end]
                    top = jnp.max(sc, axis=0, keepdims=True)
                    e = jnp.exp(sc - top)
                    total = jnp.sum(e, axis=0, keepdims=True)
                    expo.append(e.astype(bf16))
                    lse[s, pair, h : h + 1, begin:end] = top + jnp.log(total)
                right = jnp.concatenate([stack2(vm, 0, seen), stack2(om, 0, seen)], axis=1)
                o = mm(jnp.concatenate(expo, axis=0), right, 0, 0)
                here = pl.ds(pl.multiple_of(s * slot, slot) + begin, end - begin)
                ho[here, cs] = (o[:, :128] / o[:, 128:]).astype(bf16)

        def attend(first, count):
            UNROLL = 3

            def step(i, carry):
                for u in range(UNROLL):
                    n = first + i * UNROLL + u
                    attend_one(n // PAIRS, n % PAIRS)
                return carry

            lax.fori_loop(0, count // UNROLL, step, 0)

        def middle():
            def body(r):
                s = tok[r, :].astype(f32) + mm(ho[r, :], wo[...].reshape(width, width))
                sc = lax.rsqrt(jnp.mean(s * s, axis=1, keepdims=True) + epsilon)
                smid[r, :] = s
                outacc[r, :] = s
                dnf[r, :] = jnp.zeros_like(s)
                nf[r, :] = (s * sc * gains[1:2, :]).astype(bf16)
                stats[r, :] = jnp.where(
                    lax.broadcasted_iota(jnp.int32, (sc.shape[0], 128), 1) == 0, stats[r, :], sc
                )

            chunks(slot, body)

        def ffn_hidden(i):
            wg_n, wu_n = (wgu[i][a].reshape(width, NB) for a in range(2))
            wd_n = wd[i].reshape(NB, width)

            def part(r):
                g = mm(nf[r, :], wg_n)
                u = mm(nf[r, :], wu_n)
                dh = mm(db[r, :], wd_n, 1, 1)
                sg = 1.0 / (1.0 + jnp.exp(-g))
                si = g * sg
                hs[r, :] = (si * u).astype(bf16)
                dus[r, :] = (dh * si).astype(bf16)
                dgs[r, :] = (dh * u * (sg * (1.0 + g * (1.0 - sg)))).astype(bf16)

            chunks(slot, part)

        def ffn_streams(i):
            outacc[...] += mm(hs[...], wd[i].reshape(NB, width))
            dnf[...] += mm(dgs[...], wgu[i][0].reshape(width, NB), 1, 1)
            dnf[...] += mm(dus[...], wgu[i][1].reshape(width, NB), 1, 1)

        def ffn_grads(i):
            G = held[i][0]
            G[0] = mm(nf[...], dgs[...], 0, 0).astype(bf16).reshape(G.shape[1:])
            G[1] = mm(nf[...], dus[...], 0, 0).astype(bf16).reshape(G.shape[1:])
            gd = mm(hs[...], db[...], 0, 0).astype(bf16).reshape(2, 2, 2, RD, width)
            for sub in range(2):
                held[Z + sub][0][0, i // 2, i % 2] = gd[:, :, sub]

        def middle_back():
            C = 128

            def step(i, acc):
                r = pl.ds(pl.multiple_of(i * C, C), C)
                dn, s, sc = dnf[r, :], smid[r, :], stats[r, 1:2]
                w = dn * gains[1:2, :]
                acc = acc + jnp.sum((dn * (s * sc)).reshape(C // 8, 8, width), axis=0)
                back = sc * w - s * (sc * sc * sc * jnp.mean(w * s, axis=1, keepdims=True))
                dm = db[r, :].astype(f32) + back
                dnf[r, :] = dm
                db[r, :] = dm.astype(bf16)
                return acc

            acc = lax.fori_loop(0, T // C, step, jnp.zeros((8, width), f32))
            gg[0, 1:2] = jnp.sum(acc, axis=0, keepdims=True)

        def grad_out_proj():
            G = held[Z + 2][0]
            val = mm(ho[...], db[...], 0, 0).astype(bf16)
            for a in range(QB):
                G[a] = val[:, a * QN : (a + 1) * QN].reshape(G.shape[1:])

        def heads_back():
            for zi in range(ZH):
                w = wo[2 * zi : 2 * zi + 2].reshape(8 * R, width)
                nf[:, zi * 8 * R : (zi + 1) * 8 * R] = mm(db[...], w, 1, 1).astype(bf16)

        def attend_back_one(s, pair):
            rows = pl.ds(pl.multiple_of(s * slot, slot), slot)
            cs = pl.ds(pl.multiple_of(pair * 128, 128), 128)
            q2, k2, v2, d2 = q[rows, cs], k[rows, cs], v[rows, cs], nf[rows, cs]
            km, vm, qm, dm = (split_heads(a) for a in (k2, v2, q2, d2))
            B = THIRD
            P, S = {}, {}
            for name, begin, end, seen in ((0, 0, B, B), (1, B, slot, slot)):
                st = mm(stack2(km, 0, seen), q2[begin:end], 1, 1)
                dp = mm(stack2(vm, 0, seen), d2[begin:end], 1, 1)
                for h in range(2):
                    part = slice(h * seen, (h + 1) * seen)
                    p = jnp.exp(
                        st[part]
                        + bias_t[s, :seen, begin:end]
                        - lse[s, pair, h : h + 1, begin:end]
                    )
                    P[name, h] = p.astype(bf16)
                    centre = jnp.sum(p * dp[part], axis=0, keepdims=True)
                    S[name, h] = (p * (dp[part] - centre)).astype(bf16)

            def key_side(w, m):
                first = jnp.concatenate([w[0, 0], w[0, 1], w[1, 0][:B], w[1, 1][:B]], axis=1)
                top = mm(first, jnp.concatenate([stack2(m, 0, B), stack2(m, B, slot)], axis=0))
                rest = jnp.concatenate([w[1, 0][B:], w[1, 1][B:]], axis=1)
                return jnp.concatenate([top, mm(rest, stack2(m, B, slot))], axis=0)

            co, si = cos_t[rows, :], -sin_t[rows, :]
            v[rows, cs] = key_side(P, dm).astype(bf16)
            k[rows, cs] = rope(key_side(S, qm), co, si).astype(bf16)
            dq = [
                mm(jnp.concatenate([S[n, 0], S[n, 1]], axis=0), stack2(km, 0, seen), 0, 0)
                for n, seen in ((0, B), (1, slot))
            ]
            q[rows, cs] = rope(jnp.concatenate(dq, axis=0) * FACTOR, co, si).astype(bf16)

        def attend_back(block):
            per_block = QN // 128

            def step(i, carry):
                attend_back_one(i // per_block, i % per_block + block * per_block)
                return carry

            lax.fori_loop(0, slots * per_block, step, 0)

        def attend_grads(block):
            G = held[Z + 3 + block][0]
            at = slice(block * QN, (block + 1) * QN)
            grads = jnp.concatenate([q[:, at], k[:, at], v[:, at]], axis=1)
            val = mm(na[...], grads, 0, 0).astype(bf16)
            for a in range(3):
                G[a] = val[:, a * QN : (a + 1) * QN].reshape(G.shape[1:])

        def first_back():
            N = width // 2
            for i in range(2):
                def rows_of(w):
                    return w[i * ZH : (i + 1) * ZH].reshape(N, width)

                smid[:, i * N : (i + 1) * N] = (
                    mm(q[...], rows_of(wq), 1, 1)
                    + mm(k[...], rows_of(wk), 1, 1)
                    + mm(v[...], rows_of(wv), 1, 1)
                )

        def first_norm_back():
            C = 128

            def step(i, acc):
                r = pl.ds(pl.multiple_of(i * C, C), C)
                dn, s, sc = smid[r, :], tok[r, :].astype(f32), stats[r, 0:1]
                w = dn * gains[0:1, :]
                acc = acc + jnp.sum((dn * (s * sc)).reshape(C // 8, 8, width), axis=0)
                back = sc * w - s * (sc * sc * sc * jnp.mean(w * s, axis=1, keepdims=True))
                tok[r, :] = (dnf[r, :] + back).astype(bf16)
                return acc

            acc = lax.fori_loop(0, T // C, step, jnp.zeros((8, width), f32))
            gg[0, 0:1] = jnp.sum(acc, axis=0, keepdims=True)
            for s in range(slots):
                put(tok.at[pl.ds(s * slot, slot)], out_tokens.at[s])

        def result():
            parts = ((hs, 0, NB), (dus, NB, width - NB))
            for held_in, begin, n in parts:
                held_in[:, :n] = outacc[:, begin : begin + n].astype(bf16)
            for s in range(slots):
                for held_in, begin, n in parts:
                    part = held_in.at[pl.ds(s * slot, slot), pl.ds(0, n)]
                    put(part, out_main.at[s, :, pl.ds(begin, n)])

        def first_norm():
            gains[...] = gsum[NA]
            norm_first()

        def gains_step(i):
            gn_finish(i)
            if i + 1 < NA:
                gn_start(i + 1)

        def gain_grads_step(i):
            gg_finish(i)
            if i + 1 < len(all_partners):
                gg_start(i + 1)

        def reduce_step(k, r):
            plain = (rs_1, rs_2, rs_3, rs_4, rs_5, rs_6, rs_7)
            along_z = (rs_1, zs_2, zs_3, zs_4, zs_5, rs_6, rs_7)
            (along_z if r in ALONG_Z_FIRST else plain)[k - 1](r)

        quarter = slots * PAIRS // 4
        steps = {
            "Z": ag_z,
            "F": ag_f,
            "D": ag_d,
            "C": ag_c,
            "E": ag_e,
            "R": reduce_step,
            "gs": gn_start,
            "gf": gains_step,
            "gg": gg_start,
            "gh": gain_grads_step,
            "tables": tables,
            "norm": first_norm,
            "projq": lambda: project(wq, q, True, FACTOR),
            "projk": lambda: project(wk, k, True),
            "projv": lambda: project(wv, v, False),
            "att": lambda i: attend(i * quarter, quarter),
            "mid": middle,
            "ffnA": ffn_hidden,
            "ffnB": ffn_streams,
            "ffnC": ffn_grads,
            "outcast": result,
            "midback": middle_back,
            "go": grad_out_proj,
            "heads": heads_back,
            "attb": attend_back,
            "wg": attend_grads,
            "fbackA": first_back,
            "fbackB": first_norm_back,
        }
        pl.semaphore_wait(barrier, len(partners))
        for name in ORDER:
            if name == "tables":
                have("tokens")
            base = name.rstrip("0123456789_")
            steps[base](*(int(n) for n in name[len(base) :].split("_") if n))
        gn.sent(*range(NA + len(all_partners)))
        put(gg.at[len(all_partners)], out_gains)
        for copy in outs:
            copy.wait()

    VM, HB = pltpu.VMEM, pl.BlockSpec(memory_space=pl.ANY)
    S = jax.ShapeDtypeStruct

    def full(rows_half, n):
        return VM((Z, 2, 2, rows_half, n), bf16)

    def piece_bufs(i, kind):
        a, r, n = dict(g=G_SHAPE, d=D_SHAPE, q=Q_SHAPE)[kind]
        if i in ALONG_Z_FIRST:
            return [
                VM((Z - 1, a, 2, r, n), bf16),
                VM((a, r, n), bf16),
                VM((a, r, n // 2), bf16),
                VM((a, 2, r, n), bf16),
            ]
        return [
            VM((a, ZH, r, n), bf16),
            VM((a, ZH, 2, r, n // 2), bf16),
            VM((a, ZH, 2, r, n // 2), bf16),
            VM((Z - 1, a, r, n // 2), bf16),
            VM((a, 2, r, n), bf16),
        ]

    def grads_of(count, shape):
        a, r, n = shape
        return VM((count, a, ZH, 2, 2, 2, r, n), bf16)

    def first_of(count, shape):
        a, r, n = shape
        return VM((count, a, ZH, 2, 2, r, n), bf16)

    axes = 3 if Z == 4 else 2
    NL = 8 + 4 + 4 * Z + 2 * slots
    scratch = [full(R, width)] * 4 + [VM((Z, 2, 2, 2, RD, width), bf16)]
    scratch += [VM((2, Z, 2, 2, R, NB), bf16)] * Z
    scratch += [VM((T, width), bf16)] * 6
    scratch += [VM((T, width), f32), VM((T, width), bf16), VM((T, width), bf16)]
    scratch += [VM((T, width), f32)] * 2
    scratch += [VM((T, 128), f32)] * 3
    scratch += [VM((slots, slot, slot), f32), VM((slots, PAIRS, 8, slot), f32)]
    scratch += [VM((T, NB), bf16)] * 3
    scratch += [VM((axes + 1, 8, width), f32), VM((axes, 8, width), f32), VM((8, width), f32)]
    scratch += [VM((axes + 3, 8, width), f32), VM((axes + 2, 8, width), f32)]
    scratch += [grads_of(2, G_SHAPE), grads_of(2, D_SHAPE), grads_of(2, Q_SHAPE)]
    for i, (kind, _) in enumerate(PIECES):
        scratch += piece_bufs(i, kind)
    scratch += [first_of(4, G_SHAPE), first_of(2, D_SHAPE), first_of(1 + QB, Q_SHAPE)]
    DMA = pltpu.SemaphoreType.DMA
    scratch += [DMA((NL,)), DMA((NAG, 17)), DMA((NAG, 17)), DMA((NRS, 10)), DMA((NRS, 10))]
    scratch += [DMA((2 * axes + 2,)), DMA((2 * axes + 2,)), DMA((NRS + 1 + 3 * slots,))]
    out_shape = [S((slots, slot, width), bf16)] * 2 + [S((8, width), f32)]
    for _, (a, r, n) in PIECES:
        out_shape.append(S((a, 2, r, n), bf16))
    call = pl.pallas_call(
        kernel,
        out_shape=out_shape,
        in_specs=[pl.BlockSpec(memory_space=pltpu.SMEM), pl.BlockSpec(memory_space=VM)] + [HB] * 9,
        out_specs=[HB] * len(out_shape),
        scratch_shapes=scratch,
        compiler_params=pltpu.CompilerParams(
            collective_id=0, has_side_effects=True, vmem_limit_bytes=VMEM_BYTES
        ),
    )

    def finish(*refs):
        main, g_tok, gsums = refs[:3]
        pieces = refs[3 : 3 + NRS]
        o_main, o_tok, oq, ok, ov, oo, og, ou, od, o_gains = refs[3 + NRS : 13 + NRS]
        held, sem, in_sem = refs[13 + NRS : -2], refs[-2], refs[-1]
        fetched = [
            pltpu.make_async_copy(src, dst, in_sem.at[i])
            for i, (src, dst) in enumerate(zip((main, g_tok, gsums) + pieces, held))
        ]
        for copy in fetched:
            copy.start()
        for copy in fetched:
            copy.wait()
        gsums, pieces = held[2], held[3:]
        whole = [
            pltpu.make_async_copy(src, dst, sem.at[i])
            for i, (src, dst) in enumerate(((held[0], o_main), (held[1], o_tok)))
        ]
        for copy in whole:
            copy.start()
        for i in range(Z):
            for a, out in enumerate((og, ou)):
                out[:, i * NB : (i + 1) * NB] = pieces[i][a].astype(f32).reshape(per, NB)
        for c in range(2):
            for sub in range(2):
                rows = slice((2 * c + sub) * RD, (2 * c + sub + 1) * RD)
                od[rows, :] = pieces[Z + sub][0, c].astype(f32)
        for a in range(QB):
            oo[:, a * QN : (a + 1) * QN] = pieces[Z + 2][a].astype(f32).reshape(per, QN)
        for b in range(QB):
            for a, out in enumerate((oq, ok, ov)):
                out[:, b * QN : (b + 1) * QN] = pieces[Z + 3 + b][a].astype(f32).reshape(per, QN)
        f = lax.axis_index("fsdp")
        lane = lax.broadcasted_iota(jnp.int32, (width, 128), 1)
        at = lax.broadcasted_iota(jnp.int32, (width, 128), 0)
        pick = jnp.where((at == lane + f * per) & (lane < per), 1.0, 0.0).astype(bf16)
        g = gsums[...]
        total = jnp.zeros((8, 128), f32)
        for _ in range(3):
            term = g.astype(bf16)
            total = total + mm(term, pick)
            g = g - term.astype(f32)
        o_gains[...] = total
        for copy in whole:
            copy.wait()

    VS = pl.BlockSpec(memory_space=VM)
    post = pl.pallas_call(
        finish,
        out_shape=[S((slots, slot, width), bf16)] * 2
        + [S((per, width), f32)] * 4
        + [S((per, ff), f32)] * 2
        + [S((ff // fs, width), f32), S((8, 128), f32)],
        in_specs=[HB] * (3 + NRS),
        out_specs=[HB] * 2 + [VS] * 8,
        scratch_shapes=[VM(o.shape, o.dtype) for o in out_shape] + [DMA((2,)), DMA((3 + NRS,))],
        compiler_params=pltpu.CompilerParams(vmem_limit_bytes=VMEM_BYTES),
    )

    def local(tokens, lengths, wq, wk, wv, wo, wg, wu, wd, gain_attn, gain_ffn, gradient):
        gains2 = jnp.stack([gain_attn, gain_ffn])
        made = call(lengths, gains2, tokens, gradient, wq, wk, wv, wo, wg, wu, wd)
        *grads, gg = post(*made)
        return (*grads, gg[0, :per], gg[1, :per])

    return local


def layout(lengths, slot):
    pieces = lengths.shape[0]
    bounds = jnp.stack([jnp.sum(lengths[: j + 1]) for j in range(pieces)])
    places = lax.iota(jnp.int32, slot)
    piece_of = jnp.sum((places[:, None] >= bounds[None, :]).astype(jnp.int32), axis=1)
    piece_begins = bounds - lengths
    member = piece_of[:, None] == lax.iota(jnp.int32, pieces)[None, :]
    begins = jnp.sum(jnp.where(member, piece_begins[None, :], 0), axis=1)
    offsets = places - begins
    live = (piece_of < pieces - 1).astype(jnp.float32)
    visible = (piece_of[:, None] == piece_of[None, :]) & (places[None, :] <= places[:, None])
    return (offsets, live, visible)


def rotary(offsets, head_dim):
    half = head_dim // 2
    rates = jnp.power(10000.0, -2.0 * lax.iota(jnp.float32, half) / head_dim)
    angle = offsets.astype(jnp.float32)[:, None] * rates[None, :]
    angle = jnp.concatenate([angle, angle], axis=1)
    return (jnp.cos(angle), jnp.sin(angle))


def turn(values, cosine, sine, sign):
    half = values.shape[-1] // 2
    swapped = jnp.concatenate([-values[..., half:], values[..., :half]], axis=-1)
    return values * cosine[:, None, :] + sign * swapped * sine[:, None, :]


def matmul(left, right):
    return jnp.dot(left, right, preferred_element_type=jnp.float32)


def left_inner(left, right):
    return lax.dot_general(
        left, right, (((0,), (0,)), ((), ())), preferred_element_type=jnp.float32
    )


def right_inner(left, right):
    return lax.dot_general(
        left, right, (((1,), (1,)), ((), ())), preferred_element_type=jnp.float32
    )


def norm_back(grad_normed, gain, stream, scale):
    weighted = grad_normed * gain.astype(jnp.float32)
    gain_grad = jnp.sum(grad_normed * stream * scale, axis=0)
    stream_grad = scale * weighted - stream * scale * scale * scale * jnp.mean(
        weighted * stream, axis=1, keepdims=True
    )
    return (stream_grad, gain_grad)


def forward_pass(tokens_slot, weights, cosine, sine, visible):
    w_query, w_key, w_value, w_out, w_gate, w_up, w_down, gain_attn, gain_ffn = weights
    slot = tokens_slot.shape[0]
    factor = HEAD_DIM ** (-0.5)
    stream = tokens_slot.astype(jnp.float32)
    scale_attn = lax.rsqrt(jnp.mean(stream * stream, axis=1, keepdims=True) + epsilon)
    normed_attn = (stream * scale_attn * gain_attn.astype(jnp.float32)).astype(jnp.bfloat16)
    query_rows = turn(
        matmul(normed_attn, w_query).reshape(slot, HEADS, HEAD_DIM), cosine, sine, 1.0
    ).astype(jnp.bfloat16)
    key_rows = turn(
        matmul(normed_attn, w_key).reshape(slot, HEADS, HEAD_DIM), cosine, sine, 1.0
    ).astype(jnp.bfloat16)
    value_rows = matmul(normed_attn, w_value).astype(jnp.bfloat16).reshape(slot, HEADS, HEAD_DIM)
    scores = (
        jnp.einsum("qhd,khd->hqk", query_rows, key_rows, preferred_element_type=jnp.float32)
        * factor
    )
    scores = jnp.where(visible[None], scores, -1e30)
    top = jnp.max(scores, axis=-1, keepdims=True)
    weights_exp = jnp.exp(scores - top)
    totals = jnp.sum(weights_exp, axis=-1, keepdims=True)
    probs = weights_exp / totals
    log_total = top + jnp.log(totals)
    mixed = jnp.einsum(
        "hqk,khd->qhd", probs.astype(jnp.bfloat16), value_rows, preferred_element_type=jnp.float32
    )
    heads_out = mixed.reshape(slot, HEADS * HEAD_DIM).astype(jnp.bfloat16)
    stream_mid = stream + matmul(heads_out, w_out)
    scale_ffn = lax.rsqrt(jnp.mean(stream_mid * stream_mid, axis=1, keepdims=True) + epsilon)
    normed_ffn = (stream_mid * scale_ffn * gain_ffn.astype(jnp.float32)).astype(jnp.bfloat16)
    gate_pre = matmul(normed_ffn, w_gate)
    up_branch = matmul(normed_ffn, w_up)
    hidden = (gate_pre * jax.nn.sigmoid(gate_pre) * up_branch).astype(jnp.bfloat16)
    result = stream_mid + matmul(hidden, w_down)
    kept = (
        stream,
        scale_attn,
        normed_attn,
        query_rows,
        key_rows,
        value_rows,
        log_total,
        heads_out,
        stream_mid,
        scale_ffn,
        normed_ffn,
        gate_pre,
        up_branch,
        hidden,
    )
    return (kept, result)


def backward_pass(kept, weights, cotangent, live, cosine, sine, visible):
    w_query, w_key, w_value, w_out, w_gate, w_up, w_down, gain_attn, gain_ffn = weights
    (
        stream,
        scale_attn,
        normed_attn,
        query_rows,
        key_rows,
        value_rows,
        log_total,
        heads_out,
        stream_mid,
        scale_ffn,
        normed_ffn,
        gate_pre,
        up_branch,
        hidden,
    ) = kept
    slot = stream.shape[0]
    factor = HEAD_DIM ** (-0.5)
    d_out = cotangent.astype(jnp.float32) * live[:, None]
    d_branch = d_out.astype(jnp.bfloat16)
    grad_down = left_inner(hidden, d_branch)
    d_hidden = right_inner(d_branch, w_down)
    sigma = jax.nn.sigmoid(gate_pre)
    d_gate = (d_hidden * up_branch * sigma * (1.0 + gate_pre * (1.0 - sigma))).astype(jnp.bfloat16)
    d_up = (d_hidden * gate_pre * sigma).astype(jnp.bfloat16)
    grad_gate = left_inner(normed_ffn, d_gate)
    grad_up = left_inner(normed_ffn, d_up)
    d_normed_ffn = right_inner(d_gate, w_gate) + right_inner(d_up, w_up)
    mid_back, grad_gain_ffn = norm_back(d_normed_ffn, gain_ffn, stream_mid, scale_ffn)
    d_mid = d_out + mid_back
    d_attn = d_mid.astype(jnp.bfloat16)
    grad_out_proj = left_inner(heads_out, d_attn)
    d_heads = right_inner(d_attn, w_out).astype(jnp.bfloat16).reshape(slot, HEADS, HEAD_DIM)
    scores = (
        jnp.einsum("qhd,khd->hqk", query_rows, key_rows, preferred_element_type=jnp.float32)
        * factor
    )
    probs = jnp.where(visible[None], jnp.exp(scores - log_total), 0.0)
    d_probs = jnp.einsum("qhd,khd->hqk", d_heads, value_rows, preferred_element_type=jnp.float32)
    d_values = jnp.einsum(
        "hqk,qhd->khd", probs.astype(jnp.bfloat16), d_heads, preferred_element_type=jnp.float32
    )
    d_values = d_values.astype(jnp.bfloat16).reshape(slot, HEADS * HEAD_DIM)
    centre = jnp.sum(probs * d_probs, axis=-1, keepdims=True)
    d_scores = (probs * (d_probs - centre)).astype(jnp.bfloat16)
    d_query_rot = (
        jnp.einsum("hqk,khd->qhd", d_scores, key_rows, preferred_element_type=jnp.float32) * factor
    )
    d_key_rot = (
        jnp.einsum("hqk,qhd->khd", d_scores, query_rows, preferred_element_type=jnp.float32)
        * factor
    )
    d_queries = (
        turn(d_query_rot, cosine, sine, -1.0).astype(jnp.bfloat16).reshape(slot, HEADS * HEAD_DIM)
    )
    d_keys = (
        turn(d_key_rot, cosine, sine, -1.0).astype(jnp.bfloat16).reshape(slot, HEADS * HEAD_DIM)
    )
    grad_query = left_inner(normed_attn, d_queries)
    grad_key = left_inner(normed_attn, d_keys)
    grad_value = left_inner(normed_attn, d_values)
    d_normed_attn = (
        right_inner(d_queries, w_query)
        + right_inner(d_keys, w_key)
        + right_inner(d_values, w_value)
    )
    stream_back, grad_gain_attn = norm_back(d_normed_attn, gain_attn, stream, scale_attn)
    grad_input = d_mid + stream_back
    grads = (
        grad_query,
        grad_key,
        grad_value,
        grad_out_proj,
        grad_gate,
        grad_up,
        grad_down,
        grad_gain_attn,
        grad_gain_ffn,
    )
    return (grads, grad_input)


def local_general(
    tokens, lengths, w_query, w_key, w_value, w_out, w_gate, w_up, w_down, gain_attn, gain_ffn,
    output_gradient,
):
    rows = (w_query, w_key, w_value, w_out, w_gate, w_up, w_down, gain_attn, gain_ffn)
    weights = tuple(lax.all_gather(w, "fsdp", axis=0, tiled=True) for w in rows)
    results, input_grads, totals = [], [], None
    for i in range(tokens.shape[0]):
        offsets, live, visible = layout(lengths[i], tokens.shape[1])
        cosine, sine = rotary(offsets, HEAD_DIM)
        kept, result = forward_pass(tokens[i], weights, cosine, sine, visible)
        grads, grad_input = backward_pass(
            kept, weights, output_gradient[i], live, cosine, sine, visible
        )
        results.append(result.astype(jnp.bfloat16))
        input_grads.append(grad_input.astype(jnp.bfloat16))
        totals = grads if totals is None else tuple(a + b for a, b in zip(totals, grads))
    shares = (lax.psum_scatter(g, "fsdp", scatter_dimension=0, tiled=True) for g in totals)
    summed = tuple(lax.psum(g, "dp") for g in shares)
    return (jnp.stack(results), jnp.stack(input_grads)) + summed


def solution(mesh):
    row, vec = P("fsdp", None), P("fsdp")
    wide = P(("dp", "fsdp"), None, None)
    in_specs = (wide, P(("dp", "fsdp"), None)) + (row,) * 7 + (vec, vec, wide)
    out_specs = (wide, wide) + (row,) * 7 + (vec, vec)

    def local(tokens, lengths, *rest):
        slots, slot, width = tokens.shape
        ff = rest[4].shape[1]
        if (mesh.shape["dp"], mesh.shape["fsdp"]) == (4, 8) and (width, ff) == (768, 2048):
            return build(mesh, slots, slot, width, ff)(tokens, lengths, *rest)
        return local_general(tokens, lengths, *rest)

    return jax.shard_map(local, mesh=mesh, in_specs=in_specs, out_specs=out_specs, check_vma=False)
```

```python
import functools
import math
import jax
import jax.numpy as jnp
from jax import lax
from jax.experimental import pallas as pl
from jax.experimental.pallas import tpu as pltpu
from jax.sharding import PartitionSpec as P

HEADS = 12
HEAD_DIM = 64
HALF = HEAD_DIM // 2
FACTOR = HEAD_DIM ** (-0.5)
epsilon = 1e-05
f32 = jnp.float32
bf16 = jnp.bfloat16
MESH = pl.DeviceIdType.MESH
VMEM_BYTES = 66_900_000
ALONG_Z_FIRST = (1, 5)
OVER_X = (1, 2, 3, 6, 9, 10, 11)

ORDER = (
    0, 2000, 1, 2, 3000, 2100, 100, 101, 3, 200, 102, 4, 2101, 201, 300, 103, 5, 400, 202, 301,
    104, 6, 2102, 3100, 401, 203, 3200, 302, 105, 7, 3201, 204, 402, 3202, 303, 106, 107, 8, 9,
    3300, 205, 403, 3301, 304, 3302, 3303, 3400, 206, 108, 10, 404, 207, 109, 11, 305, 405,
    3500, 306, 3501, 110, 3700, 1100, 307, 208, 111, 406, 3600, 209, 1200, 407, 3502, 3503,
    3701, 1101, 210, 308, 3601, 211, 309, 1201, 408, 409, 3504, 3505, 1300, 3702, 1102, 310,
    311, 3602, 1400, 1202, 410, 411, 3506, 3507, 3703, 1103, 1104, 1105, 3603, 1302, 3800, 1204,
    1301, 1203, 3900, 1106, 1205, 1402, 4000, 4100, 1206, 1500, 4101, 1304, 4200, 1107, 1401,
    4102, 4103, 1207, 1303, 4201, 1108, 4104, 1600, 1306, 4105, 1208, 1700, 1404, 1501, 4202,
    1109, 4300, 1307, 1305, 4301, 1403, 1209, 4400, 2200, 1406, 1502, 4500, 2300, 1308, 1504,
    1601, 1407, 1701, 1405, 1503, 1309, 1602, 2301, 1506, 1702, 1408, 1604, 2302, 1505, 1507,
    1704, 1603, 1409, 1703, 1606, 1508, 2303, 1605, 1706, 1607, 1608, 1705, 1707, 1509, 1708,
    2304, 1609, 1709,
)


def mm(a, b, ca=1, cb=0):
    return lax.dot_general(a, b, (((ca,), (cb,)), ((), ())), preferred_element_type=f32)


def rope(v, cosine, sine):
    lane = lax.broadcasted_iota(jnp.int32, v.shape, 1) % HEAD_DIM
    swapped = jnp.where(lane < HALF, pltpu.roll(v, 128 - HALF, 1), pltpu.roll(v, HALF, 1))
    return v * cosine + swapped * sine


def split_heads(x):
    lane = lax.broadcasted_iota(jnp.int32, x.shape, 1)
    zero = jnp.zeros_like(x)
    return jnp.where(lane < HEAD_DIM, x, zero), jnp.where(lane < HEAD_DIM, zero, x)


def stack2(pair, begin, end):
    return jnp.concatenate([pair[0][begin:end], pair[1][begin:end]], axis=0)


class Copies:
    def __init__(self, send, recv):
        self.send, self.recv, self.started = send, recv, {}

    def start(self, key, src, dst, device, there=None):
        copy = pltpu.make_async_remote_copy(
            src_ref=src,
            dst_ref=dst,
            send_sem=self.send.at[key],
            recv_sem=self.recv.at[there or key],
            device_id=device,
            device_id_type=MESH,
        )
        copy.start()
        self.started[key] = copy

    def arrived(self, key, dst, device):
        pltpu.make_async_remote_copy(
            src_ref=dst,
            dst_ref=dst,
            send_sem=self.send.at[key],
            recv_sem=self.recv.at[key],
            device_id=device,
            device_id_type=MESH,
        ).wait_recv()

    def gone(self, key, src, device):
        pltpu.make_async_remote_copy(
            src_ref=src,
            dst_ref=src,
            send_sem=self.send.at[key],
            recv_sem=self.recv.at[key],
            device_id=device,
            device_id_type=MESH,
        ).wait_send()

    def sent(self, *keys):
        for key in keys:
            self.started.pop(key).wait_send()


def build(mesh, slots, slot, width, ff):
    dps, fs = mesh.shape["dp"], mesh.shape["fsdp"]
    Z, ZH = fs // 2, fs // 4
    T = slots * slot
    R, RD = width // fs // 2, ff // fs // 4
    per = width // fs
    NB = ff // Z
    QN = 256
    QB = width // QN
    PAIRS = width // 128
    NAG = 4 + 2 * Z
    G_SHAPE, D_SHAPE, Q_SHAPE = (2, R, NB), (1, RD, width), (3, R, QN)
    PIECES = (
        [(0, G_SHAPE)] * Z
        + [(1, D_SHAPE)] * 2
        + [(2, Q_SHAPE)] * (1 + QB)
    )
    NRS = len(PIECES)
    COUNTS = [4 if r in ALONG_Z_FIRST else 5 for r in range(NRS)]

    def kernel(
        lens, gain_first, gain_second, tokens, gradient, w_query, w_key, w_value, w_out, w_gate, w_up, w_down,
        out_main, out_tokens, out_gains, *rest,
    ):
        out_pieces, rest = rest[:NRS], rest[NRS:]
        wq, wk, wv, wo, wd = rest[:5]
        wgu, rest = rest[5 : 5 + Z], rest[5 + Z :]
        (
            tok, na, q, k, v, ho, smid, nf, db, dnf, outacc,
            cos_t, sin_t, stats, bias_t, lse, hs, dgs, dus,
            gsum, grecv, gains, gg, ggrecv,
            g_slots, d_slots, q_slots,
        ) = rest[:27]
        rest = rest[27:]
        bufs, rest = rest[: sum(COUNTS)], rest[sum(COUNTS) :]
        c1_g, c1_d, c1_q = rest[:3]
        (local_sem, ag_send, ag_recv, rs_send, rs_recv, gn_send, gn_recv, out_sem) = rest[3:]

        d, f = lax.axis_index("dp"), lax.axis_index("fsdp")
        y, c = d // 2, d % 2
        z, x = f // 2, f % 2
        nx, ny, nc = 1 - x, 1 - y, 1 - c
        dev_x, dev_y, dev_c = (d, z * 2 + nx), (ny * 2 + c, f), (y * 2 + nc, f)

        def dev_z(zt):
            return (d, zt * 2 + x)

        JS = [1, Z - 1] + list(range(2, Z - 1))

        partners = [dev_c, dev_x, dev_y] + [dev_z(lax.rem(z + j, Z)) for j in range(1, Z)]
        barrier = pltpu.get_barrier_semaphore()
        for p in partners:
            pl.semaphore_signal(barrier, inc=1, device_id=p, device_id_type=MESH)
        fetched = []
        TOKENS, DOWN = -1, -2

        def fetch(group, src, dst):
            copy = pltpu.make_async_copy(src, dst, local_sem.at[len(fetched)])
            copy.start()
            fetched.append((group, copy))

        def have(group):
            for g, copy in fetched:
                if g == group:
                    copy.wait()

        for i, (src, w) in enumerate(((w_query, wq), (w_key, wk), (w_value, wv), (w_out, wo))):
            for h in range(2):
                fetch(i, src.at[pl.ds(h * R, R)], w.at[z, x, h])
        for s in range(slots):
            fetch(TOKENS, tokens.at[s], tok.at[pl.ds(s * slot, slot)])
            fetch(TOKENS, gradient.at[s], db.at[pl.ds(s * slot, slot)])
        for h in range(2):
            fetch(DOWN, w_down.at[pl.ds(2 * h * RD, 2 * RD)], wd.at[z, x, h])
        for i in range(Z):
            for a, src in enumerate((w_gate, w_up)):
                for h in range(2):
                    part = src.at[pl.ds(h * R, R), pl.ds(i * NB, NB)]
                    fetch(4 + 2 * i, part, wgu[i].at[a, z, x, h])

        ag = Copies(ag_send, ag_recv)

        def view(p, zi, xi, ci, at=slice(None)):
            if p < 4:
                return (wq, wk, wv, wo)[p].at[zi, xi, ci, :, at]
            return wgu[p // 2 - 2].at[:, zi, xi, ci, :, at]

        def cols(n, which):
            return pl.ds(pl.multiple_of(which * (n // 2), n // 2), n // 2)

        def side_of(p):
            return [3] if p in OVER_X else []

        def width_of(p):
            return width if p < 4 else NB

        def ag_z(p):
            have(p)
            n = width_of(p)
            for j in JS:
                r = view(p, z, x, c, cols(n, y))
                ag.start((p, j - 1), r, r, dev_z(lax.rem(z + j, Z)))
            r = view(p, z, x, c)
            ag.start((p, 3), r, r, dev_x)

        def ag_f(p):
            n = width_of(p)
            for j in JS:
                zs = lax.rem(z - j + Z, Z)
                r = view(p, zs, x, c, cols(n, y))
                ag.arrived((p, j - 1), r, dev_z(zs))
                ag.start((p, 3 + j), r, r, dev_x)
                ag.start((p, 6 + j), r, r, dev_y)

        def ag_d(p):
            n = width_of(p)
            for j in JS:
                zs = lax.rem(z - j + Z, Z)
                r = view(p, zs, nx, c, cols(n, y))
                ag.arrived((p, 3 + j), r, dev_x)
                if j not in side_of(p):
                    ag.start((p, 9 + j), r, r, dev_y)
                r = view(p, zs, x, c, cols(n, ny))
                ag.arrived((p, 6 + j), r, dev_y)
                if j in side_of(p):
                    ag.start((p, 9 + j), r, r, dev_x)
                r = view(p, zs, x, c)
                ag.start((p, 12 + j), r, r, dev_c)
            ag.arrived((p, 3), view(p, z, nx, c), dev_x)

        def ag_c(p):
            n = width_of(p)
            for j in JS:
                zs = lax.rem(z - j + Z, Z)
                r = view(p, zs, nx, c, cols(n, ny))
                ag.arrived((p, 9 + j), r, dev_x if j in side_of(p) else dev_y)
            r = view(p, slice(None), nx, c)
            ag.start((p, 16), r, r, dev_c)

        def ag_e(p):
            for j in JS:
                ag.arrived((p, 12 + j), view(p, lax.rem(z - j + Z, Z), x, nc), dev_c)
            ag.arrived((p, 16), view(p, slice(None), nx, nc), dev_c)
            ag.sent(*((p, i) for i in range(17)))

        def from_plane(step):
            def run(p):
                if p < 4 or p % 2 == 0:
                    plain[step](p)
                else:
                    by_plane[step](p, p // 2 - 2)

            return run

        zs_to = [dev_z(i) for i in range(Z)]

        def down_z(p, i):
            if i == 0:
                have(DOWN)

            @pl.when(z == i)
            def _():
                r = wd.at[i, x, c, :, cols(width, y)]
                for j in JS:
                    ag.start((p, j - 1), r, r, zs_to[(i + j) % Z], (p, 0))
                r = wd.at[i, x, c]
                ag.start((p, 3), r, r, dev_x)

        def down_f(p, i):
            @pl.when(z != i)
            def _():
                r = wd.at[i, x, c, :, cols(width, y)]
                ag.arrived((p, 0), r, zs_to[i])
                ag.start((p, 4), r, r, dev_x)
                ag.start((p, 5), r, r, dev_y)

        def down_d(p, i):
            @pl.when(z != i)
            def _():
                r = wd.at[i, nx, c, :, cols(width, y)]
                ag.arrived((p, 4), r, dev_x)
                if p not in OVER_X:
                    ag.start((p, 6), r, r, dev_y)
                r = wd.at[i, x, c, :, cols(width, ny)]
                ag.arrived((p, 5), r, dev_y)
                if p in OVER_X:
                    ag.start((p, 6), r, r, dev_x)
                r = wd.at[i, x, c]
                ag.start((p, 7), r, r, dev_c)

            @pl.when(z == i)
            def _():
                ag.arrived((p, 3), wd.at[i, nx, c], dev_x)

        def down_c(p, i):
            @pl.when(z != i)
            def _():
                ag.arrived((p, 6), wd.at[i, nx, c, :, cols(width, ny)], (dev_y, dev_x)[p in OVER_X])

            r = wd.at[i, nx, c]
            ag.start((p, 8), r, r, dev_c)

        def down_e(p, i):
            half = wd.at[i, x, c, :, cols(width, y)]

            @pl.when(z != i)
            def _():
                ag.arrived((p, 7), wd.at[i, x, nc], dev_c)
                ag.gone((p, 4), half, dev_x)
                ag.gone((p, 5), half, dev_y)
                ag.gone((p, 6), half, (dev_y, dev_x)[p in OVER_X])
                ag.gone((p, 7), wd.at[i, x, c], dev_c)

            @pl.when(z == i)
            def _():
                for j in JS:
                    ag.gone((p, j - 1), half, zs_to[(i + j) % Z])
                ag.gone((p, 3), wd.at[i, x, c], dev_x)

            ag.arrived((p, 8), wd.at[i, nx, nc], dev_c)
            ag.gone((p, 8), wd.at[i, nx, c], dev_c)

        plain = (ag_z, ag_f, ag_d, ag_c, ag_e)
        by_plane = (down_z, down_f, down_d, down_c, down_e)

        rs = Copies(rs_send, rs_recv)
        held = []
        counts = [0, 0, 0]
        for r, (kind, _) in enumerate(PIECES):
            i = counts[kind]
            counts[kind] += 1
            slots_of = (g_slots, d_slots, q_slots)[kind]
            c1_of = (c1_g, c1_d, c1_q)[kind]
            held.append(
                (slots_of.at[i % slots_of.shape[0]], c1_of.at[i % c1_of.shape[0]])
                + tuple(bufs[sum(COUNTS[:r]) : sum(COUNTS[: r + 1])])
            )

        def rs_1(r):
            G, C1 = held[r][:2]
            rs.start((r, 0), G.at[:, :, :, :, nc], C1, dev_c)

        def rs_2(r):
            G, C1, XA, YB, S3, ZR, FIN = held[r]
            n = C1.shape[-1]
            rs.arrived((r, 0), C1, dev_c)
            for a in range(C1.shape[0]):
                for zh in range(ZH):
                    for zl in range(2):
                        C1[a, zh, zl] += G[a, zh, zl, :, c]
            rs.start((r, 1), C1.at[:, :, 0, nx], XA, dev_x)
            rs.start((r, 2), C1.at[:, :, 1, :, :, cols(n, ny)], YB, dev_y)
            rs.sent((r, 0))

        def rs_3(r):
            G, C1, XA, YB, S3, ZR, FIN = held[r]
            n = C1.shape[-1]
            rs.arrived((r, 1), XA, dev_x)
            XA[...] += C1[:, :, 0, x]
            rs.start((r, 3), XA.at[:, :, :, cols(n, ny)], S3.at[:, :, 0], dev_y)
            rs.arrived((r, 2), YB, dev_y)
            YB[...] += C1[:, :, 1, :, :, cols(n, y)]
            rs.start((r, 4), YB.at[:, :, nx], S3.at[:, :, 1], dev_x)
            rs.sent((r, 1), (r, 2))

        def rs_4(r):
            G, C1, XA, YB, S3, ZR, FIN = held[r]
            n = C1.shape[-1]
            rs.arrived((r, 3), S3.at[:, :, 0], dev_y)
            S3[:, :, 0] += XA[:, :, :, cols(n, y)]
            rs.arrived((r, 4), S3.at[:, :, 1], dev_x)
            S3[:, :, 1] += YB[:, :, x]
            for j in JS:
                zt = lax.rem(z + j, Z)
                rs.start((r, 4 + j), S3.at[:, zt // 2, zt % 2], ZR.at[j - 1], dev_z(zt))
            rs.sent((r, 3), (r, 4))

        def rs_5(r):
            G, C1, XA, YB, S3, ZR, FIN = held[r]
            n = C1.shape[-1]
            total = S3[:, z // 2, z % 2].astype(f32)
            for j in JS:
                rs.arrived((r, 4 + j), ZR.at[j - 1], dev_z(lax.rem(z - j + Z, Z)))
                total = total + ZR[j - 1].astype(f32)
            FIN[:, c, :, cols(n, y)] = total.astype(bf16)
            part = FIN.at[:, c, :, cols(n, y)]
            rs.start((r, 8), part, part, dev_y)
            rs.sent((r, 5), (r, 6), (r, 7))

        def zs_2(r):
            G, C1, ZR, XR, YR, FIN = held[r]
            rs.arrived((r, 0), C1, dev_c)
            for a in range(C1.shape[0]):
                for zh in range(ZH):
                    for zl in range(2):
                        C1[a, zh, zl] += G[a, zh, zl, :, c]
            for j in JS:
                zt = lax.rem(z + j, Z)
                rs.start((r, 4 + j), C1.at[:, zt // 2, zt % 2], ZR.at[j - 1], dev_z(zt))
            rs.sent((r, 0))

        def zs_3(r):
            G, C1, ZR, XR, YR, FIN = held[r]
            total = C1[:, z // 2, z % 2].astype(f32)
            for j in JS:
                rs.arrived((r, 4 + j), ZR.at[j - 1], dev_z(lax.rem(z - j + Z, Z)))
                total = total + ZR[j - 1].astype(f32)
            C1[:, z // 2, z % 2] = total.astype(bf16)
            rs.start((r, 1), C1.at[:, z // 2, z % 2, nx], XR, dev_x)
            rs.sent((r, 5), (r, 6), (r, 7))

        def zs_4(r):
            G, C1, ZR, XR, YR, FIN = held[r]
            rs.arrived((r, 1), XR, dev_x)
            XR[...] += C1[:, z // 2, z % 2, x]
            rs.start((r, 3), XR.at[:, :, cols(XR.shape[-1], ny)], YR, dev_y)
            rs.sent((r, 1))

        def zs_5(r):
            G, C1, ZR, XR, YR, FIN = held[r]
            n = XR.shape[-1]
            rs.arrived((r, 3), YR, dev_y)
            FIN[:, c, :, cols(n, y)] = XR[:, :, cols(n, y)] + YR[...]
            part = FIN.at[:, c, :, cols(n, y)]
            rs.start((r, 8), part, part, dev_y)
            rs.sent((r, 3))

        def rs_6(r):
            FIN = held[r][-1]
            n = FIN.shape[-1]
            rs.arrived((r, 8), FIN.at[:, c, :, cols(n, ny)], dev_y)
            rs.start((r, 9), FIN.at[:, c], FIN.at[:, c], dev_c)
            rs.sent((r, 8))

        outs = []

        def put(src, dst):
            copy = pltpu.make_async_copy(src, dst, out_sem.at[len(outs)])
            copy.start()
            outs.append(copy)

        def rs_7(r):
            FIN = held[r][-1]
            rs.arrived((r, 9), FIN.at[:, nc], dev_c)
            rs.sent((r, 9))
            put(FIN, out_pieces[r])

        gn = Copies(gn_send, gn_recv)
        axis_partners = [dev_x, dev_z(z ^ 1)] + ([dev_z(z ^ 2)] if Z == 4 else [])
        lane = lax.broadcasted_iota(jnp.int32, (per, width), 0)
        at = lax.broadcasted_iota(jnp.int32, (per, width), 1)
        place = jnp.where(lane == at % per, 1.0, 0.0).astype(bf16)
        spread = [mm(g[...], place) for g in (gain_first, gain_second)]
        spread = jnp.concatenate(spread + [jnp.zeros((6, width), f32)], axis=0)
        mine = lax.broadcasted_iota(jnp.int32, (8, width), 1) // per == f
        gsum[0] = jnp.where(mine, spread, 0.0)

        def gn_start(i):
            gn.start(i, gsum.at[i], grecv.at[i], axis_partners[i])

        def gn_finish(i):
            gn.arrived(i, grecv.at[i], axis_partners[i])
            gsum[i + 1] = gsum[i] + grecv[i]

        all_partners = [dev_c, dev_y] + axis_partners
        NA = len(axis_partners)

        def gg_start(i):
            gn.start(NA + i, gg.at[i], ggrecv.at[i], all_partners[i])

        def gg_finish(i):
            gn.arrived(NA + i, ggrecv.at[i], all_partners[i])
            gg[i + 1] = gg[i] + ggrecv[i]

        lane128 = lax.broadcasted_iota(jnp.int32, (slot, 128), 1) % HEAD_DIM
        prow = lax.broadcasted_iota(jnp.int32, (slot, 128), 0)

        def tables():
            rate = jnp.exp(
                (lane128 % HALF).astype(f32) * (-2.0 * math.log(10000.0) / HEAD_DIM)
            )
            for s in range(slots):
                e0 = lens[s, 0]
                e1 = e0 + lens[s, 1]
                e2 = e1 + lens[s, 2]
                e3 = e2 + lens[s, 3]

                def begins(p):
                    b = jnp.where(p >= e0, e0, 0)
                    b = jnp.where(p >= e1, e1, b)
                    b = jnp.where(p >= e2, e2, b)
                    return jnp.where(p >= e3, e3, b)

                angle = (prow - begins(prow)).astype(f32) * rate
                sine = jnp.sin(angle)
                rows = slice(s * slot, (s + 1) * slot)
                cos_t[rows, :] = jnp.cos(angle)
                sin_t[rows, :] = jnp.where(lane128 < HALF, -sine, sine)
                kpos = lax.broadcasted_iota(jnp.int32, (slot, slot), 0)
                qpos = lax.broadcasted_iota(jnp.int32, (slot, slot), 1)
                seen = (kpos >= begins(qpos)) & (kpos <= qpos)
                bias_t[s] = jnp.where(seen, 0.0, -1e30).astype(f32)
                live = jnp.where(prow < e2, 1.0, 0.0)[:, 0:1]
                db[rows, :] = (db[rows, :].astype(f32) * live).astype(bf16)

        def chunks(rows_each, body):
            def step(i, carry):
                body(pl.ds(pl.multiple_of(i * rows_each, rows_each), rows_each))
                return carry

            lax.fori_loop(0, T // rows_each, step, 0)

        def norm_first():
            def body(r):
                s = tok[r, :].astype(f32)
                sc = lax.rsqrt(jnp.mean(s * s, axis=1, keepdims=True) + epsilon)
                na[r, :] = (s * sc * gains[0:1, :]).astype(bf16)
                stats[r, :] = jnp.broadcast_to(sc, (sc.shape[0], 128))

            chunks(128, body)

        def flat(w, n0, n):
            val = w[:, :, :, :, pl.ds(n0, n)]
            return val.reshape(-1, n)

        def project(w, o, turned, factor=1.0):
            N = 256

            def step(i, carry):
                n0 = pl.multiple_of(i * N, N)
                a = mm(na[...], flat(w, n0, N))
                if turned:
                    for j in range(N // 128):
                        turned_part = rope(
                            a[:, j * 128 : (j + 1) * 128], cos_t[...], sin_t[...]
                        )
                        o[:, pl.ds(n0 + j * 128, 128)] = (turned_part * factor).astype(bf16)
                else:
                    o[:, pl.ds(n0, N)] = a.astype(bf16)
                return carry

            lax.fori_loop(0, width // N, step, 0)

        THIRD = slot // 3
        BLOCKS = [(i * THIRD, (i + 1) * THIRD, (i + 1) * THIRD) for i in range(3)]

        def attend_one(s, pair):
            rows = pl.ds(pl.multiple_of(s * slot, slot), slot)
            cs = pl.ds(pl.multiple_of(pair * 128, 128), 128)
            q2, k2, v2 = q[rows, cs], k[rows, cs], v[rows, cs]
            km, vm, om = split_heads(k2), split_heads(v2), split_heads(jnp.ones_like(v2))
            for begin, end, seen in BLOCKS:
                st = mm(stack2(km, 0, seen), q2[begin:end], 1, 1)
                expo = []
                for h in range(2):
                    sc = st[h * seen : (h + 1) * seen] + bias_t[s, :seen, begin:end]
                    top = jnp.max(sc, axis=0, keepdims=True)
                    e = jnp.exp(sc - top)
                    total = jnp.sum(e, axis=0, keepdims=True)
                    expo.append(e.astype(bf16))
                    lse[s, pair, h : h + 1, begin:end] = top + jnp.log(total)
                right = jnp.concatenate([stack2(vm, 0, seen), stack2(om, 0, seen)], axis=1)
                o = mm(jnp.concatenate(expo, axis=0), right, 0, 0)
                here = pl.ds(pl.multiple_of(s * slot, slot) + begin, end - begin)
                ho[here, cs] = (o[:, :128] / o[:, 128:]).astype(bf16)

        def attend(first, count):
            UNROLL = 3

            def step(i, carry):
                for u in range(UNROLL):
                    n = first + i * UNROLL + u
                    attend_one(n // PAIRS, n % PAIRS)
                return carry

            lax.fori_loop(0, count // UNROLL, step, 0)

        def middle():
            def body(r):
                s = tok[r, :].astype(f32) + mm(ho[r, :], wo[...].reshape(width, width))
                sc = lax.rsqrt(jnp.mean(s * s, axis=1, keepdims=True) + epsilon)
                smid[r, :] = s
                outacc[r, :] = s
                dnf[r, :] = jnp.zeros_like(s)
                nf[r, :] = (s * sc * gains[1:2, :]).astype(bf16)
                stats[r, :] = jnp.where(
                    lax.broadcasted_iota(jnp.int32, (sc.shape[0], 128), 1) == 0, stats[r, :], sc
                )

            chunks(slot, body)

        def ffn_hidden(i, s):
            wg_n, wu_n = (wgu[i][a].reshape(width, NB) for a in range(2))
            wd_n = wd[i].reshape(NB, width)

            r = slice(s * slot, (s + 1) * slot)
            g = mm(nf[r, :], wg_n)
            u = mm(nf[r, :], wu_n)
            dh = mm(db[r, :], wd_n, 1, 1)
            sg = 1.0 / (1.0 + jnp.exp(-g))
            si = g * sg
            hs[r, :] = (si * u).astype(bf16)
            dus[r, :] = (dh * si).astype(bf16)
            dgs[r, :] = (dh * u * (sg * (1.0 + g * (1.0 - sg)))).astype(bf16)

        def ffn_streams(i):
            outacc[...] += mm(hs[...], wd[i].reshape(NB, width))
            dnf[...] += mm(dgs[...], wgu[i][0].reshape(width, NB), 1, 1)
            dnf[...] += mm(dus[...], wgu[i][1].reshape(width, NB), 1, 1)

        def ffn_grads(i):
            G = held[i][0]
            G[0] = mm(nf[...], dgs[...], 0, 0).astype(bf16).reshape(G.shape[1:])
            G[1] = mm(nf[...], dus[...], 0, 0).astype(bf16).reshape(G.shape[1:])
            gd = mm(hs[...], db[...], 0, 0).astype(bf16).reshape(2, 2, 2, RD, width)
            for sub in range(2):
                held[Z + sub][0][0, i // 2, i % 2] = gd[:, :, sub]

        def middle_back():
            C = 128

            def step(i, acc):
                r = pl.ds(pl.multiple_of(i * C, C), C)
                dn, s, sc = dnf[r, :], smid[r, :], stats[r, 1:2]
                w = dn * gains[1:2, :]
                acc = acc + jnp.sum((dn * (s * sc)).reshape(C // 8, 8, width), axis=0)
                back = sc * w - s * (sc * sc * sc * jnp.mean(w * s, axis=1, keepdims=True))
                dm = db[r, :].astype(f32) + back
                dnf[r, :] = dm
                db[r, :] = dm.astype(bf16)
                return acc

            acc = lax.fori_loop(0, T // C, step, jnp.zeros((8, width), f32))
            gg[0, 1:2] = jnp.sum(acc, axis=0, keepdims=True)

        def grad_out_proj():
            G = held[Z + 2][0]
            val = mm(ho[...], db[...], 0, 0).astype(bf16)
            for a in range(QB):
                G[a] = val[:, a * QN : (a + 1) * QN].reshape(G.shape[1:])

        def heads_back():
            for zi in range(ZH):
                w = wo[2 * zi : 2 * zi + 2].reshape(8 * R, width)
                nf[:, zi * 8 * R : (zi + 1) * 8 * R] = mm(db[...], w, 1, 1).astype(bf16)

        def attend_back_one(s, pair):
            rows = pl.ds(pl.multiple_of(s * slot, slot), slot)
            cs = pl.ds(pl.multiple_of(pair * 128, 128), 128)
            q2, k2, v2, d2 = q[rows, cs], k[rows, cs], v[rows, cs], nf[rows, cs]
            km, vm, qm, dm = (split_heads(a) for a in (k2, v2, q2, d2))
            B = THIRD
            P, S = {}, {}
            for name, begin, end, seen in ((0, 0, B, B), (1, B, slot, slot)):
                st = mm(stack2(km, 0, seen), q2[begin:end], 1, 1)
                dp = mm(stack2(vm, 0, seen), d2[begin:end], 1, 1)
                for h in range(2):
                    part = slice(h * seen, (h + 1) * seen)
                    p = jnp.exp(
                        st[part]
                        + bias_t[s, :seen, begin:end]
                        - lse[s, pair, h : h + 1, begin:end]
                    )
                    P[name, h] = p.astype(bf16)
                    centre = jnp.sum(p * dp[part], axis=0, keepdims=True)
                    S[name, h] = (p * (dp[part] - centre)).astype(bf16)

            def key_side(w, m):
                first = jnp.concatenate([w[0, 0], w[0, 1], w[1, 0][:B], w[1, 1][:B]], axis=1)
                top = mm(first, jnp.concatenate([stack2(m, 0, B), stack2(m, B, slot)], axis=0))
                rest = jnp.concatenate([w[1, 0][B:], w[1, 1][B:]], axis=1)
                return jnp.concatenate([top, mm(rest, stack2(m, B, slot))], axis=0)

            co, si = cos_t[rows, :], -sin_t[rows, :]
            v[rows, cs] = key_side(P, dm).astype(bf16)
            k[rows, cs] = rope(key_side(S, qm), co, si).astype(bf16)
            dq = [
                mm(jnp.concatenate([S[n, 0], S[n, 1]], axis=0), stack2(km, 0, seen), 0, 0)
                for n, seen in ((0, B), (1, slot))
            ]
            q[rows, cs] = rope(jnp.concatenate(dq, axis=0) * FACTOR, co, si).astype(bf16)

        def attend_back(block, s):
            per_block = QN // 128

            def step(i, carry):
                attend_back_one(s, i + block * per_block)
                return carry

            lax.fori_loop(0, per_block, step, 0)

        def attend_grads(block):
            G = held[Z + 3 + block][0]
            at = slice(block * QN, (block + 1) * QN)
            grads = jnp.concatenate([q[:, at], k[:, at], v[:, at]], axis=1)
            val = mm(na[...], grads, 0, 0).astype(bf16)
            for a in range(3):
                G[a] = val[:, a * QN : (a + 1) * QN].reshape(G.shape[1:])

        def first_back(i):
            N = width // 2

            def rows_of(w):
                return w[i * ZH : (i + 1) * ZH].reshape(N, width)

            smid[:, i * N : (i + 1) * N] = (
                mm(q[...], rows_of(wq), 1, 1)
                + mm(k[...], rows_of(wk), 1, 1)
                + mm(v[...], rows_of(wv), 1, 1)
            )

        def first_norm_back():
            C = 128

            def step(i, acc):
                r = pl.ds(pl.multiple_of(i * C, C), C)
                dn, s, sc = smid[r, :], tok[r, :].astype(f32), stats[r, 0:1]
                w = dn * gains[0:1, :]
                acc = acc + jnp.sum((dn * (s * sc)).reshape(C // 8, 8, width), axis=0)
                back = sc * w - s * (sc * sc * sc * jnp.mean(w * s, axis=1, keepdims=True))
                tok[r, :] = (dnf[r, :] + back).astype(bf16)
                return acc

            acc = lax.fori_loop(0, T // C, step, jnp.zeros((8, width), f32))
            gg[0, 0:1] = jnp.sum(acc, axis=0, keepdims=True)

        def result():
            parts = ((hs, 0, NB), (dus, NB, width - NB))
            for held_in, begin, n in parts:
                held_in[:, :n] = outacc[:, begin : begin + n].astype(bf16)
            for s in range(slots):
                for held_in, begin, n in parts:
                    part = held_in.at[pl.ds(s * slot, slot), pl.ds(0, n)]
                    put(part, out_main.at[s, :, pl.ds(begin, n)])

        def first_norm():
            gains[...] = gsum[NA]
            norm_first()

        def gains_step(i):
            gn_finish(i)
            if i + 1 < NA:
                gn_start(i + 1)

        def gain_grads_step(i):
            gg_finish(i)
            if i + 1 < len(all_partners):
                gg_start(i + 1)

        def reduce_step(k, r):
            plain = (rs_1, rs_2, rs_3, rs_4, rs_5, rs_6, rs_7)
            along_z = (rs_1, zs_2, zs_3, zs_4, zs_5, rs_6, rs_7)
            (along_z if r in ALONG_Z_FIRST else plain)[k - 1](r)

        quarter = slots * PAIRS // 4
        comm = (
            *(from_plane(k) for k in range(5)), *(None,) * 5,
            None, *(functools.partial(reduce_step, k) for k in range(1, 8)), None, None,
            gn_start, gains_step, gg_start, gain_grads_step,
        )
        compute = (
            lambda _: tables(),
            lambda _: first_norm(),
            lambda i: project((wq, wk, wv)[i], (q, k, v)[i], i < 2, (FACTOR, 1.0, 1.0)[i]),
            lambda i: attend(i * quarter, quarter),
            lambda _: middle(),
            lambda i: ffn_hidden(i // 2, i % 2),
            ffn_streams,
            ffn_grads,
            lambda _: middle_back(),
            lambda _: grad_out_proj(),
            lambda _: heads_back(),
            lambda i: attend_back(i // 2, i % 2),
            attend_grads,
            first_back,
            lambda _: first_norm_back(),
            lambda _: result(),
        )
        TABLES, FIRST_NORM_BACK, RESULT = 30, 44, 45
        pl.semaphore_wait(barrier, len(partners))
        for code in ORDER:
            kind, n = divmod(code, 100)
            if kind == TABLES:
                have(TOKENS)
            if kind < 30:
                comm[kind](n)
            elif kind == RESULT:
                result()
            else:
                pl.when(f >= 0)(functools.partial(compute[kind - 30], n))
            if kind == FIRST_NORM_BACK:
                for s in range(slots):
                    put(tok.at[pl.ds(s * slot, slot)], out_tokens.at[s])
        gn.sent(*range(NA + len(all_partners)))
        put(gg.at[len(all_partners)], out_gains)
        for copy in outs:
            copy.wait()

    VM, HB = pltpu.VMEM, pl.BlockSpec(memory_space=pl.ANY)
    S = jax.ShapeDtypeStruct

    def full(rows_half, n):
        return VM((Z, 2, 2, rows_half, n), bf16)

    def piece_bufs(i, kind):
        a, r, n = (G_SHAPE, D_SHAPE, Q_SHAPE)[kind]
        if i in ALONG_Z_FIRST:
            return [
                VM((Z - 1, a, 2, r, n), bf16),
                VM((a, r, n), bf16),
                VM((a, r, n // 2), bf16),
                VM((a, 2, r, n), bf16),
            ]
        return [
            VM((a, ZH, r, n), bf16),
            VM((a, ZH, 2, r, n // 2), bf16),
            VM((a, ZH, 2, r, n // 2), bf16),
            VM((Z - 1, a, r, n // 2), bf16),
            VM((a, 2, r, n), bf16),
        ]

    def grads_of(count, shape):
        a, r, n = shape
        return VM((count, a, ZH, 2, 2, 2, r, n), bf16)

    def first_of(count, shape):
        a, r, n = shape
        return VM((count, a, ZH, 2, 2, r, n), bf16)

    axes = 3 if Z == 4 else 2
    NL = 8 + 2 + 4 * Z + 2 * slots
    scratch = [full(R, width)] * 4 + [VM((Z, 2, 2, 2 * RD, width), bf16)]
    scratch += [VM((2, Z, 2, 2, R, NB), bf16)] * Z
    scratch += [VM((T, width), bf16)] * 6
    scratch += [VM((T, width), f32), VM((T, width), bf16), VM((T, width), bf16)]
    scratch += [VM((T, width), f32)] * 2
    scratch += [VM((T, 128), f32)] * 3
    scratch += [VM((slots, slot, slot), f32), VM((slots, PAIRS, 8, slot), f32)]
    scratch += [VM((T, NB), bf16)] * 3
    scratch += [VM((axes + 1, 8, width), f32), VM((axes, 8, width), f32), VM((8, width), f32)]
    scratch += [VM((axes + 3, 8, width), f32), VM((axes + 2, 8, width), f32)]
    scratch += [grads_of(2, G_SHAPE), grads_of(2, D_SHAPE), grads_of(2, Q_SHAPE)]
    for i, (kind, _) in enumerate(PIECES):
        scratch += piece_bufs(i, kind)
    scratch += [first_of(4, G_SHAPE), first_of(2, D_SHAPE), first_of(1 + QB, Q_SHAPE)]
    DMA = pltpu.SemaphoreType.DMA
    scratch += [DMA((NL,)), DMA((NAG, 17)), DMA((NAG, 17)), DMA((NRS, 10)), DMA((NRS, 10))]
    scratch += [DMA((2 * axes + 2,)), DMA((2 * axes + 2,)), DMA((NRS + 1 + 3 * slots,))]
    out_shape = [S((slots, slot, width), bf16)] * 2 + [S((8, width), f32)]
    for _, (a, r, n) in PIECES:
        out_shape.append(S((a, 2, r, n), bf16))
    call = pl.pallas_call(
        kernel,
        out_shape=out_shape,
        in_specs=[pl.BlockSpec(memory_space=pltpu.SMEM)] + [pl.BlockSpec(memory_space=VM)] * 2 + [HB] * 9,
        out_specs=[HB] * len(out_shape),
        scratch_shapes=scratch,
        compiler_params=pltpu.CompilerParams(
            collective_id=0, has_side_effects=True, vmem_limit_bytes=VMEM_BYTES
        ),
    )

    FINAL = [S((slots, slot, width), bf16)] * 2 + [S((per, width), f32)] * 4
    FINAL += [S((per, ff), f32)] * 2 + [S((ff // fs, width), f32)] + [S((1, per), f32)] * 2
    NF = len(FINAL)

    def finish(*refs):
        made, outs = refs[: 3 + NRS], refs[3 + NRS : 3 + NRS + NF]
        held = refs[3 + NRS + NF : 2 * (3 + NRS) + NF]
        done = refs[2 * (3 + NRS) + NF : -2]
        in_sem, sem = refs[-2:]
        fetched = [
            pltpu.make_async_copy(src, dst, in_sem.at[i])
            for i, (src, dst) in enumerate(zip(made, held))
        ]
        for copy in fetched:
            copy.start()
        stored = []

        def store(i, src):
            copy = pltpu.make_async_copy(src, outs[i], sem.at[i])
            copy.start()
            stored.append(copy)

        for i in range(2):
            fetched[i].wait()
            store(i, held[i])
        pieces = held[3:]
        dq, dk, dv, do, dg, du, dd, first, second = done
        for i in range(Z):
            fetched[3 + i].wait()
            for a, out in enumerate((dg, du)):
                out[:, i * NB : (i + 1) * NB] = pieces[i][a].astype(f32).reshape(per, NB)
        store(6, dg)
        store(7, du)
        for sub in range(2):
            fetched[3 + Z + sub].wait()
            for c in range(2):
                rows = slice((2 * c + sub) * RD, (2 * c + sub + 1) * RD)
                dd[rows, :] = pieces[Z + sub][0, c].astype(f32)
        store(8, dd)
        fetched[5 + Z].wait()
        for a in range(QB):
            do[:, a * QN : (a + 1) * QN] = pieces[Z + 2][a].astype(f32).reshape(per, QN)
        store(5, do)
        for b in range(QB):
            fetched[6 + Z + b].wait()
            for a, out in enumerate((dq, dk, dv)):
                out[:, b * QN : (b + 1) * QN] = pieces[Z + 3 + b][a].astype(f32).reshape(per, QN)
        for i, out in enumerate((dq, dk, dv)):
            store(2 + i, out)
        fetched[2].wait()
        f = lax.axis_index("fsdp")
        lane = lax.broadcasted_iota(jnp.int32, (width, 128), 1)
        at = lax.broadcasted_iota(jnp.int32, (width, 128), 0)
        pick = jnp.where((at == lane + f * per) & (lane < per), 1.0, 0.0).astype(bf16)
        g = held[2][...]
        total = jnp.zeros((8, 128), f32)
        for _ in range(3):
            term = g.astype(bf16)
            total = total + mm(term, pick)
            g = g - term.astype(f32)
        first[...] = total[0:1, :per]
        second[...] = total[1:2, :per]
        store(9, first)
        store(10, second)
        for copy in stored:
            copy.wait()

    post = pl.pallas_call(
        finish,
        out_shape=FINAL,
        in_specs=[HB] * (3 + NRS),
        out_specs=[HB] * NF,
        scratch_shapes=[VM(o.shape, o.dtype) for o in out_shape + FINAL[2:]]
        + [DMA((3 + NRS,)), DMA((NF,))],
        compiler_params=pltpu.CompilerParams(vmem_limit_bytes=VMEM_BYTES),
    )

    def local(tokens, lengths, wq, wk, wv, wo, wg, wu, wd, gain_attn, gain_ffn, gradient):
        rows = (gain_attn.reshape(1, per), gain_ffn.reshape(1, per))
        made = call(lengths, *rows, tokens, gradient, wq, wk, wv, wo, wg, wu, wd)
        *grads, first, second = post(*made)
        return (*grads, first.reshape(per), second.reshape(per))

    return local


def layout(lengths, slot):
    pieces = lengths.shape[0]
    bounds = jnp.stack([jnp.sum(lengths[: j + 1]) for j in range(pieces)])
    places = lax.iota(jnp.int32, slot)
    piece_of = jnp.sum((places[:, None] >= bounds[None, :]).astype(jnp.int32), axis=1)
    piece_begins = bounds - lengths
    member = piece_of[:, None] == lax.iota(jnp.int32, pieces)[None, :]
    begins = jnp.sum(jnp.where(member, piece_begins[None, :], 0), axis=1)
    offsets = places - begins
    live = (piece_of < pieces - 1).astype(jnp.float32)
    visible = (piece_of[:, None] == piece_of[None, :]) & (places[None, :] <= places[:, None])
    return (offsets, live, visible)


def rotary(offsets, head_dim):
    half = head_dim // 2
    rates = jnp.power(10000.0, -2.0 * lax.iota(jnp.float32, half) / head_dim)
    angle = offsets.astype(jnp.float32)[:, None] * rates[None, :]
    angle = jnp.concatenate([angle, angle], axis=1)
    return (jnp.cos(angle), jnp.sin(angle))


def turn(values, cosine, sine, sign):
    half = values.shape[-1] // 2
    swapped = jnp.concatenate([-values[..., half:], values[..., :half]], axis=-1)
    return values * cosine[:, None, :] + sign * swapped * sine[:, None, :]


def matmul(left, right):
    return jnp.dot(left, right, preferred_element_type=jnp.float32)


def left_inner(left, right):
    return lax.dot_general(
        left, right, (((0,), (0,)), ((), ())), preferred_element_type=jnp.float32
    )


def right_inner(left, right):
    return lax.dot_general(
        left, right, (((1,), (1,)), ((), ())), preferred_element_type=jnp.float32
    )


def norm_back(grad_normed, gain, stream, scale):
    weighted = grad_normed * gain.astype(jnp.float32)
    gain_grad = jnp.sum(grad_normed * stream * scale, axis=0)
    stream_grad = scale * weighted - stream * scale * scale * scale * jnp.mean(
        weighted * stream, axis=1, keepdims=True
    )
    return (stream_grad, gain_grad)


def forward_pass(tokens_slot, weights, cosine, sine, visible):
    w_query, w_key, w_value, w_out, w_gate, w_up, w_down, gain_attn, gain_ffn = weights
    slot = tokens_slot.shape[0]
    factor = HEAD_DIM ** (-0.5)
    stream = tokens_slot.astype(jnp.float32)
    scale_attn = lax.rsqrt(jnp.mean(stream * stream, axis=1, keepdims=True) + epsilon)
    normed_attn = (stream * scale_attn * gain_attn.astype(jnp.float32)).astype(jnp.bfloat16)
    query_rows = turn(
        matmul(normed_attn, w_query).reshape(slot, HEADS, HEAD_DIM), cosine, sine, 1.0
    ).astype(jnp.bfloat16)
    key_rows = turn(
        matmul(normed_attn, w_key).reshape(slot, HEADS, HEAD_DIM), cosine, sine, 1.0
    ).astype(jnp.bfloat16)
    value_rows = matmul(normed_attn, w_value).astype(jnp.bfloat16).reshape(slot, HEADS, HEAD_DIM)
    scores = (
        jnp.einsum("qhd,khd->hqk", query_rows, key_rows, preferred_element_type=jnp.float32)
        * factor
    )
    scores = jnp.where(visible[None], scores, -1e30)
    top = jnp.max(scores, axis=-1, keepdims=True)
    weights_exp = jnp.exp(scores - top)
    totals = jnp.sum(weights_exp, axis=-1, keepdims=True)
    probs = weights_exp / totals
    log_total = top + jnp.log(totals)
    mixed = jnp.einsum(
        "hqk,khd->qhd", probs.astype(jnp.bfloat16), value_rows, preferred_element_type=jnp.float32
    )
    heads_out = mixed.reshape(slot, HEADS * HEAD_DIM).astype(jnp.bfloat16)
    stream_mid = stream + matmul(heads_out, w_out)
    scale_ffn = lax.rsqrt(jnp.mean(stream_mid * stream_mid, axis=1, keepdims=True) + epsilon)
    normed_ffn = (stream_mid * scale_ffn * gain_ffn.astype(jnp.float32)).astype(jnp.bfloat16)
    gate_pre = matmul(normed_ffn, w_gate)
    up_branch = matmul(normed_ffn, w_up)
    hidden = (gate_pre * jax.nn.sigmoid(gate_pre) * up_branch).astype(jnp.bfloat16)
    result = stream_mid + matmul(hidden, w_down)
    kept = (
        stream,
        scale_attn,
        normed_attn,
        query_rows,
        key_rows,
        value_rows,
        log_total,
        heads_out,
        stream_mid,
        scale_ffn,
        normed_ffn,
        gate_pre,
        up_branch,
        hidden,
    )
    return (kept, result)


def backward_pass(kept, weights, cotangent, live, cosine, sine, visible):
    w_query, w_key, w_value, w_out, w_gate, w_up, w_down, gain_attn, gain_ffn = weights
    (
        stream,
        scale_attn,
        normed_attn,
        query_rows,
        key_rows,
        value_rows,
        log_total,
        heads_out,
        stream_mid,
        scale_ffn,
        normed_ffn,
        gate_pre,
        up_branch,
        hidden,
    ) = kept
    slot = stream.shape[0]
    factor = HEAD_DIM ** (-0.5)
    d_out = cotangent.astype(jnp.float32) * live[:, None]
    d_branch = d_out.astype(jnp.bfloat16)
    grad_down = left_inner(hidden, d_branch)
    d_hidden = right_inner(d_branch, w_down)
    sigma = jax.nn.sigmoid(gate_pre)
    d_gate = (d_hidden * up_branch * sigma * (1.0 + gate_pre * (1.0 - sigma))).astype(jnp.bfloat16)
    d_up = (d_hidden * gate_pre * sigma).astype(jnp.bfloat16)
    grad_gate = left_inner(normed_ffn, d_gate)
    grad_up = left_inner(normed_ffn, d_up)
    d_normed_ffn = right_inner(d_gate, w_gate) + right_inner(d_up, w_up)
    mid_back, grad_gain_ffn = norm_back(d_normed_ffn, gain_ffn, stream_mid, scale_ffn)
    d_mid = d_out + mid_back
    d_attn = d_mid.astype(jnp.bfloat16)
    grad_out_proj = left_inner(heads_out, d_attn)
    d_heads = right_inner(d_attn, w_out).astype(jnp.bfloat16).reshape(slot, HEADS, HEAD_DIM)
    scores = (
        jnp.einsum("qhd,khd->hqk", query_rows, key_rows, preferred_element_type=jnp.float32)
        * factor
    )
    probs = jnp.where(visible[None], jnp.exp(scores - log_total), 0.0)
    d_probs = jnp.einsum("qhd,khd->hqk", d_heads, value_rows, preferred_element_type=jnp.float32)
    d_values = jnp.einsum(
        "hqk,qhd->khd", probs.astype(jnp.bfloat16), d_heads, preferred_element_type=jnp.float32
    )
    d_values = d_values.astype(jnp.bfloat16).reshape(slot, HEADS * HEAD_DIM)
    centre = jnp.sum(probs * d_probs, axis=-1, keepdims=True)
    d_scores = (probs * (d_probs - centre)).astype(jnp.bfloat16)
    d_query_rot = (
        jnp.einsum("hqk,khd->qhd", d_scores, key_rows, preferred_element_type=jnp.float32) * factor
    )
    d_key_rot = (
        jnp.einsum("hqk,qhd->khd", d_scores, query_rows, preferred_element_type=jnp.float32)
        * factor
    )
    d_queries = (
        turn(d_query_rot, cosine, sine, -1.0).astype(jnp.bfloat16).reshape(slot, HEADS * HEAD_DIM)
    )
    d_keys = (
        turn(d_key_rot, cosine, sine, -1.0).astype(jnp.bfloat16).reshape(slot, HEADS * HEAD_DIM)
    )
    grad_query = left_inner(normed_attn, d_queries)
    grad_key = left_inner(normed_attn, d_keys)
    grad_value = left_inner(normed_attn, d_values)
    d_normed_attn = (
        right_inner(d_queries, w_query)
        + right_inner(d_keys, w_key)
        + right_inner(d_values, w_value)
    )
    stream_back, grad_gain_attn = norm_back(d_normed_attn, gain_attn, stream, scale_attn)
    grad_input = d_mid + stream_back
    grads = (
        grad_query,
        grad_key,
        grad_value,
        grad_out_proj,
        grad_gate,
        grad_up,
        grad_down,
        grad_gain_attn,
        grad_gain_ffn,
    )
    return (grads, grad_input)


def local_general(
    tokens, lengths, w_query, w_key, w_value, w_out, w_gate, w_up, w_down, gain_attn, gain_ffn,
    output_gradient,
):
    rows = (w_query, w_key, w_value, w_out, w_gate, w_up, w_down, gain_attn, gain_ffn)
    weights = tuple(lax.all_gather(w, "fsdp", axis=0, tiled=True) for w in rows)
    results, input_grads, totals = [], [], None
    for i in range(tokens.shape[0]):
        offsets, live, visible = layout(lengths[i], tokens.shape[1])
        cosine, sine = rotary(offsets, HEAD_DIM)
        kept, result = forward_pass(tokens[i], weights, cosine, sine, visible)
        grads, grad_input = backward_pass(
            kept, weights, output_gradient[i], live, cosine, sine, visible
        )
        results.append(result.astype(jnp.bfloat16))
        input_grads.append(grad_input.astype(jnp.bfloat16))
        totals = grads if totals is None else tuple(a + b for a, b in zip(totals, grads))
    shares = (lax.psum_scatter(g, "fsdp", scatter_dimension=0, tiled=True) for g in totals)
    summed = tuple(lax.psum(g, "dp") for g in shares)
    return (jnp.stack(results), jnp.stack(input_grads)) + summed


def solution(mesh):
    row, vec = P("fsdp", None), P("fsdp")
    wide = P(("dp", "fsdp"), None, None)
    in_specs = (wide, P(("dp", "fsdp"), None)) + (row,) * 7 + (vec, vec, wide)
    out_specs = (wide, wide) + (row,) * 7 + (vec, vec)

    def local(tokens, lengths, *rest):
        slots, slot, width = tokens.shape
        ff = rest[4].shape[1]
        if (mesh.shape["dp"], mesh.shape["fsdp"]) == (4, 8) and (width, ff) == (768, 2048):
            return build(mesh, slots, slot, width, ff)(tokens, lengths, *rest)
        return local_general(tokens, lengths, *rest)

    return jax.shard_map(local, mesh=mesh, in_specs=in_specs, out_specs=out_specs, check_vma=False)
```

```python
import functools
import math
import jax
import jax.numpy as jnp
from jax import lax
from jax.experimental import pallas as pl
from jax.experimental.pallas import tpu as pltpu
from jax.sharding import PartitionSpec as P

HEADS = 12
HEAD_DIM = 64
HALF = HEAD_DIM // 2
FACTOR = HEAD_DIM ** (-0.5)
epsilon = 1e-05
f32 = jnp.float32
bf16 = jnp.bfloat16
MESH = pl.DeviceIdType.MESH
VMEM_BYTES = 66_900_000
ALONG_Z_FIRST = (1, 5)
OVER_X = (1, 2, 3, 6, 9, 10, 11)

ORDER = (
    0, 2000, 1, 2, 3000, 2100, 100, 101, 3, 200, 102, 4, 2101, 201, 300, 103, 5, 400, 202, 301,
    104, 6, 2102, 3100, 401, 203, 3200, 302, 105, 7, 3201, 204, 402, 3202, 303, 106, 107, 8, 9,
    3300, 205, 403, 3301, 304, 3302, 3303, 3400, 206, 108, 10, 404, 207, 109, 11, 305, 405,
    3500, 306, 3501, 110, 3700, 1100, 307, 208, 111, 406, 3600, 209, 1200, 407, 3502, 3503,
    3701, 1101, 210, 308, 3601, 211, 309, 1201, 408, 409, 3504, 3505, 1300, 3702, 1102, 310,
    311, 3602, 1400, 1202, 410, 411, 3506, 3507, 3703, 1103, 1104, 1105, 3603, 1302, 3800, 1204,
    1301, 1203, 3900, 1106, 1205, 1402, 4000, 4100, 1206, 1500, 4101, 1304, 4200, 1107, 1401,
    4102, 4103, 1207, 1303, 4201, 1108, 4104, 1600, 1306, 4105, 1208, 1700, 1404, 1501, 4202,
    1109, 4300, 1307, 1305, 4301, 1403, 1209, 4400, 2200, 1406, 1502, 4500, 2300, 1308, 1504,
    1601, 1407, 1701, 1405, 1503, 1309, 1602, 2301, 1506, 1702, 1408, 1604, 2302, 1505, 1507,
    1704, 1603, 1409, 1703, 1606, 1508, 2303, 1605, 1706, 1607, 1608, 1705, 1707, 1509, 1708,
    2304, 1609, 1709,
)


def mm(a, b, ca=1, cb=0):
    return lax.dot_general(a, b, (((ca,), (cb,)), ((), ())), preferred_element_type=f32)


def rope(v, cosine, sine):
    lane = lax.broadcasted_iota(jnp.int32, v.shape, 1) % HEAD_DIM
    swapped = jnp.where(lane < HALF, pltpu.roll(v, 128 - HALF, 1), pltpu.roll(v, HALF, 1))
    return v * cosine + swapped * sine


def split_heads(x):
    lane = lax.broadcasted_iota(jnp.int32, x.shape, 1)
    zero = jnp.zeros_like(x)
    return jnp.where(lane < HEAD_DIM, x, zero), jnp.where(lane < HEAD_DIM, zero, x)


def stack2(pair, begin, end):
    return jnp.concatenate([pair[0][begin:end], pair[1][begin:end]], axis=0)


class Copies:
    def __init__(self, send, recv):
        self.send, self.recv, self.started = send, recv, {}

    def start(self, key, src, dst, device, there=None):
        copy = pltpu.make_async_remote_copy(
            src_ref=src,
            dst_ref=dst,
            send_sem=self.send.at[key],
            recv_sem=self.recv.at[there or key],
            device_id=device,
            device_id_type=MESH,
        )
        copy.start()
        self.started[key] = copy

    def arrived(self, key, dst, device):
        pltpu.make_async_remote_copy(
            src_ref=dst,
            dst_ref=dst,
            send_sem=self.send.at[key],
            recv_sem=self.recv.at[key],
            device_id=device,
            device_id_type=MESH,
        ).wait_recv()

    def gone(self, key, src, device):
        pltpu.make_async_remote_copy(
            src_ref=src,
            dst_ref=src,
            send_sem=self.send.at[key],
            recv_sem=self.recv.at[key],
            device_id=device,
            device_id_type=MESH,
        ).wait_send()

    def sent(self, *keys):
        for key in keys:
            self.started.pop(key).wait_send()


def build(mesh, slots, slot, width, ff):
    dps, fs = mesh.shape["dp"], mesh.shape["fsdp"]
    Z, ZH = fs // 2, fs // 4
    T = slots * slot
    R, RD = width // fs // 2, ff // fs // 4
    per = width // fs
    NB = ff // Z
    QN = 256
    QB = width // QN
    PAIRS = width // 128
    NAG = 4 + 2 * Z
    G_SHAPE, D_SHAPE, Q_SHAPE = (2, R, NB), (1, RD, width), (3, R, QN)
    PIECES = (
        [(0, G_SHAPE)] * Z
        + [(1, D_SHAPE)] * 2
        + [(2, Q_SHAPE)] * (1 + QB)
    )
    NRS = len(PIECES)
    COUNTS = [4 if r in ALONG_Z_FIRST else 5 for r in range(NRS)]

    def kernel(
        lens, gain_first, gain_second, tokens, gradient, w_query, w_key, w_value, w_out, w_gate, w_up, w_down,
        out_main, out_tokens, out_gains, *rest,
    ):
        out_pieces, rest = rest[:NRS], rest[NRS:]
        wq, wk, wv, wo, wd = rest[:5]
        wgu, rest = rest[5 : 5 + Z], rest[5 + Z :]
        (
            tok, na, q, k, v, ho, smid, nf, db, dnf, outacc,
            cos_t, sin_t, stats, bias_t, lse, hs, dgs, dus,
            gsum, grecv, gains, gg, ggrecv,
            g_slots, d_slots, q_slots,
        ) = rest[:27]
        rest = rest[27:]
        bufs, rest = rest[: sum(COUNTS)], rest[sum(COUNTS) :]
        c1_g, c1_d, c1_q = rest[:3]
        (local_sem, ag_send, ag_recv, rs_send, rs_recv, gn_send, gn_recv, out_sem) = rest[3:]

        d, f = lax.axis_index("dp"), lax.axis_index("fsdp")
        y, c = d // 2, d % 2
        z, x = f // 2, f % 2
        nx, ny, nc = 1 - x, 1 - y, 1 - c
        dev_x, dev_y, dev_c = (d, z * 2 + nx), (ny * 2 + c, f), (y * 2 + nc, f)

        def dev_z(zt):
            return (d, zt * 2 + x)

        JS = [1, Z - 1] + list(range(2, Z - 1))

        partners = [dev_c, dev_x, dev_y] + [dev_z(lax.rem(z + j, Z)) for j in range(1, Z)]
        barrier = pltpu.get_barrier_semaphore()
        for p in partners:
            pl.semaphore_signal(barrier, inc=1, device_id=p, device_id_type=MESH)
        fetched = []
        TOKENS, DOWN = -1, -2

        def fetch(group, src, dst):
            copy = pltpu.make_async_copy(src, dst, local_sem.at[len(fetched)])
            copy.start()
            fetched.append((group, copy))

        def have(group):
            for g, copy in fetched:
                if g == group:
                    copy.wait()

        for i, (src, w) in enumerate(((w_query, wq), (w_key, wk), (w_value, wv), (w_out, wo))):
            for h in range(2):
                fetch(i, src.at[pl.ds(h * R, R)], w.at[z, x, h])

        def fetch_rest():
            for s in range(slots):
                fetch(TOKENS, tokens.at[s], tok.at[pl.ds(s * slot, slot)])
                fetch(TOKENS, gradient.at[s], db.at[pl.ds(s * slot, slot)])
            for h in range(2):
                fetch(DOWN, w_down.at[pl.ds(2 * h * RD, 2 * RD)], wd.at[z, x, h])
            for i in range(Z):
                for a, src in enumerate((w_gate, w_up)):
                    for h in range(2):
                        part = src.at[pl.ds(h * R, R), pl.ds(i * NB, NB)]
                        fetch(4 + 2 * i, part, wgu[i].at[a, z, x, h])

        ag = Copies(ag_send, ag_recv)

        def view(p, zi, xi, ci, at=slice(None)):
            if p < 4:
                return (wq, wk, wv, wo)[p].at[zi, xi, ci, :, at]
            return wgu[p // 2 - 2].at[:, zi, xi, ci, :, at]

        def cols(n, which):
            return pl.ds(pl.multiple_of(which * (n // 2), n // 2), n // 2)

        def side_of(p):
            return [3] if p in OVER_X else []

        def width_of(p):
            return width if p < 4 else NB

        def ag_z(p):
            have(p)
            n = width_of(p)
            for j in JS:
                r = view(p, z, x, c, cols(n, y))
                ag.start((p, j - 1), r, r, dev_z(lax.rem(z + j, Z)))
            r = view(p, z, x, c)
            ag.start((p, 3), r, r, dev_x)

        def ag_f(p):
            n = width_of(p)
            for j in JS:
                zs = lax.rem(z - j + Z, Z)
                r = view(p, zs, x, c, cols(n, y))
                ag.arrived((p, j - 1), r, dev_z(zs))
                ag.start((p, 3 + j), r, r, dev_x)
                ag.start((p, 6 + j), r, r, dev_y)

        def ag_d(p):
            n = width_of(p)
            for j in JS:
                zs = lax.rem(z - j + Z, Z)
                r = view(p, zs, nx, c, cols(n, y))
                ag.arrived((p, 3 + j), r, dev_x)
                if j not in side_of(p):
                    ag.start((p, 9 + j), r, r, dev_y)
                r = view(p, zs, x, c, cols(n, ny))
                ag.arrived((p, 6 + j), r, dev_y)
                if j in side_of(p):
                    ag.start((p, 9 + j), r, r, dev_x)
                r = view(p, zs, x, c)
                ag.start((p, 12 + j), r, r, dev_c)
            ag.arrived((p, 3), view(p, z, nx, c), dev_x)

        def ag_c(p):
            n = width_of(p)
            for j in JS:
                zs = lax.rem(z - j + Z, Z)
                r = view(p, zs, nx, c, cols(n, ny))
                ag.arrived((p, 9 + j), r, dev_x if j in side_of(p) else dev_y)
            r = view(p, slice(None), nx, c)
            ag.start((p, 16), r, r, dev_c)

        def ag_e(p):
            for j in JS:
                ag.arrived((p, 12 + j), view(p, lax.rem(z - j + Z, Z), x, nc), dev_c)
            ag.arrived((p, 16), view(p, slice(None), nx, nc), dev_c)
            ag.sent(*((p, i) for i in range(17)))

        def from_plane(step):
            def run(p):
                if p < 4 or p % 2 == 0:
                    plain[step](p)
                else:
                    by_plane[step](p, p // 2 - 2)

            return run

        zs_to = [dev_z(i) for i in range(Z)]

        def down_z(p, i):
            if i == 0:
                have(DOWN)

            @pl.when(z == i)
            def _():
                r = wd.at[i, x, c, :, cols(width, y)]
                for j in JS:
                    ag.start((p, j - 1), r, r, zs_to[(i + j) % Z], (p, 0))
                r = wd.at[i, x, c]
                ag.start((p, 3), r, r, dev_x)

        def down_f(p, i):
            @pl.when(z != i)
            def _():
                r = wd.at[i, x, c, :, cols(width, y)]
                ag.arrived((p, 0), r, zs_to[i])
                ag.start((p, 4), r, r, dev_x)
                ag.start((p, 5), r, r, dev_y)

        def down_d(p, i):
            @pl.when(z != i)
            def _():
                r = wd.at[i, nx, c, :, cols(width, y)]
                ag.arrived((p, 4), r, dev_x)
                if p not in OVER_X:
                    ag.start((p, 6), r, r, dev_y)
                r = wd.at[i, x, c, :, cols(width, ny)]
                ag.arrived((p, 5), r, dev_y)
                if p in OVER_X:
                    ag.start((p, 6), r, r, dev_x)
                r = wd.at[i, x, c]
                ag.start((p, 7), r, r, dev_c)

            @pl.when(z == i)
            def _():
                ag.arrived((p, 3), wd.at[i, nx, c], dev_x)

        def down_c(p, i):
            @pl.when(z != i)
            def _():
                ag.arrived((p, 6), wd.at[i, nx, c, :, cols(width, ny)], (dev_y, dev_x)[p in OVER_X])

            r = wd.at[i, nx, c]
            ag.start((p, 8), r, r, dev_c)

        def down_e(p, i):
            half = wd.at[i, x, c, :, cols(width, y)]

            @pl.when(z != i)
            def _():
                ag.arrived((p, 7), wd.at[i, x, nc], dev_c)
                ag.gone((p, 4), half, dev_x)
                ag.gone((p, 5), half, dev_y)
                ag.gone((p, 6), half, (dev_y, dev_x)[p in OVER_X])
                ag.gone((p, 7), wd.at[i, x, c], dev_c)

            @pl.when(z == i)
            def _():
                for j in JS:
                    ag.gone((p, j - 1), half, zs_to[(i + j) % Z])
                ag.gone((p, 3), wd.at[i, x, c], dev_x)

            ag.arrived((p, 8), wd.at[i, nx, nc], dev_c)
            ag.gone((p, 8), wd.at[i, nx, c], dev_c)

        plain = (ag_z, ag_f, ag_d, ag_c, ag_e)
        by_plane = (down_z, down_f, down_d, down_c, down_e)

        rs = Copies(rs_send, rs_recv)
        held = []
        counts = [0, 0, 0]
        for r, (kind, _) in enumerate(PIECES):
            i = counts[kind]
            counts[kind] += 1
            slots_of = (g_slots, d_slots, q_slots)[kind]
            c1_of = (c1_g, c1_d, c1_q)[kind]
            held.append(
                (slots_of.at[i % slots_of.shape[0]], c1_of.at[i % c1_of.shape[0]])
                + tuple(bufs[sum(COUNTS[:r]) : sum(COUNTS[: r + 1])])
            )

        def rs_1(r):
            G, C1 = held[r][:2]
            rs.start((r, 0), G.at[:, :, :, :, nc], C1, dev_c)

        def rs_2(r):
            G, C1, XA, YB, S3, ZR, FIN = held[r]
            n = C1.shape[-1]
            rs.arrived((r, 0), C1, dev_c)
            for a in range(C1.shape[0]):
                for zh in range(ZH):
                    for zl in range(2):
                        C1[a, zh, zl] += G[a, zh, zl, :, c]
            rs.start((r, 1), C1.at[:, :, 0, nx], XA, dev_x)
            rs.start((r, 2), C1.at[:, :, 1, :, :, cols(n, ny)], YB, dev_y)
            rs.sent((r, 0))

        def rs_3(r):
            G, C1, XA, YB, S3, ZR, FIN = held[r]
            n = C1.shape[-1]
            rs.arrived((r, 1), XA, dev_x)
            XA[...] += C1[:, :, 0, x]
            rs.start((r, 3), XA.at[:, :, :, cols(n, ny)], S3.at[:, :, 0], dev_y)
            rs.arrived((r, 2), YB, dev_y)
            YB[...] += C1[:, :, 1, :, :, cols(n, y)]
            rs.start((r, 4), YB.at[:, :, nx], S3.at[:, :, 1], dev_x)
            rs.sent((r, 1), (r, 2))

        def rs_4(r):
            G, C1, XA, YB, S3, ZR, FIN = held[r]
            n = C1.shape[-1]
            rs.arrived((r, 3), S3.at[:, :, 0], dev_y)
            S3[:, :, 0] += XA[:, :, :, cols(n, y)]
            rs.arrived((r, 4), S3.at[:, :, 1], dev_x)
            S3[:, :, 1] += YB[:, :, x]
            for j in JS:
                zt = lax.rem(z + j, Z)
                rs.start((r, 4 + j), S3.at[:, zt // 2, zt % 2], ZR.at[j - 1], dev_z(zt))
            rs.sent((r, 3), (r, 4))

        def rs_5(r):
            G, C1, XA, YB, S3, ZR, FIN = held[r]
            n = C1.shape[-1]
            total = S3[:, z // 2, z % 2].astype(f32)
            for j in JS:
                rs.arrived((r, 4 + j), ZR.at[j - 1], dev_z(lax.rem(z - j + Z, Z)))
                total = total + ZR[j - 1].astype(f32)
            FIN[:, c, :, cols(n, y)] = total.astype(bf16)
            part = FIN.at[:, c, :, cols(n, y)]
            rs.start((r, 8), part, part, dev_y)
            rs.sent((r, 5), (r, 6), (r, 7))

        def zs_2(r):
            G, C1, ZR, XR, YR, FIN = held[r]
            rs.arrived((r, 0), C1, dev_c)
            for a in range(C1.shape[0]):
                for zh in range(ZH):
                    for zl in range(2):
                        C1[a, zh, zl] += G[a, zh, zl, :, c]
            for j in JS:
                zt = lax.rem(z + j, Z)
                rs.start((r, 4 + j), C1.at[:, zt // 2, zt % 2], ZR.at[j - 1], dev_z(zt))
            rs.sent((r, 0))

        def zs_3(r):
            G, C1, ZR, XR, YR, FIN = held[r]
            total = C1[:, z // 2, z % 2].astype(f32)
            for j in JS:
                rs.arrived((r, 4 + j), ZR.at[j - 1], dev_z(lax.rem(z - j + Z, Z)))
                total = total + ZR[j - 1].astype(f32)
            C1[:, z // 2, z % 2] = total.astype(bf16)
            rs.start((r, 1), C1.at[:, z // 2, z % 2, nx], XR, dev_x)
            rs.sent((r, 5), (r, 6), (r, 7))

        def zs_4(r):
            G, C1, ZR, XR, YR, FIN = held[r]
            rs.arrived((r, 1), XR, dev_x)
            XR[...] += C1[:, z // 2, z % 2, x]
            rs.start((r, 3), XR.at[:, :, cols(XR.shape[-1], ny)], YR, dev_y)
            rs.sent((r, 1))

        def zs_5(r):
            G, C1, ZR, XR, YR, FIN = held[r]
            n = XR.shape[-1]
            rs.arrived((r, 3), YR, dev_y)
            FIN[:, c, :, cols(n, y)] = XR[:, :, cols(n, y)] + YR[...]
            part = FIN.at[:, c, :, cols(n, y)]
            rs.start((r, 8), part, part, dev_y)
            rs.sent((r, 3))

        def rs_6(r):
            FIN = held[r][-1]
            n = FIN.shape[-1]
            rs.arrived((r, 8), FIN.at[:, c, :, cols(n, ny)], dev_y)
            rs.start((r, 9), FIN.at[:, c], FIN.at[:, c], dev_c)
            rs.sent((r, 8))

        outs = []

        def put(src, dst):
            copy = pltpu.make_async_copy(src, dst, out_sem.at[len(outs)])
            copy.start()
            outs.append(copy)

        def rs_7(r):
            FIN = held[r][-1]
            rs.arrived((r, 9), FIN.at[:, nc], dev_c)
            rs.sent((r, 9))
            put(FIN, out_pieces[r])

        gn = Copies(gn_send, gn_recv)
        axis_partners = [dev_x, dev_z(z ^ 1)] + ([dev_z(z ^ 2)] if Z == 4 else [])
        def spread_gains():
            lane = lax.broadcasted_iota(jnp.int32, (per, width), 0)
            at = lax.broadcasted_iota(jnp.int32, (per, width), 1)
            place = jnp.where(lane == at % per, 1.0, 0.0).astype(bf16)
            spread = [mm(g[...], place) for g in (gain_first, gain_second)]
            spread = jnp.concatenate(spread + [jnp.zeros((6, width), f32)], axis=0)
            mine = lax.broadcasted_iota(jnp.int32, (8, width), 1) // per == f
            gsum[0] = jnp.where(mine, spread, 0.0)

        def gn_start(i):
            gn.start(i, gsum.at[i], grecv.at[i], axis_partners[i])

        def gn_finish(i):
            gn.arrived(i, grecv.at[i], axis_partners[i])
            gsum[i + 1] = gsum[i] + grecv[i]

        all_partners = [dev_c, dev_y] + axis_partners
        NA = len(axis_partners)

        def gg_start(i):
            gn.start(NA + i, gg.at[i], ggrecv.at[i], all_partners[i])

        def gg_finish(i):
            gn.arrived(NA + i, ggrecv.at[i], all_partners[i])
            gg[i + 1] = gg[i] + ggrecv[i]

        lane128 = lax.broadcasted_iota(jnp.int32, (slot, 128), 1) % HEAD_DIM
        prow = lax.broadcasted_iota(jnp.int32, (slot, 128), 0)

        def tables():
            rate = jnp.exp(
                (lane128 % HALF).astype(f32) * (-2.0 * math.log(10000.0) / HEAD_DIM)
            )
            for s in range(slots):
                e0 = lens[s, 0]
                e1 = e0 + lens[s, 1]
                e2 = e1 + lens[s, 2]
                e3 = e2 + lens[s, 3]

                def begins(p):
                    b = jnp.where(p >= e0, e0, 0)
                    b = jnp.where(p >= e1, e1, b)
                    b = jnp.where(p >= e2, e2, b)
                    return jnp.where(p >= e3, e3, b)

                angle = (prow - begins(prow)).astype(f32) * rate
                sine = jnp.sin(angle)
                rows = slice(s * slot, (s + 1) * slot)
                cos_t[rows, :] = jnp.cos(angle)
                sin_t[rows, :] = jnp.where(lane128 < HALF, -sine, sine)
                kpos = lax.broadcasted_iota(jnp.int32, (slot, slot), 0)
                qpos = lax.broadcasted_iota(jnp.int32, (slot, slot), 1)
                seen = (kpos >= begins(qpos)) & (kpos <= qpos)
                bias_t[s] = jnp.where(seen, 0.0, -1e30).astype(f32)
                live = jnp.where(prow < e2, 1.0, 0.0)[:, 0:1]
                db[rows, :] = (db[rows, :].astype(f32) * live).astype(bf16)

        def chunks(rows_each, body):
            def step(i, carry):
                body(pl.ds(pl.multiple_of(i * rows_each, rows_each), rows_each))
                return carry

            lax.fori_loop(0, T // rows_each, step, 0)

        def norm_first():
            def body(r):
                s = tok[r, :].astype(f32)
                sc = lax.rsqrt(jnp.mean(s * s, axis=1, keepdims=True) + epsilon)
                na[r, :] = (s * sc * gains[0:1, :]).astype(bf16)
                stats[r, :] = jnp.broadcast_to(sc, (sc.shape[0], 128))

            chunks(128, body)

        def flat(w, n0, n):
            val = w[:, :, :, :, pl.ds(n0, n)]
            return val.reshape(-1, n)

        def project(w, o, turned, factor=1.0):
            N = 256

            def step(i, carry):
                n0 = pl.multiple_of(i * N, N)
                a = mm(na[...], flat(w, n0, N))
                if turned:
                    for j in range(N // 128):
                        turned_part = rope(
                            a[:, j * 128 : (j + 1) * 128], cos_t[...], sin_t[...]
                        )
                        o[:, pl.ds(n0 + j * 128, 128)] = (turned_part * factor).astype(bf16)
                else:
                    o[:, pl.ds(n0, N)] = a.astype(bf16)
                return carry

            lax.fori_loop(0, width // N, step, 0)

        THIRD = slot // 3
        BLOCKS = [(i * THIRD, (i + 1) * THIRD, (i + 1) * THIRD) for i in range(3)]

        def attend_one(s, pair):
            rows = pl.ds(pl.multiple_of(s * slot, slot), slot)
            cs = pl.ds(pl.multiple_of(pair * 128, 128), 128)
            q2, k2, v2 = q[rows, cs], k[rows, cs], v[rows, cs]
            km, vm, om = split_heads(k2), split_heads(v2), split_heads(jnp.ones_like(v2))
            for begin, end, seen in BLOCKS:
                st = mm(stack2(km, 0, seen), q2[begin:end], 1, 1)
                expo = []
                for h in range(2):
                    sc = st[h * seen : (h + 1) * seen] + bias_t[s, :seen, begin:end]
                    top = jnp.max(sc, axis=0, keepdims=True)
                    e = jnp.exp(sc - top)
                    total = jnp.sum(e, axis=0, keepdims=True)
                    expo.append(e.astype(bf16))
                    lse[s, pair, h : h + 1, begin:end] = top + jnp.log(total)
                right = jnp.concatenate([stack2(vm, 0, seen), stack2(om, 0, seen)], axis=1)
                o = mm(jnp.concatenate(expo, axis=0), right, 0, 0)
                here = pl.ds(pl.multiple_of(s * slot, slot) + begin, end - begin)
                ho[here, cs] = (o[:, :128] / o[:, 128:]).astype(bf16)

        def attend(first, count):
            UNROLL = 3

            def step(i, carry):
                for u in range(UNROLL):
                    n = first + i * UNROLL + u
                    attend_one(n // PAIRS, n % PAIRS)
                return carry

            lax.fori_loop(0, count // UNROLL, step, 0)

        def middle():
            def body(r):
                s = tok[r, :].astype(f32) + mm(ho[r, :], wo[...].reshape(width, width))
                sc = lax.rsqrt(jnp.mean(s * s, axis=1, keepdims=True) + epsilon)
                smid[r, :] = s
                outacc[r, :] = s
                dnf[r, :] = jnp.zeros_like(s)
                nf[r, :] = (s * sc * gains[1:2, :]).astype(bf16)
                stats[r, :] = jnp.where(
                    lax.broadcasted_iota(jnp.int32, (sc.shape[0], 128), 1) == 0, stats[r, :], sc
                )

            chunks(slot, body)

        def ffn_hidden(i, s):
            wg_n, wu_n = (wgu[i][a].reshape(width, NB) for a in range(2))
            wd_n = wd[i].reshape(NB, width)

            r = slice(s * slot, (s + 1) * slot)
            g = mm(nf[r, :], wg_n)
            u = mm(nf[r, :], wu_n)
            dh = mm(db[r, :], wd_n, 1, 1)
            sg = 1.0 / (1.0 + jnp.exp(-g))
            si = g * sg
            hs[r, :] = (si * u).astype(bf16)
            dus[r, :] = (dh * si).astype(bf16)
            dgs[r, :] = (dh * u * (sg * (1.0 + g * (1.0 - sg)))).astype(bf16)

        def ffn_streams(i):
            outacc[...] += mm(hs[...], wd[i].reshape(NB, width))
            dnf[...] += mm(dgs[...], wgu[i][0].reshape(width, NB), 1, 1)
            dnf[...] += mm(dus[...], wgu[i][1].reshape(width, NB), 1, 1)

        def ffn_grads(i):
            G = held[i][0]
            G[0] = mm(nf[...], dgs[...], 0, 0).astype(bf16).reshape(G.shape[1:])
            G[1] = mm(nf[...], dus[...], 0, 0).astype(bf16).reshape(G.shape[1:])
            gd = mm(hs[...], db[...], 0, 0).astype(bf16).reshape(2, 2, 2, RD, width)
            for sub in range(2):
                held[Z + sub][0][0, i // 2, i % 2] = gd[:, :, sub]

        def middle_back():
            C = 128

            def step(i, acc):
                r = pl.ds(pl.multiple_of(i * C, C), C)
                dn, s, sc = dnf[r, :], smid[r, :], stats[r, 1:2]
                w = dn * gains[1:2, :]
                acc = acc + jnp.sum((dn * (s * sc)).reshape(C // 8, 8, width), axis=0)
                back = sc * w - s * (sc * sc * sc * jnp.mean(w * s, axis=1, keepdims=True))
                dm = db[r, :].astype(f32) + back
                dnf[r, :] = dm
                db[r, :] = dm.astype(bf16)
                return acc

            acc = lax.fori_loop(0, T // C, step, jnp.zeros((8, width), f32))
            gg[0, 1:2] = jnp.sum(acc, axis=0, keepdims=True)

        def grad_out_proj():
            G = held[Z + 2][0]
            val = mm(ho[...], db[...], 0, 0).astype(bf16)
            for a in range(QB):
                G[a] = val[:, a * QN : (a + 1) * QN].reshape(G.shape[1:])

        def heads_back():
            for zi in range(ZH):
                w = wo[2 * zi : 2 * zi + 2].reshape(8 * R, width)
                nf[:, zi * 8 * R : (zi + 1) * 8 * R] = mm(db[...], w, 1, 1).astype(bf16)

        def attend_back_one(s, pair):
            rows = pl.ds(pl.multiple_of(s * slot, slot), slot)
            cs = pl.ds(pl.multiple_of(pair * 128, 128), 128)
            q2, k2, v2, d2 = q[rows, cs], k[rows, cs], v[rows, cs], nf[rows, cs]
            km, vm, qm, dm = (split_heads(a) for a in (k2, v2, q2, d2))
            B = THIRD
            P, S = {}, {}
            for name, begin, end, seen in ((0, 0, B, B), (1, B, slot, slot)):
                st = mm(stack2(km, 0, seen), q2[begin:end], 1, 1)
                dp = mm(stack2(vm, 0, seen), d2[begin:end], 1, 1)
                for h in range(2):
                    part = slice(h * seen, (h + 1) * seen)
                    p = jnp.exp(
                        st[part]
                        + bias_t[s, :seen, begin:end]
                        - lse[s, pair, h : h + 1, begin:end]
                    )
                    P[name, h] = p.astype(bf16)
                    centre = jnp.sum(p * dp[part], axis=0, keepdims=True)
                    S[name, h] = (p * (dp[part] - centre)).astype(bf16)

            def key_side(w, m):
                first = jnp.concatenate([w[0, 0], w[0, 1], w[1, 0][:B], w[1, 1][:B]], axis=1)
                top = mm(first, jnp.concatenate([stack2(m, 0, B), stack2(m, B, slot)], axis=0))
                rest = jnp.concatenate([w[1, 0][B:], w[1, 1][B:]], axis=1)
                return jnp.concatenate([top, mm(rest, stack2(m, B, slot))], axis=0)

            co, si = cos_t[rows, :], -sin_t[rows, :]
            v[rows, cs] = key_side(P, dm).astype(bf16)
            k[rows, cs] = rope(key_side(S, qm), co, si).astype(bf16)
            dq = [
                mm(jnp.concatenate([S[n, 0], S[n, 1]], axis=0), stack2(km, 0, seen), 0, 0)
                for n, seen in ((0, B), (1, slot))
            ]
            q[rows, cs] = rope(jnp.concatenate(dq, axis=0) * FACTOR, co, si).astype(bf16)

        def attend_back(block, s):
            per_block = QN // 128

            def step(i, carry):
                attend_back_one(s, i + block * per_block)
                return carry

            lax.fori_loop(0, per_block, step, 0)

        def attend_grads(block):
            G = held[Z + 3 + block][0]
            at = slice(block * QN, (block + 1) * QN)
            grads = jnp.concatenate([q[:, at], k[:, at], v[:, at]], axis=1)
            val = mm(na[...], grads, 0, 0).astype(bf16)
            for a in range(3):
                G[a] = val[:, a * QN : (a + 1) * QN].reshape(G.shape[1:])

        def first_back(i):
            N = width // 2

            def rows_of(w):
                return w[i * ZH : (i + 1) * ZH].reshape(N, width)

            smid[:, i * N : (i + 1) * N] = (
                mm(q[...], rows_of(wq), 1, 1)
                + mm(k[...], rows_of(wk), 1, 1)
                + mm(v[...], rows_of(wv), 1, 1)
            )

        def first_norm_back():
            C = 128

            def step(i, acc):
                r = pl.ds(pl.multiple_of(i * C, C), C)
                dn, s, sc = smid[r, :], tok[r, :].astype(f32), stats[r, 0:1]
                w = dn * gains[0:1, :]
                acc = acc + jnp.sum((dn * (s * sc)).reshape(C // 8, 8, width), axis=0)
                back = sc * w - s * (sc * sc * sc * jnp.mean(w * s, axis=1, keepdims=True))
                tok[r, :] = (dnf[r, :] + back).astype(bf16)
                return acc

            acc = lax.fori_loop(0, T // C, step, jnp.zeros((8, width), f32))
            gg[0, 0:1] = jnp.sum(acc, axis=0, keepdims=True)

        def result():
            parts = ((hs, 0, NB), (dus, NB, width - NB))
            for held_in, begin, n in parts:
                held_in[:, :n] = outacc[:, begin : begin + n].astype(bf16)
            for s in range(slots):
                for held_in, begin, n in parts:
                    part = held_in.at[pl.ds(s * slot, slot), pl.ds(0, n)]
                    put(part, out_main.at[s, :, pl.ds(begin, n)])

        def first_norm():
            gains[...] = gsum[NA]
            norm_first()

        def gains_step(i):
            gn_finish(i)
            if i + 1 < NA:
                gn_start(i + 1)

        def gain_grads_step(i):
            gg_finish(i)
            if i + 1 < len(all_partners):
                gg_start(i + 1)

        def reduce_step(k, r):
            plain = (rs_1, rs_2, rs_3, rs_4, rs_5, rs_6, rs_7)
            along_z = (rs_1, zs_2, zs_3, zs_4, zs_5, rs_6, rs_7)
            (along_z if r in ALONG_Z_FIRST else plain)[k - 1](r)

        quarter = slots * PAIRS // 4
        comm = (
            *(from_plane(k) for k in range(5)), *(None,) * 5,
            None, *(functools.partial(reduce_step, k) for k in range(1, 8)), None, None,
            gn_start, gains_step, gg_start, gain_grads_step,
        )
        compute = (
            lambda _: tables(),
            lambda _: first_norm(),
            lambda i: project((wq, wk, wv)[i], (q, k, v)[i], i < 2, (FACTOR, 1.0, 1.0)[i]),
            lambda i: attend(i * quarter, quarter),
            lambda _: middle(),
            lambda i: ffn_hidden(i // 2, i % 2),
            ffn_streams,
            ffn_grads,
            lambda _: middle_back(),
            lambda _: grad_out_proj(),
            lambda _: heads_back(),
            lambda i: attend_back(i // 2, i % 2),
            attend_grads,
            first_back,
            lambda _: first_norm_back(),
            lambda _: result(),
        )
        FIRST_GAINS, TABLES, FIRST_NORM_BACK, RESULT = 20, 30, 44, 45
        pl.semaphore_wait(barrier, len(partners))
        for i, code in enumerate(ORDER):
            kind, n = divmod(code, 100)
            if i == 1:
                fetch_rest()
            if kind == FIRST_GAINS:
                spread_gains()
            if kind == TABLES:
                have(TOKENS)
            if kind < 30:
                comm[kind](n)
            elif kind == RESULT:
                result()
            else:
                pl.when(f >= 0)(functools.partial(compute[kind - 30], n))
            if kind == FIRST_NORM_BACK:
                for s in range(slots):
                    put(tok.at[pl.ds(s * slot, slot)], out_tokens.at[s])
        gn.sent(*range(NA + len(all_partners)))
        put(gg.at[len(all_partners)], out_gains)
        for copy in outs:
            copy.wait()

    VM, HB = pltpu.VMEM, pl.BlockSpec(memory_space=pl.ANY)
    S = jax.ShapeDtypeStruct

    def full(rows_half, n):
        return VM((Z, 2, 2, rows_half, n), bf16)

    def piece_bufs(i, kind):
        a, r, n = (G_SHAPE, D_SHAPE, Q_SHAPE)[kind]
        if i in ALONG_Z_FIRST:
            return [
                VM((Z - 1, a, 2, r, n), bf16),
                VM((a, r, n), bf16),
                VM((a, r, n // 2), bf16),
                VM((a, 2, r, n), bf16),
            ]
        return [
            VM((a, ZH, r, n), bf16),
            VM((a, ZH, 2, r, n // 2), bf16),
            VM((a, ZH, 2, r, n // 2), bf16),
            VM((Z - 1, a, r, n // 2), bf16),
            VM((a, 2, r, n), bf16),
        ]

    def grads_of(count, shape):
        a, r, n = shape
        return VM((count, a, ZH, 2, 2, 2, r, n), bf16)

    def first_of(count, shape):
        a, r, n = shape
        return VM((count, a, ZH, 2, 2, r, n), bf16)

    axes = 3 if Z == 4 else 2
    NL = 8 + 2 + 4 * Z + 2 * slots
    scratch = [full(R, width)] * 4 + [VM((Z, 2, 2, 2 * RD, width), bf16)]
    scratch += [VM((2, Z, 2, 2, R, NB), bf16)] * Z
    scratch += [VM((T, width), bf16)] * 6
    scratch += [VM((T, width), f32), VM((T, width), bf16), VM((T, width), bf16)]
    scratch += [VM((T, width), f32)] * 2
    scratch += [VM((T, 128), f32)] * 3
    scratch += [VM((slots, slot, slot), f32), VM((slots, PAIRS, 8, slot), f32)]
    scratch += [VM((T, NB), bf16)] * 3
    scratch += [VM((axes + 1, 8, width), f32), VM((axes, 8, width), f32), VM((8, width), f32)]
    scratch += [VM((axes + 3, 8, width), f32), VM((axes + 2, 8, width), f32)]
    scratch += [grads_of(2, G_SHAPE), grads_of(2, D_SHAPE), grads_of(2, Q_SHAPE)]
    for i, (kind, _) in enumerate(PIECES):
        scratch += piece_bufs(i, kind)
    scratch += [first_of(4, G_SHAPE), first_of(2, D_SHAPE), first_of(1 + QB, Q_SHAPE)]
    DMA = pltpu.SemaphoreType.DMA
    scratch += [DMA((NL,)), DMA((NAG, 17)), DMA((NAG, 17)), DMA((NRS, 10)), DMA((NRS, 10))]
    scratch += [DMA((2 * axes + 2,)), DMA((2 * axes + 2,)), DMA((NRS + 1 + 3 * slots,))]
    out_shape = [S((slots, slot, width), bf16)] * 2 + [S((8, width), f32)]
    for _, (a, r, n) in PIECES:
        out_shape.append(S((a, 2, r, n), bf16))
    call = pl.pallas_call(
        kernel,
        out_shape=out_shape,
        in_specs=[pl.BlockSpec(memory_space=pltpu.SMEM)] + [pl.BlockSpec(memory_space=VM)] * 2 + [HB] * 9,
        out_specs=[HB] * len(out_shape),
        scratch_shapes=scratch,
        compiler_params=pltpu.CompilerParams(
            collective_id=0, has_side_effects=True, vmem_limit_bytes=VMEM_BYTES
        ),
    )

    FINAL = [S((slots, slot, width), bf16)] * 2 + [S((per, width), f32)] * 4
    FINAL += [S((per, ff), f32)] * 2 + [S((ff // fs, width), f32)] + [S((1, per), f32)] * 2
    NF = len(FINAL)

    def finish(*refs):
        made, outs = refs[: 3 + NRS], refs[3 + NRS : 3 + NRS + NF]
        held = refs[3 + NRS + NF : 2 * (3 + NRS) + NF]
        done = refs[2 * (3 + NRS) + NF : -2]
        in_sem, sem = refs[-2:]
        fetched = [
            pltpu.make_async_copy(src, dst, in_sem.at[i])
            for i, (src, dst) in enumerate(zip(made, held))
        ]
        for copy in fetched:
            copy.start()
        f = lax.axis_index("fsdp")
        lane = lax.broadcasted_iota(jnp.int32, (width, 128), 1)
        at = lax.broadcasted_iota(jnp.int32, (width, 128), 0)
        pick = jnp.where((at == lane + f * per) & (lane < per), 1.0, 0.0).astype(bf16)
        stored = []

        def store(i, src):
            copy = pltpu.make_async_copy(src, outs[i], sem.at[i])
            copy.start()
            stored.append(copy)

        for i in range(2):
            fetched[i].wait()
            store(i, held[i])
        pieces = held[3:]
        dq, dk, dv, do, dg, du, dd, first, second = done
        for i in range(Z):
            fetched[3 + i].wait()
            for a, out in enumerate((dg, du)):
                out[:, i * NB : (i + 1) * NB] = pieces[i][a].astype(f32).reshape(per, NB)
        store(6, dg)
        store(7, du)
        for sub in range(2):
            fetched[3 + Z + sub].wait()
            for c in range(2):
                rows = slice((2 * c + sub) * RD, (2 * c + sub + 1) * RD)
                dd[rows, :] = pieces[Z + sub][0, c].astype(f32)
        store(8, dd)
        fetched[5 + Z].wait()
        for a in range(QB):
            do[:, a * QN : (a + 1) * QN] = pieces[Z + 2][a].astype(f32).reshape(per, QN)
        store(5, do)
        for b in range(QB):
            fetched[6 + Z + b].wait()
            for a, out in enumerate((dq, dk, dv)):
                out[:, b * QN : (b + 1) * QN] = pieces[Z + 3 + b][a].astype(f32).reshape(per, QN)
        for i, out in enumerate((dq, dk, dv)):
            store(2 + i, out)
        fetched[2].wait()
        g = held[2][...]
        total = jnp.zeros((8, 128), f32)
        for _ in range(3):
            term = g.astype(bf16)
            total = total + mm(term, pick)
            g = g - term.astype(f32)
        first[...] = total[0:1, :per]
        second[...] = total[1:2, :per]
        store(9, first)
        store(10, second)
        for copy in stored:
            copy.wait()

    post = pl.pallas_call(
        finish,
        out_shape=FINAL,
        in_specs=[HB] * (3 + NRS),
        out_specs=[HB] * NF,
        scratch_shapes=[VM(o.shape, o.dtype) for o in out_shape + FINAL[2:]]
        + [DMA((3 + NRS,)), DMA((NF,))],
        compiler_params=pltpu.CompilerParams(vmem_limit_bytes=VMEM_BYTES),
    )

    def local(tokens, lengths, wq, wk, wv, wo, wg, wu, wd, gain_attn, gain_ffn, gradient):
        rows = (gain_attn.reshape(1, per), gain_ffn.reshape(1, per))
        made = call(lengths, *rows, tokens, gradient, wq, wk, wv, wo, wg, wu, wd)
        *grads, first, second = post(*made)
        return (*grads, first.reshape(per), second.reshape(per))

    return local


def layout(lengths, slot):
    pieces = lengths.shape[0]
    bounds = jnp.stack([jnp.sum(lengths[: j + 1]) for j in range(pieces)])
    places = lax.iota(jnp.int32, slot)
    piece_of = jnp.sum((places[:, None] >= bounds[None, :]).astype(jnp.int32), axis=1)
    piece_begins = bounds - lengths
    member = piece_of[:, None] == lax.iota(jnp.int32, pieces)[None, :]
    begins = jnp.sum(jnp.where(member, piece_begins[None, :], 0), axis=1)
    offsets = places - begins
    live = (piece_of < pieces - 1).astype(jnp.float32)
    visible = (piece_of[:, None] == piece_of[None, :]) & (places[None, :] <= places[:, None])
    return (offsets, live, visible)


def rotary(offsets, head_dim):
    half = head_dim // 2
    rates = jnp.power(10000.0, -2.0 * lax.iota(jnp.float32, half) / head_dim)
    angle = offsets.astype(jnp.float32)[:, None] * rates[None, :]
    angle = jnp.concatenate([angle, angle], axis=1)
    return (jnp.cos(angle), jnp.sin(angle))


def turn(values, cosine, sine, sign):
    half = values.shape[-1] // 2
    swapped = jnp.concatenate([-values[..., half:], values[..., :half]], axis=-1)
    return values * cosine[:, None, :] + sign * swapped * sine[:, None, :]


def matmul(left, right):
    return jnp.dot(left, right, preferred_element_type=jnp.float32)


def left_inner(left, right):
    return lax.dot_general(
        left, right, (((0,), (0,)), ((), ())), preferred_element_type=jnp.float32
    )


def right_inner(left, right):
    return lax.dot_general(
        left, right, (((1,), (1,)), ((), ())), preferred_element_type=jnp.float32
    )


def norm_back(grad_normed, gain, stream, scale):
    weighted = grad_normed * gain.astype(jnp.float32)
    gain_grad = jnp.sum(grad_normed * stream * scale, axis=0)
    stream_grad = scale * weighted - stream * scale * scale * scale * jnp.mean(
        weighted * stream, axis=1, keepdims=True
    )
    return (stream_grad, gain_grad)


def forward_pass(tokens_slot, weights, cosine, sine, visible):
    w_query, w_key, w_value, w_out, w_gate, w_up, w_down, gain_attn, gain_ffn = weights
    slot = tokens_slot.shape[0]
    factor = HEAD_DIM ** (-0.5)
    stream = tokens_slot.astype(jnp.float32)
    scale_attn = lax.rsqrt(jnp.mean(stream * stream, axis=1, keepdims=True) + epsilon)
    normed_attn = (stream * scale_attn * gain_attn.astype(jnp.float32)).astype(jnp.bfloat16)
    query_rows = turn(
        matmul(normed_attn, w_query).reshape(slot, HEADS, HEAD_DIM), cosine, sine, 1.0
    ).astype(jnp.bfloat16)
    key_rows = turn(
        matmul(normed_attn, w_key).reshape(slot, HEADS, HEAD_DIM), cosine, sine, 1.0
    ).astype(jnp.bfloat16)
    value_rows = matmul(normed_attn, w_value).astype(jnp.bfloat16).reshape(slot, HEADS, HEAD_DIM)
    scores = (
        jnp.einsum("qhd,khd->hqk", query_rows, key_rows, preferred_element_type=jnp.float32)
        * factor
    )
    scores = jnp.where(visible[None], scores, -1e30)
    top = jnp.max(scores, axis=-1, keepdims=True)
    weights_exp = jnp.exp(scores - top)
    totals = jnp.sum(weights_exp, axis=-1, keepdims=True)
    probs = weights_exp / totals
    log_total = top + jnp.log(totals)
    mixed = jnp.einsum(
        "hqk,khd->qhd", probs.astype(jnp.bfloat16), value_rows, preferred_element_type=jnp.float32
    )
    heads_out = mixed.reshape(slot, HEADS * HEAD_DIM).astype(jnp.bfloat16)
    stream_mid = stream + matmul(heads_out, w_out)
    scale_ffn = lax.rsqrt(jnp.mean(stream_mid * stream_mid, axis=1, keepdims=True) + epsilon)
    normed_ffn = (stream_mid * scale_ffn * gain_ffn.astype(jnp.float32)).astype(jnp.bfloat16)
    gate_pre = matmul(normed_ffn, w_gate)
    up_branch = matmul(normed_ffn, w_up)
    hidden = (gate_pre * jax.nn.sigmoid(gate_pre) * up_branch).astype(jnp.bfloat16)
    result = stream_mid + matmul(hidden, w_down)
    kept = (
        stream,
        scale_attn,
        normed_attn,
        query_rows,
        key_rows,
        value_rows,
        log_total,
        heads_out,
        stream_mid,
        scale_ffn,
        normed_ffn,
        gate_pre,
        up_branch,
        hidden,
    )
    return (kept, result)


def backward_pass(kept, weights, cotangent, live, cosine, sine, visible):
    w_query, w_key, w_value, w_out, w_gate, w_up, w_down, gain_attn, gain_ffn = weights
    (
        stream,
        scale_attn,
        normed_attn,
        query_rows,
        key_rows,
        value_rows,
        log_total,
        heads_out,
        stream_mid,
        scale_ffn,
        normed_ffn,
        gate_pre,
        up_branch,
        hidden,
    ) = kept
    slot = stream.shape[0]
    factor = HEAD_DIM ** (-0.5)
    d_out = cotangent.astype(jnp.float32) * live[:, None]
    d_branch = d_out.astype(jnp.bfloat16)
    grad_down = left_inner(hidden, d_branch)
    d_hidden = right_inner(d_branch, w_down)
    sigma = jax.nn.sigmoid(gate_pre)
    d_gate = (d_hidden * up_branch * sigma * (1.0 + gate_pre * (1.0 - sigma))).astype(jnp.bfloat16)
    d_up = (d_hidden * gate_pre * sigma).astype(jnp.bfloat16)
    grad_gate = left_inner(normed_ffn, d_gate)
    grad_up = left_inner(normed_ffn, d_up)
    d_normed_ffn = right_inner(d_gate, w_gate) + right_inner(d_up, w_up)
    mid_back, grad_gain_ffn = norm_back(d_normed_ffn, gain_ffn, stream_mid, scale_ffn)
    d_mid = d_out + mid_back
    d_attn = d_mid.astype(jnp.bfloat16)
    grad_out_proj = left_inner(heads_out, d_attn)
    d_heads = right_inner(d_attn, w_out).astype(jnp.bfloat16).reshape(slot, HEADS, HEAD_DIM)
    scores = (
        jnp.einsum("qhd,khd->hqk", query_rows, key_rows, preferred_element_type=jnp.float32)
        * factor
    )
    probs = jnp.where(visible[None], jnp.exp(scores - log_total), 0.0)
    d_probs = jnp.einsum("qhd,khd->hqk", d_heads, value_rows, preferred_element_type=jnp.float32)
    d_values = jnp.einsum(
        "hqk,qhd->khd", probs.astype(jnp.bfloat16), d_heads, preferred_element_type=jnp.float32
    )
    d_values = d_values.astype(jnp.bfloat16).reshape(slot, HEADS * HEAD_DIM)
    centre = jnp.sum(probs * d_probs, axis=-1, keepdims=True)
    d_scores = (probs * (d_probs - centre)).astype(jnp.bfloat16)
    d_query_rot = (
        jnp.einsum("hqk,khd->qhd", d_scores, key_rows, preferred_element_type=jnp.float32) * factor
    )
    d_key_rot = (
        jnp.einsum("hqk,qhd->khd", d_scores, query_rows, preferred_element_type=jnp.float32)
        * factor
    )
    d_queries = (
        turn(d_query_rot, cosine, sine, -1.0).astype(jnp.bfloat16).reshape(slot, HEADS * HEAD_DIM)
    )
    d_keys = (
        turn(d_key_rot, cosine, sine, -1.0).astype(jnp.bfloat16).reshape(slot, HEADS * HEAD_DIM)
    )
    grad_query = left_inner(normed_attn, d_queries)
    grad_key = left_inner(normed_attn, d_keys)
    grad_value = left_inner(normed_attn, d_values)
    d_normed_attn = (
        right_inner(d_queries, w_query)
        + right_inner(d_keys, w_key)
        + right_inner(d_values, w_value)
    )
    stream_back, grad_gain_attn = norm_back(d_normed_attn, gain_attn, stream, scale_attn)
    grad_input = d_mid + stream_back
    grads = (
        grad_query,
        grad_key,
        grad_value,
        grad_out_proj,
        grad_gate,
        grad_up,
        grad_down,
        grad_gain_attn,
        grad_gain_ffn,
    )
    return (grads, grad_input)


def local_general(
    tokens, lengths, w_query, w_key, w_value, w_out, w_gate, w_up, w_down, gain_attn, gain_ffn,
    output_gradient,
):
    rows = (w_query, w_key, w_value, w_out, w_gate, w_up, w_down, gain_attn, gain_ffn)
    weights = tuple(lax.all_gather(w, "fsdp", axis=0, tiled=True) for w in rows)
    results, input_grads, totals = [], [], None
    for i in range(tokens.shape[0]):
        offsets, live, visible = layout(lengths[i], tokens.shape[1])
        cosine, sine = rotary(offsets, HEAD_DIM)
        kept, result = forward_pass(tokens[i], weights, cosine, sine, visible)
        grads, grad_input = backward_pass(
            kept, weights, output_gradient[i], live, cosine, sine, visible
        )
        results.append(result.astype(jnp.bfloat16))
        input_grads.append(grad_input.astype(jnp.bfloat16))
        totals = grads if totals is None else tuple(a + b for a, b in zip(totals, grads))
    shares = (lax.psum_scatter(g, "fsdp", scatter_dimension=0, tiled=True) for g in totals)
    summed = tuple(lax.psum(g, "dp") for g in shares)
    return (jnp.stack(results), jnp.stack(input_grads)) + summed


def solution(mesh):
    row, vec = P("fsdp", None), P("fsdp")
    wide = P(("dp", "fsdp"), None, None)
    in_specs = (wide, P(("dp", "fsdp"), None)) + (row,) * 7 + (vec, vec, wide)
    out_specs = (wide, wide) + (row,) * 7 + (vec, vec)

    def local(tokens, lengths, *rest):
        slots, slot, width = tokens.shape
        ff = rest[4].shape[1]
        if (mesh.shape["dp"], mesh.shape["fsdp"]) == (4, 8) and (width, ff) == (768, 2048):
            return build(mesh, slots, slot, width, ff)(tokens, lengths, *rest)
        return local_general(tokens, lengths, *rest)

    return jax.shard_map(local, mesh=mesh, in_specs=in_specs, out_specs=out_specs, check_vma=False)
```

```python
import functools
import math
import jax
import jax.numpy as jnp
from jax import lax
from jax.experimental import pallas as pl
from jax.experimental.pallas import tpu as pltpu
from jax.sharding import PartitionSpec as P

HEADS = 12
HEAD_DIM = 64
HALF = HEAD_DIM // 2
FACTOR = HEAD_DIM ** (-0.5)
epsilon = 1e-05
f32 = jnp.float32
bf16 = jnp.bfloat16
MESH = pl.DeviceIdType.MESH
VMEM_BYTES = 66_900_000
ALONG_Z_FIRST = (1, 5)
OVER_X = (1, 2, 3, 6, 9, 10, 11)

ORDER = (
    0, 2000, 1, 2, 3000, 2100, 100, 101, 3, 200, 102, 4, 2101, 201, 300, 103, 5, 400, 202, 301,
    104, 6, 2102, 3100, 401, 203, 3200, 302, 105, 7, 3201, 204, 402, 3202, 303, 106, 107, 8, 9,
    3300, 205, 403, 3301, 304, 3302, 3303, 3400, 206, 108, 10, 404, 207, 109, 11, 305, 405,
    3500, 306, 3501, 110, 3700, 1100, 307, 208, 111, 406, 3600, 209, 1200, 407, 3502, 3503,
    3701, 1101, 210, 308, 3601, 211, 309, 1201, 408, 409, 3504, 3505, 1300, 3702, 1102, 310,
    311, 3602, 1400, 1202, 410, 411, 3506, 3507, 3703, 1103, 1104, 1105, 3603, 1302, 3800, 1204,
    1301, 1203, 3900, 1106, 1205, 1402, 4000, 4100, 1206, 1500, 4101, 1304, 4200, 1107, 1401,
    4102, 4103, 1207, 1303, 4201, 1108, 4104, 1600, 1306, 4105, 1208, 1700, 1404, 1501, 4202,
    1109, 4300, 1307, 1305, 4301, 1403, 1209, 4400, 2200, 1406, 1502, 4500, 2300, 1308, 1504,
    1601, 1407, 1701, 1405, 1503, 1309, 1602, 2301, 1506, 1702, 1408, 1604, 2302, 1505, 1507,
    1704, 1603, 1409, 1703, 1606, 1508, 2303, 1605, 1706, 1607, 1608, 1705, 1707, 1509, 1708,
    2304, 1609, 1709,
)


def mm(a, b, ca=1, cb=0):
    return lax.dot_general(a, b, (((ca,), (cb,)), ((), ())), preferred_element_type=f32)


def rope(v, cosine, sine):
    lane = lax.broadcasted_iota(jnp.int32, v.shape, 1) % HEAD_DIM
    swapped = jnp.where(lane < HALF, pltpu.roll(v, 128 - HALF, 1), pltpu.roll(v, HALF, 1))
    return v * cosine + swapped * sine


def split_heads(x):
    lane = lax.broadcasted_iota(jnp.int32, x.shape, 1)
    zero = jnp.zeros_like(x)
    return jnp.where(lane < HEAD_DIM, x, zero), jnp.where(lane < HEAD_DIM, zero, x)


def stack2(pair, begin, end):
    return jnp.concatenate([pair[0][begin:end], pair[1][begin:end]], axis=0)


class Copies:
    def __init__(self, send, recv):
        self.send, self.recv, self.started = send, recv, {}

    def start(self, key, src, dst, device, there=None):
        copy = pltpu.make_async_remote_copy(
            src_ref=src,
            dst_ref=dst,
            send_sem=self.send.at[key],
            recv_sem=self.recv.at[there or key],
            device_id=device,
            device_id_type=MESH,
        )
        copy.start()
        self.started[key] = copy

    def arrived(self, key, dst, device):
        pltpu.make_async_remote_copy(
            src_ref=dst,
            dst_ref=dst,
            send_sem=self.send.at[key],
            recv_sem=self.recv.at[key],
            device_id=device,
            device_id_type=MESH,
        ).wait_recv()

    def gone(self, key, src, device):
        pltpu.make_async_remote_copy(
            src_ref=src,
            dst_ref=src,
            send_sem=self.send.at[key],
            recv_sem=self.recv.at[key],
            device_id=device,
            device_id_type=MESH,
        ).wait_send()

    def sent(self, *keys):
        for key in keys:
            self.started.pop(key).wait_send()


def build(mesh, slots, slot, width, ff):
    dps, fs = mesh.shape["dp"], mesh.shape["fsdp"]
    Z, ZH = fs // 2, fs // 4
    T = slots * slot
    R, RD = width // fs // 2, ff // fs // 4
    per = width // fs
    NB = ff // Z
    QN = 256
    QB = width // QN
    PAIRS = width // 128
    NAG = 4 + 2 * Z
    G_SHAPE, D_SHAPE, Q_SHAPE = (2, R, NB), (1, RD, width), (3, R, QN)
    PIECES = (
        [(0, G_SHAPE)] * Z
        + [(1, D_SHAPE)] * 2
        + [(2, Q_SHAPE)] * (1 + QB)
    )
    NRS = len(PIECES)
    COUNTS = [4 if r in ALONG_Z_FIRST else 5 for r in range(NRS)]

    def kernel(
        lens, gain_first, gain_second, tokens, gradient, w_query, w_key, w_value, w_out, w_gate, w_up, w_down,
        out_main, out_tokens, out_gains, *rest,
    ):
        out_pieces, rest = rest[:NRS], rest[NRS:]
        wq, wk, wv, wo, wd = rest[:5]
        wgu, rest = rest[5 : 5 + Z], rest[5 + Z :]
        (
            tok, na, q, k, v, ho, smid, nf, db, dnf, outacc,
            cos_t, sin_t, stats, bias_t, lse, hs, dgs, dus,
            gsum, grecv, gains, gg, ggrecv,
            g_slots, d_slots, q_slots,
        ) = rest[:27]
        rest = rest[27:]
        bufs, rest = rest[: sum(COUNTS)], rest[sum(COUNTS) :]
        c1_g, c1_d, c1_q = rest[:3]
        (local_sem, ag_send, ag_recv, rs_send, rs_recv, gn_send, gn_recv, out_sem) = rest[3:]

        d, f = lax.axis_index("dp"), lax.axis_index("fsdp")
        y, c = d // 2, d % 2
        z, x = f // 2, f % 2
        nx, ny, nc = 1 - x, 1 - y, 1 - c
        dev_x, dev_y, dev_c = (d, z * 2 + nx), (ny * 2 + c, f), (y * 2 + nc, f)

        def dev_z(zt):
            return (d, zt * 2 + x)

        JS = [1, Z - 1] + list(range(2, Z - 1))

        partners = [dev_c, dev_x, dev_y] + [dev_z(lax.rem(z + j, Z)) for j in range(1, Z)]
        barrier = pltpu.get_barrier_semaphore()
        for p in partners:
            pl.semaphore_signal(barrier, inc=1, device_id=p, device_id_type=MESH)
        fetched = []
        TOKENS, DOWN = -1, -2

        def fetch(group, src, dst):
            copy = pltpu.make_async_copy(src, dst, local_sem.at[len(fetched)])
            copy.start()
            fetched.append((group, copy))

        def have(group):
            for g, copy in fetched:
                if g == group:
                    copy.wait()

        for i, (src, w) in enumerate(((w_query, wq), (w_key, wk), (w_value, wv), (w_out, wo))):
            for h in range(2):
                fetch(i, src.at[pl.ds(h * R, R)], w.at[z, x, h])

        def fetch_rest():
            for s in range(slots):
                fetch(TOKENS, tokens.at[s], tok.at[pl.ds(s * slot, slot)])
                fetch(TOKENS, gradient.at[s], db.at[pl.ds(s * slot, slot)])
            for h in range(2):
                fetch(DOWN, w_down.at[pl.ds(2 * h * RD, 2 * RD)], wd.at[z, x, h])
            for i in range(Z):
                for a, src in enumerate((w_gate, w_up)):
                    for h in range(2):
                        part = src.at[pl.ds(h * R, R), pl.ds(i * NB, NB)]
                        fetch(4 + 2 * i, part, wgu[i].at[a, z, x, h])

        ag = Copies(ag_send, ag_recv)

        def view(p, zi, xi, ci, at=slice(None)):
            if p < 4:
                return (wq, wk, wv, wo)[p].at[zi, xi, ci, :, at]
            return wgu[p // 2 - 2].at[:, zi, xi, ci, :, at]

        def cols(n, which):
            return pl.ds(pl.multiple_of(which * (n // 2), n // 2), n // 2)

        def side_of(p):
            return [3] if p in OVER_X else []

        def width_of(p):
            return width if p < 4 else NB

        def ag_z(p):
            have(p)
            n = width_of(p)
            for j in JS:
                r = view(p, z, x, c, cols(n, y))
                ag.start((p, j - 1), r, r, dev_z(lax.rem(z + j, Z)))
            r = view(p, z, x, c)
            ag.start((p, 3), r, r, dev_x)

        def ag_f(p):
            n = width_of(p)
            for j in JS:
                zs = lax.rem(z - j + Z, Z)
                r = view(p, zs, x, c, cols(n, y))
                ag.arrived((p, j - 1), r, dev_z(zs))
                ag.start((p, 3 + j), r, r, dev_x)
                ag.start((p, 6 + j), r, r, dev_y)

        def ag_d(p):
            n = width_of(p)
            for j in JS:
                zs = lax.rem(z - j + Z, Z)
                r = view(p, zs, nx, c, cols(n, y))
                ag.arrived((p, 3 + j), r, dev_x)
                if j not in side_of(p):
                    ag.start((p, 9 + j), r, r, dev_y)
                r = view(p, zs, x, c, cols(n, ny))
                ag.arrived((p, 6 + j), r, dev_y)
                if j in side_of(p):
                    ag.start((p, 9 + j), r, r, dev_x)
                r = view(p, zs, x, c)
                ag.start((p, 12 + j), r, r, dev_c)
            ag.arrived((p, 3), view(p, z, nx, c), dev_x)

        def ag_c(p):
            n = width_of(p)
            for j in JS:
                zs = lax.rem(z - j + Z, Z)
                r = view(p, zs, nx, c, cols(n, ny))
                ag.arrived((p, 9 + j), r, dev_x if j in side_of(p) else dev_y)
            r = view(p, slice(None), nx, c)
            ag.start((p, 16), r, r, dev_c)

        def ag_e(p):
            for j in JS:
                ag.arrived((p, 12 + j), view(p, lax.rem(z - j + Z, Z), x, nc), dev_c)
            ag.arrived((p, 16), view(p, slice(None), nx, nc), dev_c)

        def from_plane(step):
            def run(p):
                if p < 4 or p % 2 == 0:
                    plain[step](p)
                else:
                    by_plane[step](p, p // 2 - 2)

            return run

        zs_to = [dev_z(i) for i in range(Z)]

        def down_z(p, i):
            if i == 0:
                have(DOWN)

            @pl.when(z == i)
            def _():
                r = wd.at[i, x, c, :, cols(width, y)]
                for j in JS:
                    ag.start((p, j - 1), r, r, zs_to[(i + j) % Z], (p, 0))
                r = wd.at[i, x, c]
                ag.start((p, 3), r, r, dev_x)

        def down_f(p, i):
            @pl.when(z != i)
            def _():
                r = wd.at[i, x, c, :, cols(width, y)]
                ag.arrived((p, 0), r, zs_to[i])
                ag.start((p, 4), r, r, dev_x)
                ag.start((p, 5), r, r, dev_y)

        def down_d(p, i):
            @pl.when(z != i)
            def _():
                r = wd.at[i, nx, c, :, cols(width, y)]
                ag.arrived((p, 4), r, dev_x)
                if p not in OVER_X:
                    ag.start((p, 6), r, r, dev_y)
                r = wd.at[i, x, c, :, cols(width, ny)]
                ag.arrived((p, 5), r, dev_y)
                if p in OVER_X:
                    ag.start((p, 6), r, r, dev_x)
                r = wd.at[i, x, c]
                ag.start((p, 7), r, r, dev_c)

            @pl.when(z == i)
            def _():
                ag.arrived((p, 3), wd.at[i, nx, c], dev_x)

        def down_c(p, i):
            @pl.when(z != i)
            def _():
                ag.arrived((p, 6), wd.at[i, nx, c, :, cols(width, ny)], (dev_y, dev_x)[p in OVER_X])

            r = wd.at[i, nx, c]
            ag.start((p, 8), r, r, dev_c)

        def down_e(p, i):
            half = wd.at[i, x, c, :, cols(width, y)]

            @pl.when(z != i)
            def _():
                ag.arrived((p, 7), wd.at[i, x, nc], dev_c)
                ag.gone((p, 4), half, dev_x)
                ag.gone((p, 5), half, dev_y)
                ag.gone((p, 6), half, (dev_y, dev_x)[p in OVER_X])
                ag.gone((p, 7), wd.at[i, x, c], dev_c)

            @pl.when(z == i)
            def _():
                for j in JS:
                    ag.gone((p, j - 1), half, zs_to[(i + j) % Z])
                ag.gone((p, 3), wd.at[i, x, c], dev_x)

            ag.arrived((p, 8), wd.at[i, nx, nc], dev_c)
            ag.gone((p, 8), wd.at[i, nx, c], dev_c)

        plain = (ag_z, ag_f, ag_d, ag_c, ag_e)
        by_plane = (down_z, down_f, down_d, down_c, down_e)

        rs = Copies(rs_send, rs_recv)
        held = []
        counts = [0, 0, 0]
        for r, (kind, _) in enumerate(PIECES):
            i = counts[kind]
            counts[kind] += 1
            slots_of = (g_slots, d_slots, q_slots)[kind]
            c1_of = (c1_g, c1_d, c1_q)[kind]
            held.append(
                (slots_of.at[i % slots_of.shape[0]], c1_of.at[i % c1_of.shape[0]])
                + tuple(bufs[sum(COUNTS[:r]) : sum(COUNTS[: r + 1])])
            )

        def rs_1(r):
            G, C1 = held[r][:2]
            rs.start((r, 0), G.at[:, :, :, :, nc], C1, dev_c)

        def rs_2(r):
            G, C1, XA, YB, S3, ZR, FIN = held[r]
            n = C1.shape[-1]
            rs.arrived((r, 0), C1, dev_c)
            for a in range(C1.shape[0]):
                for zh in range(ZH):
                    for zl in range(2):
                        C1[a, zh, zl] += G[a, zh, zl, :, c]
            rs.start((r, 1), C1.at[:, :, 0, nx], XA, dev_x)
            rs.start((r, 2), C1.at[:, :, 1, :, :, cols(n, ny)], YB, dev_y)
            rs.sent((r, 0))

        def rs_3(r):
            G, C1, XA, YB, S3, ZR, FIN = held[r]
            n = C1.shape[-1]
            rs.arrived((r, 1), XA, dev_x)
            XA[...] += C1[:, :, 0, x]
            rs.start((r, 3), XA.at[:, :, :, cols(n, ny)], S3.at[:, :, 0], dev_y)
            rs.arrived((r, 2), YB, dev_y)
            YB[...] += C1[:, :, 1, :, :, cols(n, y)]
            rs.start((r, 4), YB.at[:, :, nx], S3.at[:, :, 1], dev_x)

        def rs_4(r):
            G, C1, XA, YB, S3, ZR, FIN = held[r]
            n = C1.shape[-1]
            rs.arrived((r, 3), S3.at[:, :, 0], dev_y)
            S3[:, :, 0] += XA[:, :, :, cols(n, y)]
            rs.arrived((r, 4), S3.at[:, :, 1], dev_x)
            S3[:, :, 1] += YB[:, :, x]
            for j in JS:
                zt = lax.rem(z + j, Z)
                rs.start((r, 4 + j), S3.at[:, zt // 2, zt % 2], ZR.at[j - 1], dev_z(zt))

        def rs_5(r):
            G, C1, XA, YB, S3, ZR, FIN = held[r]
            n = C1.shape[-1]
            total = S3[:, z // 2, z % 2].astype(f32)
            for j in JS:
                rs.arrived((r, 4 + j), ZR.at[j - 1], dev_z(lax.rem(z - j + Z, Z)))
                total = total + ZR[j - 1].astype(f32)
            FIN[:, c, :, cols(n, y)] = total.astype(bf16)
            part = FIN.at[:, c, :, cols(n, y)]
            rs.start((r, 8), part, part, dev_y)

        def zs_2(r):
            G, C1, ZR, XR, YR, FIN = held[r]
            rs.arrived((r, 0), C1, dev_c)
            for a in range(C1.shape[0]):
                for zh in range(ZH):
                    for zl in range(2):
                        C1[a, zh, zl] += G[a, zh, zl, :, c]
            for j in JS:
                zt = lax.rem(z + j, Z)
                rs.start((r, 4 + j), C1.at[:, zt // 2, zt % 2], ZR.at[j - 1], dev_z(zt))
            rs.sent((r, 0))

        def zs_3(r):
            G, C1, ZR, XR, YR, FIN = held[r]
            total = C1[:, z // 2, z % 2].astype(f32)
            for j in JS:
                rs.arrived((r, 4 + j), ZR.at[j - 1], dev_z(lax.rem(z - j + Z, Z)))
                total = total + ZR[j - 1].astype(f32)
            C1[:, z // 2, z % 2] = total.astype(bf16)
            rs.start((r, 1), C1.at[:, z // 2, z % 2, nx], XR, dev_x)

        def zs_4(r):
            G, C1, ZR, XR, YR, FIN = held[r]
            rs.arrived((r, 1), XR, dev_x)
            XR[...] += C1[:, z // 2, z % 2, x]
            rs.start((r, 3), XR.at[:, :, cols(XR.shape[-1], ny)], YR, dev_y)

        def zs_5(r):
            G, C1, ZR, XR, YR, FIN = held[r]
            n = XR.shape[-1]
            rs.arrived((r, 3), YR, dev_y)
            FIN[:, c, :, cols(n, y)] = XR[:, :, cols(n, y)] + YR[...]
            part = FIN.at[:, c, :, cols(n, y)]
            rs.start((r, 8), part, part, dev_y)

        def rs_6(r):
            FIN = held[r][-1]
            n = FIN.shape[-1]
            rs.arrived((r, 8), FIN.at[:, c, :, cols(n, ny)], dev_y)
            rs.start((r, 9), FIN.at[:, c], FIN.at[:, c], dev_c)

        outs = []

        def put(src, dst):
            copy = pltpu.make_async_copy(src, dst, out_sem.at[len(outs)])
            copy.start()
            outs.append(copy)

        def rs_7(r):
            FIN = held[r][-1]
            rs.arrived((r, 9), FIN.at[:, nc], dev_c)
            put(FIN, out_pieces[r])

        gn = Copies(gn_send, gn_recv)
        axis_partners = [dev_x, dev_z(z ^ 1)] + ([dev_z(z ^ 2)] if Z == 4 else [])
        def spread_gains():
            lane = lax.broadcasted_iota(jnp.int32, (per, width), 0)
            at = lax.broadcasted_iota(jnp.int32, (per, width), 1)
            place = jnp.where(lane == at % per, 1.0, 0.0).astype(bf16)
            spread = [mm(g[...], place) for g in (gain_first, gain_second)]
            spread = jnp.concatenate(spread + [jnp.zeros((6, width), f32)], axis=0)
            mine = lax.broadcasted_iota(jnp.int32, (8, width), 1) // per == f
            gsum[0] = jnp.where(mine, spread, 0.0)

        def gn_start(i):
            gn.start(i, gsum.at[i], grecv.at[i], axis_partners[i])

        def gn_finish(i):
            gn.arrived(i, grecv.at[i], axis_partners[i])
            gsum[i + 1] = gsum[i] + grecv[i]

        all_partners = [dev_c, dev_y] + axis_partners
        NA = len(axis_partners)

        def gg_start(i):
            gn.start(NA + i, gg.at[i], ggrecv.at[i], all_partners[i])

        def gg_finish(i):
            gn.arrived(NA + i, ggrecv.at[i], all_partners[i])
            gg[i + 1] = gg[i] + ggrecv[i]

        lane128 = lax.broadcasted_iota(jnp.int32, (slot, 128), 1) % HEAD_DIM
        prow = lax.broadcasted_iota(jnp.int32, (slot, 128), 0)

        def tables():
            rate = jnp.exp(
                (lane128 % HALF).astype(f32) * (-2.0 * math.log(10000.0) / HEAD_DIM)
            )
            for s in range(slots):
                e0 = lens[s, 0]
                e1 = e0 + lens[s, 1]
                e2 = e1 + lens[s, 2]
                e3 = e2 + lens[s, 3]

                def begins(p):
                    b = jnp.where(p >= e0, e0, 0)
                    b = jnp.where(p >= e1, e1, b)
                    b = jnp.where(p >= e2, e2, b)
                    return jnp.where(p >= e3, e3, b)

                angle = (prow - begins(prow)).astype(f32) * rate
                sine = jnp.sin(angle)
                rows = slice(s * slot, (s + 1) * slot)
                cos_t[rows, :] = jnp.cos(angle)
                sin_t[rows, :] = jnp.where(lane128 < HALF, -sine, sine)
                kpos = lax.broadcasted_iota(jnp.int32, (slot, slot), 0)
                qpos = lax.broadcasted_iota(jnp.int32, (slot, slot), 1)
                seen = (kpos >= begins(qpos)) & (kpos <= qpos)
                bias_t[s] = jnp.where(seen, 0.0, -1e30).astype(f32)
                live = jnp.where(prow < e2, 1.0, 0.0)[:, 0:1]
                db[rows, :] = (db[rows, :].astype(f32) * live).astype(bf16)

        def chunks(rows_each, body):
            def step(i, carry):
                body(pl.ds(pl.multiple_of(i * rows_each, rows_each), rows_each))
                return carry

            lax.fori_loop(0, T // rows_each, step, 0)

        def norm_first():
            def body(r):
                s = tok[r, :].astype(f32)
                sc = lax.rsqrt(jnp.mean(s * s, axis=1, keepdims=True) + epsilon)
                na[r, :] = (s * sc * gains[0:1, :]).astype(bf16)
                stats[r, :] = jnp.broadcast_to(sc, (sc.shape[0], 128))

            chunks(128, body)

        def flat(w, n0, n):
            val = w[:, :, :, :, pl.ds(n0, n)]
            return val.reshape(-1, n)

        def project(w, o, turned, factor=1.0):
            N = 256

            def step(i, carry):
                n0 = pl.multiple_of(i * N, N)
                a = mm(na[...], flat(w, n0, N))
                if turned:
                    for j in range(N // 128):
                        turned_part = rope(
                            a[:, j * 128 : (j + 1) * 128], cos_t[...], sin_t[...]
                        )
                        o[:, pl.ds(n0 + j * 128, 128)] = (turned_part * factor).astype(bf16)
                else:
                    o[:, pl.ds(n0, N)] = a.astype(bf16)
                return carry

            lax.fori_loop(0, width // N, step, 0)

        THIRD = slot // 3
        BLOCKS = [(i * THIRD, (i + 1) * THIRD, (i + 1) * THIRD) for i in range(3)]

        def attend_one(s, pair):
            rows = pl.ds(pl.multiple_of(s * slot, slot), slot)
            cs = pl.ds(pl.multiple_of(pair * 128, 128), 128)
            q2, k2, v2 = q[rows, cs], k[rows, cs], v[rows, cs]
            km, vm, om = split_heads(k2), split_heads(v2), split_heads(jnp.ones_like(v2))
            for begin, end, seen in BLOCKS:
                st = mm(stack2(km, 0, seen), q2[begin:end], 1, 1)
                expo = []
                for h in range(2):
                    sc = st[h * seen : (h + 1) * seen] + bias_t[s, :seen, begin:end]
                    top = jnp.max(sc, axis=0, keepdims=True)
                    e = jnp.exp(sc - top)
                    total = jnp.sum(e, axis=0, keepdims=True)
                    expo.append(e.astype(bf16))
                    lse[s, pair, h : h + 1, begin:end] = top + jnp.log(total)
                right = jnp.concatenate([stack2(vm, 0, seen), stack2(om, 0, seen)], axis=1)
                o = mm(jnp.concatenate(expo, axis=0), right, 0, 0)
                here = pl.ds(pl.multiple_of(s * slot, slot) + begin, end - begin)
                ho[here, cs] = (o[:, :128] / o[:, 128:]).astype(bf16)

        def attend(first, count):
            UNROLL = 3

            def step(i, carry):
                for u in range(UNROLL):
                    n = first + i * UNROLL + u
                    attend_one(n // PAIRS, n % PAIRS)
                return carry

            lax.fori_loop(0, count // UNROLL, step, 0)

        def middle():
            def body(r):
                s = tok[r, :].astype(f32) + mm(ho[r, :], wo[...].reshape(width, width))
                sc = lax.rsqrt(jnp.mean(s * s, axis=1, keepdims=True) + epsilon)
                smid[r, :] = s
                outacc[r, :] = s
                dnf[r, :] = jnp.zeros_like(s)
                nf[r, :] = (s * sc * gains[1:2, :]).astype(bf16)
                stats[r, :] = jnp.where(
                    lax.broadcasted_iota(jnp.int32, (sc.shape[0], 128), 1) == 0, stats[r, :], sc
                )

            chunks(slot, body)

        def ffn_hidden(i, s):
            wg_n, wu_n = (wgu[i][a].reshape(width, NB) for a in range(2))
            wd_n = wd[i].reshape(NB, width)

            r = slice(s * slot, (s + 1) * slot)
            g = mm(nf[r, :], wg_n)
            u = mm(nf[r, :], wu_n)
            dh = mm(db[r, :], wd_n, 1, 1)
            sg = 1.0 / (1.0 + jnp.exp(-g))
            si = g * sg
            hs[r, :] = (si * u).astype(bf16)
            dus[r, :] = (dh * si).astype(bf16)
            dgs[r, :] = (dh * u * (sg * (1.0 + g * (1.0 - sg)))).astype(bf16)

        def ffn_streams(i):
            outacc[...] += mm(hs[...], wd[i].reshape(NB, width))
            dnf[...] += mm(dgs[...], wgu[i][0].reshape(width, NB), 1, 1)
            dnf[...] += mm(dus[...], wgu[i][1].reshape(width, NB), 1, 1)

        def ffn_grads(i):
            G = held[i][0]
            G[0] = mm(nf[...], dgs[...], 0, 0).astype(bf16).reshape(G.shape[1:])
            G[1] = mm(nf[...], dus[...], 0, 0).astype(bf16).reshape(G.shape[1:])
            gd = mm(hs[...], db[...], 0, 0).astype(bf16).reshape(2, 2, 2, RD, width)
            for sub in range(2):
                held[Z + sub][0][0, i // 2, i % 2] = gd[:, :, sub]

        def middle_back():
            C = 128

            def step(i, acc):
                r = pl.ds(pl.multiple_of(i * C, C), C)
                dn, s, sc = dnf[r, :], smid[r, :], stats[r, 1:2]
                w = dn * gains[1:2, :]
                acc = acc + jnp.sum((dn * (s * sc)).reshape(C // 8, 8, width), axis=0)
                back = sc * w - s * (sc * sc * sc * jnp.mean(w * s, axis=1, keepdims=True))
                dm = db[r, :].astype(f32) + back
                dnf[r, :] = dm
                db[r, :] = dm.astype(bf16)
                return acc

            acc = lax.fori_loop(0, T // C, step, jnp.zeros((8, width), f32))
            gg[0, 1:2] = jnp.sum(acc, axis=0, keepdims=True)

        def grad_out_proj():
            G = held[Z + 2][0]
            val = mm(ho[...], db[...], 0, 0).astype(bf16)
            for a in range(QB):
                G[a] = val[:, a * QN : (a + 1) * QN].reshape(G.shape[1:])

        def heads_back():
            for zi in range(ZH):
                w = wo[2 * zi : 2 * zi + 2].reshape(8 * R, width)
                nf[:, zi * 8 * R : (zi + 1) * 8 * R] = mm(db[...], w, 1, 1).astype(bf16)

        def attend_back_one(s, pair):
            rows = pl.ds(pl.multiple_of(s * slot, slot), slot)
            cs = pl.ds(pl.multiple_of(pair * 128, 128), 128)
            q2, k2, v2, d2 = q[rows, cs], k[rows, cs], v[rows, cs], nf[rows, cs]
            km, vm, qm, dm = (split_heads(a) for a in (k2, v2, q2, d2))
            B = THIRD
            P, S = {}, {}
            for name, begin, end, seen in ((0, 0, B, B), (1, B, slot, slot)):
                st = mm(stack2(km, 0, seen), q2[begin:end], 1, 1)
                dp = mm(stack2(vm, 0, seen), d2[begin:end], 1, 1)
                for h in range(2):
                    part = slice(h * seen, (h + 1) * seen)
                    p = jnp.exp(
                        st[part]
                        + bias_t[s, :seen, begin:end]
                        - lse[s, pair, h : h + 1, begin:end]
                    )
                    P[name, h] = p.astype(bf16)
                    centre = jnp.sum(p * dp[part], axis=0, keepdims=True)
                    S[name, h] = (p * (dp[part] - centre)).astype(bf16)

            def key_side(w, m):
                first = jnp.concatenate([w[0, 0], w[0, 1], w[1, 0][:B], w[1, 1][:B]], axis=1)
                top = mm(first, jnp.concatenate([stack2(m, 0, B), stack2(m, B, slot)], axis=0))
                rest = jnp.concatenate([w[1, 0][B:], w[1, 1][B:]], axis=1)
                return jnp.concatenate([top, mm(rest, stack2(m, B, slot))], axis=0)

            co, si = cos_t[rows, :], -sin_t[rows, :]
            v[rows, cs] = key_side(P, dm).astype(bf16)
            k[rows, cs] = rope(key_side(S, qm), co, si).astype(bf16)
            dq = [
                mm(jnp.concatenate([S[n, 0], S[n, 1]], axis=0), stack2(km, 0, seen), 0, 0)
                for n, seen in ((0, B), (1, slot))
            ]
            q[rows, cs] = rope(jnp.concatenate(dq, axis=0) * FACTOR, co, si).astype(bf16)

        def attend_back(block, s):
            per_block = QN // 128

            def step(i, carry):
                attend_back_one(s, i + block * per_block)
                return carry

            lax.fori_loop(0, per_block, step, 0)

        def attend_grads(block):
            G = held[Z + 3 + block][0]
            at = slice(block * QN, (block + 1) * QN)
            grads = jnp.concatenate([q[:, at], k[:, at], v[:, at]], axis=1)
            val = mm(na[...], grads, 0, 0).astype(bf16)
            for a in range(3):
                G[a] = val[:, a * QN : (a + 1) * QN].reshape(G.shape[1:])

        def first_back(i):
            N = width // 2

            def rows_of(w):
                return w[i * ZH : (i + 1) * ZH].reshape(N, width)

            smid[:, i * N : (i + 1) * N] = (
                mm(q[...], rows_of(wq), 1, 1)
                + mm(k[...], rows_of(wk), 1, 1)
                + mm(v[...], rows_of(wv), 1, 1)
            )

        def first_norm_back():
            C = 128

            def step(i, acc):
                r = pl.ds(pl.multiple_of(i * C, C), C)
                dn, s, sc = smid[r, :], tok[r, :].astype(f32), stats[r, 0:1]
                w = dn * gains[0:1, :]
                acc = acc + jnp.sum((dn * (s * sc)).reshape(C // 8, 8, width), axis=0)
                back = sc * w - s * (sc * sc * sc * jnp.mean(w * s, axis=1, keepdims=True))
                tok[r, :] = (dnf[r, :] + back).astype(bf16)
                return acc

            acc = lax.fori_loop(0, T // C, step, jnp.zeros((8, width), f32))
            gg[0, 0:1] = jnp.sum(acc, axis=0, keepdims=True)

        def result():
            parts = ((hs, 0, NB), (dus, NB, width - NB))
            for held_in, begin, n in parts:
                held_in[:, :n] = outacc[:, begin : begin + n].astype(bf16)
            for s in range(slots):
                for held_in, begin, n in parts:
                    part = held_in.at[pl.ds(s * slot, slot), pl.ds(0, n)]
                    put(part, out_main.at[s, :, pl.ds(begin, n)])

        def first_norm():
            gains[...] = gsum[NA]
            norm_first()

        def gains_step(i):
            gn_finish(i)
            if i + 1 < NA:
                gn_start(i + 1)

        def gain_grads_step(i):
            gg_finish(i)
            if i + 1 < len(all_partners):
                gg_start(i + 1)

        def reduce_step(k, r):
            plain = (rs_1, rs_2, rs_3, rs_4, rs_5, rs_6, rs_7)
            along_z = (rs_1, zs_2, zs_3, zs_4, zs_5, rs_6, rs_7)
            (along_z if r in ALONG_Z_FIRST else plain)[k - 1](r)

        quarter = slots * PAIRS // 4
        comm = (
            *(from_plane(k) for k in range(5)), *(None,) * 5,
            None, *(functools.partial(reduce_step, k) for k in range(1, 8)), None, None,
            gn_start, gains_step, gg_start, gain_grads_step,
        )
        compute = (
            lambda _: tables(),
            lambda _: first_norm(),
            lambda i: project((wq, wk, wv)[i], (q, k, v)[i], i < 2, (FACTOR, 1.0, 1.0)[i]),
            lambda i: attend(i * quarter, quarter),
            lambda _: middle(),
            lambda i: ffn_hidden(i // 2, i % 2),
            ffn_streams,
            ffn_grads,
            lambda _: middle_back(),
            lambda _: grad_out_proj(),
            lambda _: heads_back(),
            lambda i: attend_back(i // 2, i % 2),
            attend_grads,
            first_back,
            lambda _: first_norm_back(),
            lambda _: result(),
        )
        FIRST_GAINS, TABLES, FIRST_NORM_BACK, RESULT = 20, 30, 44, 45
        pl.semaphore_wait(barrier, len(partners))
        for i, code in enumerate(ORDER):
            kind, n = divmod(code, 100)
            if i == 1:
                fetch_rest()
            if kind == FIRST_GAINS:
                spread_gains()
            if kind == TABLES:
                have(TOKENS)
            if kind < 30:
                comm[kind](n)
            elif kind == RESULT:
                result()
            else:
                pl.when(f >= 0)(functools.partial(compute[kind - 30], n))
            if kind == FIRST_NORM_BACK:
                for s in range(slots):
                    put(tok.at[pl.ds(s * slot, slot)], out_tokens.at[s])
        ag.sent(*(key for key in list(ag.started) if key[0] < 4 or key[0] % 2 == 0))
        rs.sent(*list(rs.started))
        gn.sent(*range(NA + len(all_partners)))
        put(gg.at[len(all_partners)], out_gains)
        for copy in outs:
            copy.wait()

    VM, HB = pltpu.VMEM, pl.BlockSpec(memory_space=pl.ANY)
    S = jax.ShapeDtypeStruct

    def full(rows_half, n):
        return VM((Z, 2, 2, rows_half, n), bf16)

    def piece_bufs(i, kind):
        a, r, n = (G_SHAPE, D_SHAPE, Q_SHAPE)[kind]
        if i in ALONG_Z_FIRST:
            return [
                VM((Z - 1, a, 2, r, n), bf16),
                VM((a, r, n), bf16),
                VM((a, r, n // 2), bf16),
                VM((a, 2, r, n), bf16),
            ]
        return [
            VM((a, ZH, r, n), bf16),
            VM((a, ZH, 2, r, n // 2), bf16),
            VM((a, ZH, 2, r, n // 2), bf16),
            VM((Z - 1, a, r, n // 2), bf16),
            VM((a, 2, r, n), bf16),
        ]

    def grads_of(count, shape):
        a, r, n = shape
        return VM((count, a, ZH, 2, 2, 2, r, n), bf16)

    def first_of(count, shape):
        a, r, n = shape
        return VM((count, a, ZH, 2, 2, r, n), bf16)

    axes = 3 if Z == 4 else 2
    NL = 8 + 2 + 4 * Z + 2 * slots
    scratch = [full(R, width)] * 4 + [VM((Z, 2, 2, 2 * RD, width), bf16)]
    scratch += [VM((2, Z, 2, 2, R, NB), bf16)] * Z
    scratch += [VM((T, width), bf16)] * 6
    scratch += [VM((T, width), f32), VM((T, width), bf16), VM((T, width), bf16)]
    scratch += [VM((T, width), f32)] * 2
    scratch += [VM((T, 128), f32)] * 3
    scratch += [VM((slots, slot, slot), f32), VM((slots, PAIRS, 8, slot), f32)]
    scratch += [VM((T, NB), bf16)] * 3
    scratch += [VM((axes + 1, 8, width), f32), VM((axes, 8, width), f32), VM((8, width), f32)]
    scratch += [VM((axes + 3, 8, width), f32), VM((axes + 2, 8, width), f32)]
    scratch += [grads_of(2, G_SHAPE), grads_of(2, D_SHAPE), grads_of(2, Q_SHAPE)]
    for i, (kind, _) in enumerate(PIECES):
        scratch += piece_bufs(i, kind)
    scratch += [first_of(4, G_SHAPE), first_of(2, D_SHAPE), first_of(1 + QB, Q_SHAPE)]
    DMA = pltpu.SemaphoreType.DMA
    scratch += [DMA((NL,)), DMA((NAG, 17)), DMA((NAG, 17)), DMA((NRS, 10)), DMA((NRS, 10))]
    scratch += [DMA((2 * axes + 2,)), DMA((2 * axes + 2,)), DMA((NRS + 1 + 3 * slots,))]
    out_shape = [S((slots, slot, width), bf16)] * 2 + [S((8, width), f32)]
    for _, (a, r, n) in PIECES:
        out_shape.append(S((a, 2, r, n), bf16))
    call = pl.pallas_call(
        kernel,
        out_shape=out_shape,
        in_specs=[pl.BlockSpec(memory_space=pltpu.SMEM)] + [pl.BlockSpec(memory_space=VM)] * 2 + [HB] * 9,
        out_specs=[HB] * len(out_shape),
        scratch_shapes=scratch,
        compiler_params=pltpu.CompilerParams(
            collective_id=0, has_side_effects=True, vmem_limit_bytes=VMEM_BYTES
        ),
    )

    FINAL = [S((slots, slot, width), bf16)] * 2 + [S((per, width), f32)] * 4
    FINAL += [S((per, ff), f32)] * 2 + [S((ff // fs, width), f32)] + [S((1, per), f32)] * 2
    NF = len(FINAL)

    def finish(*refs):
        made, outs = refs[: 3 + NRS], refs[3 + NRS : 3 + NRS + NF]
        held = refs[3 + NRS + NF : 2 * (3 + NRS) + NF]
        done = refs[2 * (3 + NRS) + NF : -2]
        in_sem, sem = refs[-2:]
        fetched = [
            pltpu.make_async_copy(src, dst, in_sem.at[i])
            for i, (src, dst) in enumerate(zip(made, held))
        ]
        for copy in fetched:
            copy.start()
        f = lax.axis_index("fsdp")
        lane = lax.broadcasted_iota(jnp.int32, (width, 128), 1)
        at = lax.broadcasted_iota(jnp.int32, (width, 128), 0)
        pick = jnp.where((at == lane + f * per) & (lane < per), 1.0, 0.0).astype(bf16)
        stored = []

        def store(i, src):
            copy = pltpu.make_async_copy(src, outs[i], sem.at[i])
            copy.start()
            stored.append(copy)

        for i in range(2):
            fetched[i].wait()
            store(i, held[i])
        pieces = held[3:]
        dq, dk, dv, do, dg, du, dd, first, second = done
        for i in range(Z):
            fetched[3 + i].wait()
            for a, out in enumerate((dg, du)):
                out[:, i * NB : (i + 1) * NB] = pieces[i][a].astype(f32).reshape(per, NB)
        store(6, dg)
        store(7, du)
        for sub in range(2):
            fetched[3 + Z + sub].wait()
            for c in range(2):
                rows = slice((2 * c + sub) * RD, (2 * c + sub + 1) * RD)
                dd[rows, :] = pieces[Z + sub][0, c].astype(f32)
        store(8, dd)
        fetched[5 + Z].wait()
        for a in range(QB):
            do[:, a * QN : (a + 1) * QN] = pieces[Z + 2][a].astype(f32).reshape(per, QN)
        store(5, do)
        for b in range(QB):
            fetched[6 + Z + b].wait()
            for a, out in enumerate((dq, dk, dv)):
                out[:, b * QN : (b + 1) * QN] = pieces[Z + 3 + b][a].astype(f32).reshape(per, QN)
        for i, out in enumerate((dq, dk, dv)):
            store(2 + i, out)
        fetched[2].wait()
        g = held[2][...]
        total = jnp.zeros((8, 128), f32)
        for _ in range(3):
            term = g.astype(bf16)
            total = total + mm(term, pick)
            g = g - term.astype(f32)
        first[...] = total[0:1, :per]
        second[...] = total[1:2, :per]
        store(9, first)
        store(10, second)
        for copy in stored:
            copy.wait()

    post = pl.pallas_call(
        finish,
        out_shape=FINAL,
        in_specs=[HB] * (3 + NRS),
        out_specs=[HB] * NF,
        scratch_shapes=[VM(o.shape, o.dtype) for o in out_shape + FINAL[2:]]
        + [DMA((3 + NRS,)), DMA((NF,))],
        compiler_params=pltpu.CompilerParams(vmem_limit_bytes=VMEM_BYTES),
    )

    def local(tokens, lengths, wq, wk, wv, wo, wg, wu, wd, gain_attn, gain_ffn, gradient):
        rows = (gain_attn.reshape(1, per), gain_ffn.reshape(1, per))
        made = call(lengths, *rows, tokens, gradient, wq, wk, wv, wo, wg, wu, wd)
        *grads, first, second = post(*made)
        return (*grads, first.reshape(per), second.reshape(per))

    return local


def layout(lengths, slot):
    pieces = lengths.shape[0]
    bounds = jnp.stack([jnp.sum(lengths[: j + 1]) for j in range(pieces)])
    places = lax.iota(jnp.int32, slot)
    piece_of = jnp.sum((places[:, None] >= bounds[None, :]).astype(jnp.int32), axis=1)
    piece_begins = bounds - lengths
    member = piece_of[:, None] == lax.iota(jnp.int32, pieces)[None, :]
    begins = jnp.sum(jnp.where(member, piece_begins[None, :], 0), axis=1)
    offsets = places - begins
    live = (piece_of < pieces - 1).astype(jnp.float32)
    visible = (piece_of[:, None] == piece_of[None, :]) & (places[None, :] <= places[:, None])
    return (offsets, live, visible)


def rotary(offsets, head_dim):
    half = head_dim // 2
    rates = jnp.power(10000.0, -2.0 * lax.iota(jnp.float32, half) / head_dim)
    angle = offsets.astype(jnp.float32)[:, None] * rates[None, :]
    angle = jnp.concatenate([angle, angle], axis=1)
    return (jnp.cos(angle), jnp.sin(angle))


def turn(values, cosine, sine, sign):
    half = values.shape[-1] // 2
    swapped = jnp.concatenate([-values[..., half:], values[..., :half]], axis=-1)
    return values * cosine[:, None, :] + sign * swapped * sine[:, None, :]


def matmul(left, right):
    return jnp.dot(left, right, preferred_element_type=jnp.float32)


def left_inner(left, right):
    return lax.dot_general(
        left, right, (((0,), (0,)), ((), ())), preferred_element_type=jnp.float32
    )


def right_inner(left, right):
    return lax.dot_general(
        left, right, (((1,), (1,)), ((), ())), preferred_element_type=jnp.float32
    )


def norm_back(grad_normed, gain, stream, scale):
    weighted = grad_normed * gain.astype(jnp.float32)
    gain_grad = jnp.sum(grad_normed * stream * scale, axis=0)
    stream_grad = scale * weighted - stream * scale * scale * scale * jnp.mean(
        weighted * stream, axis=1, keepdims=True
    )
    return (stream_grad, gain_grad)


def forward_pass(tokens_slot, weights, cosine, sine, visible):
    w_query, w_key, w_value, w_out, w_gate, w_up, w_down, gain_attn, gain_ffn = weights
    slot = tokens_slot.shape[0]
    factor = HEAD_DIM ** (-0.5)
    stream = tokens_slot.astype(jnp.float32)
    scale_attn = lax.rsqrt(jnp.mean(stream * stream, axis=1, keepdims=True) + epsilon)
    normed_attn = (stream * scale_attn * gain_attn.astype(jnp.float32)).astype(jnp.bfloat16)
    query_rows = turn(
        matmul(normed_attn, w_query).reshape(slot, HEADS, HEAD_DIM), cosine, sine, 1.0
    ).astype(jnp.bfloat16)
    key_rows = turn(
        matmul(normed_attn, w_key).reshape(slot, HEADS, HEAD_DIM), cosine, sine, 1.0
    ).astype(jnp.bfloat16)
    value_rows = matmul(normed_attn, w_value).astype(jnp.bfloat16).reshape(slot, HEADS, HEAD_DIM)
    scores = (
        jnp.einsum("qhd,khd->hqk", query_rows, key_rows, preferred_element_type=jnp.float32)
        * factor
    )
    scores = jnp.where(visible[None], scores, -1e30)
    top = jnp.max(scores, axis=-1, keepdims=True)
    weights_exp = jnp.exp(scores - top)
    totals = jnp.sum(weights_exp, axis=-1, keepdims=True)
    probs = weights_exp / totals
    log_total = top + jnp.log(totals)
    mixed = jnp.einsum(
        "hqk,khd->qhd", probs.astype(jnp.bfloat16), value_rows, preferred_element_type=jnp.float32
    )
    heads_out = mixed.reshape(slot, HEADS * HEAD_DIM).astype(jnp.bfloat16)
    stream_mid = stream + matmul(heads_out, w_out)
    scale_ffn = lax.rsqrt(jnp.mean(stream_mid * stream_mid, axis=1, keepdims=True) + epsilon)
    normed_ffn = (stream_mid * scale_ffn * gain_ffn.astype(jnp.float32)).astype(jnp.bfloat16)
    gate_pre = matmul(normed_ffn, w_gate)
    up_branch = matmul(normed_ffn, w_up)
    hidden = (gate_pre * jax.nn.sigmoid(gate_pre) * up_branch).astype(jnp.bfloat16)
    result = stream_mid + matmul(hidden, w_down)
    kept = (
        stream,
        scale_attn,
        normed_attn,
        query_rows,
        key_rows,
        value_rows,
        log_total,
        heads_out,
        stream_mid,
        scale_ffn,
        normed_ffn,
        gate_pre,
        up_branch,
        hidden,
    )
    return (kept, result)


def backward_pass(kept, weights, cotangent, live, cosine, sine, visible):
    w_query, w_key, w_value, w_out, w_gate, w_up, w_down, gain_attn, gain_ffn = weights
    (
        stream,
        scale_attn,
        normed_attn,
        query_rows,
        key_rows,
        value_rows,
        log_total,
        heads_out,
        stream_mid,
        scale_ffn,
        normed_ffn,
        gate_pre,
        up_branch,
        hidden,
    ) = kept
    slot = stream.shape[0]
    factor = HEAD_DIM ** (-0.5)
    d_out = cotangent.astype(jnp.float32) * live[:, None]
    d_branch = d_out.astype(jnp.bfloat16)
    grad_down = left_inner(hidden, d_branch)
    d_hidden = right_inner(d_branch, w_down)
    sigma = jax.nn.sigmoid(gate_pre)
    d_gate = (d_hidden * up_branch * sigma * (1.0 + gate_pre * (1.0 - sigma))).astype(jnp.bfloat16)
    d_up = (d_hidden * gate_pre * sigma).astype(jnp.bfloat16)
    grad_gate = left_inner(normed_ffn, d_gate)
    grad_up = left_inner(normed_ffn, d_up)
    d_normed_ffn = right_inner(d_gate, w_gate) + right_inner(d_up, w_up)
    mid_back, grad_gain_ffn = norm_back(d_normed_ffn, gain_ffn, stream_mid, scale_ffn)
    d_mid = d_out + mid_back
    d_attn = d_mid.astype(jnp.bfloat16)
    grad_out_proj = left_inner(heads_out, d_attn)
    d_heads = right_inner(d_attn, w_out).astype(jnp.bfloat16).reshape(slot, HEADS, HEAD_DIM)
    scores = (
        jnp.einsum("qhd,khd->hqk", query_rows, key_rows, preferred_element_type=jnp.float32)
        * factor
    )
    probs = jnp.where(visible[None], jnp.exp(scores - log_total), 0.0)
    d_probs = jnp.einsum("qhd,khd->hqk", d_heads, value_rows, preferred_element_type=jnp.float32)
    d_values = jnp.einsum(
        "hqk,qhd->khd", probs.astype(jnp.bfloat16), d_heads, preferred_element_type=jnp.float32
    )
    d_values = d_values.astype(jnp.bfloat16).reshape(slot, HEADS * HEAD_DIM)
    centre = jnp.sum(probs * d_probs, axis=-1, keepdims=True)
    d_scores = (probs * (d_probs - centre)).astype(jnp.bfloat16)
    d_query_rot = (
        jnp.einsum("hqk,khd->qhd", d_scores, key_rows, preferred_element_type=jnp.float32) * factor
    )
    d_key_rot = (
        jnp.einsum("hqk,qhd->khd", d_scores, query_rows, preferred_element_type=jnp.float32)
        * factor
    )
    d_queries = (
        turn(d_query_rot, cosine, sine, -1.0).astype(jnp.bfloat16).reshape(slot, HEADS * HEAD_DIM)
    )
    d_keys = (
        turn(d_key_rot, cosine, sine, -1.0).astype(jnp.bfloat16).reshape(slot, HEADS * HEAD_DIM)
    )
    grad_query = left_inner(normed_attn, d_queries)
    grad_key = left_inner(normed_attn, d_keys)
    grad_value = left_inner(normed_attn, d_values)
    d_normed_attn = (
        right_inner(d_queries, w_query)
        + right_inner(d_keys, w_key)
        + right_inner(d_values, w_value)
    )
    stream_back, grad_gain_attn = norm_back(d_normed_attn, gain_attn, stream, scale_attn)
    grad_input = d_mid + stream_back
    grads = (
        grad_query,
        grad_key,
        grad_value,
        grad_out_proj,
        grad_gate,
        grad_up,
        grad_down,
        grad_gain_attn,
        grad_gain_ffn,
    )
    return (grads, grad_input)


def local_general(
    tokens, lengths, w_query, w_key, w_value, w_out, w_gate, w_up, w_down, gain_attn, gain_ffn,
    output_gradient,
):
    rows = (w_query, w_key, w_value, w_out, w_gate, w_up, w_down, gain_attn, gain_ffn)
    weights = tuple(lax.all_gather(w, "fsdp", axis=0, tiled=True) for w in rows)
    results, input_grads, totals = [], [], None
    for i in range(tokens.shape[0]):
        offsets, live, visible = layout(lengths[i], tokens.shape[1])
        cosine, sine = rotary(offsets, HEAD_DIM)
        kept, result = forward_pass(tokens[i], weights, cosine, sine, visible)
        grads, grad_input = backward_pass(
            kept, weights, output_gradient[i], live, cosine, sine, visible
        )
        results.append(result.astype(jnp.bfloat16))
        input_grads.append(grad_input.astype(jnp.bfloat16))
        totals = grads if totals is None else tuple(a + b for a, b in zip(totals, grads))
    shares = (lax.psum_scatter(g, "fsdp", scatter_dimension=0, tiled=True) for g in totals)
    summed = tuple(lax.psum(g, "dp") for g in shares)
    return (jnp.stack(results), jnp.stack(input_grads)) + summed


def solution(mesh):
    row, vec = P("fsdp", None), P("fsdp")
    wide = P(("dp", "fsdp"), None, None)
    in_specs = (wide, P(("dp", "fsdp"), None)) + (row,) * 7 + (vec, vec, wide)
    out_specs = (wide, wide) + (row,) * 7 + (vec, vec)

    def local(tokens, lengths, *rest):
        slots, slot, width = tokens.shape
        ff = rest[4].shape[1]
        if (mesh.shape["dp"], mesh.shape["fsdp"]) == (4, 8) and (width, ff) == (768, 2048):
            return build(mesh, slots, slot, width, ff)(tokens, lengths, *rest)
        return local_general(tokens, lengths, *rest)

    return jax.shard_map(local, mesh=mesh, in_specs=in_specs, out_specs=out_specs, check_vma=False)
```
